128 devices in a mesh: calib: 32 (over z_lo, y, x), peak: 4 (over z_hi, core).
Axes of the slice: x: 4, y: 4, z: 4 (z_hi: 2, z_lo: 2; z = z_hi * 2 + z_lo), core: 2. Of those that a mesh axis runs over, the one named last changes fastest.
Arguments:
- raw: int32 [8, 32, 512, 1024], P('peak', None, 'calib'), may hold values from 256 to 8184, as said below
- pedestal: float32 [3, 32, 512, 1024], P(None, None, 'calib'), may hold values from 594 to 1406
- gain: bfloat16 [3, 32, 512, 1024], P(None, None, 'calib'), may hold values from 16 to 64
- good: int32 [32, 512, 1024], P(None, 'calib'), may hold values from 0 to 1, as said below
- bounds: int32 [32, 7], replicated, may hold values from 1 to 1023, as said below
- table: int32 [32], replicated, may hold values from 0 to 31, as said below
Outputs:
- snr: bfloat16 [8, 32, 512, 1024], P(None, 'calib', None, 'peak')
- curvature: bfloat16 [8, 32, 512, 1024], P(None, 'calib', None, 'peak')
The draws below stay inside these ranges and needn't reach their ends.
Inputs may be any that keep to these rules, and one draw needn't show every extreme that they name: raw // 2048 is the gain code (0, 1 or 3) and raw % 2048 the ADC count, which lies between 256 and 2040. `good`: some module rows are bad in every column. `bounds`: strictly increasing along the last dimension. `table`: each slot is named once.
All inputs are finite; a program needn't handle non-finite values.
Results may differ from the reference program's by a relative error of at most 0.0007.
The reference program's roundings to bfloat16 on the way (of `corrected` and `frame`) count: a program that leaves them out, or rounds other values in their place, can miss the bound.
Values may be sent and summed in bfloat16 or wider, within the bound.
A program may use at most 128 MiB of HBM per device.

```python
import math
import jax
import jax.numpy as jnp
from jax import lax

COLS = 1024
BANDS = 8
SLOT_C = 4
CYCLES = 32
CYCLE_W = 64
MODS = 32
MROWS = 512
SLOT_R = 8
FRAMES = 8


def shared_levels(key):
    return jax.random.randint(jax.random.fold_in(key, 11), (3, MODS, MROWS, COLS), 600, 1400, dtype=jnp.int32)


def shared_table(key):
    return jax.random.permutation(jax.random.fold_in(key, 41), MODS).astype(jnp.int32)


def placed_profile(key):
    table = shared_table(key)
    rows = jnp.arange(MROWS, dtype=jnp.int32)
    columns = jnp.arange(COLS, dtype=jnp.int32)
    ypos = (table // SLOT_C)[:, None] * MROWS + rows[None, :]
    xpos = (table % SLOT_C)[:, None] * COLS + columns[None, :]
    dy_two = 2 * ypos + 1 - SLOT_R * MROWS
    dx_two = 2 * xpos + 1 - SLOT_C * COLS
    dist = dy_two[:, :, None] * dy_two[:, :, None] + dx_two[:, None, :] * dx_two[:, None, :]
    annulus = jnp.zeros(dist.shape, jnp.int32)
    for index in range(1, CYCLES):
        edge = 2 * CYCLE_W * index * (2 * CYCLE_W * index)
        annulus = annulus + (dist >= edge).astype(jnp.int32)
    lower = 2 * CYCLE_W * annulus * (2 * CYCLE_W * annulus)
    upper = 2 * CYCLE_W * (annulus + 1) * (2 * CYCLE_W * (annulus + 1))
    within = jnp.minimum((dist - lower) * 64 // (upper - lower), 63)
    return (annulus, within)


def draw_table(key, part):
    return shared_table(key)


def draw_raw(key, part):
    levels = shared_levels(key)
    picks = jax.random.randint(jax.random.fold_in(key, 12), (FRAMES, MODS, MROWS, COLS), 0, 8, dtype=jnp.int32)
    section = jnp.where(picks < 6, 0, jnp.where(picks == 6, 1, 2))
    code = jnp.where(section == 2, 3, section)
    level = jnp.where(section == 0, levels[0], jnp.where(section == 1, levels[1], levels[2]))
    rows = jnp.arange(MROWS, dtype=jnp.int32)
    signal = jax.random.randint(jax.random.fold_in(key, 13), (FRAMES, MODS, MROWS, COLS), -32, 128, dtype=jnp.int32)
    signal = signal * (MROWS + 2 * rows)[None, None, :, None] // MROWS
    offset = jax.random.randint(jax.random.fold_in(key, 14), (FRAMES, MODS, MROWS, COLS // 32), -64, 64, dtype=jnp.int32)
    offset = jnp.repeat(offset, 32, axis=3)
    annulus, within = placed_profile(key)
    steps_drawn = jax.random.randint(jax.random.fold_in(key, 16), (FRAMES, CYCLES), -96, 97, dtype=jnp.int32)
    slopes = jax.random.randint(jax.random.fold_in(key, 17), (FRAMES, CYCLES), -1, 2, dtype=jnp.int32)
    background = jnp.take(steps_drawn, annulus, axis=1) + jnp.take(slopes, annulus, axis=1) * within[None]
    return code * 2048 + level + signal + offset + background


def draw_pedestal(key, part):
    levels = shared_levels(key).astype(jnp.float32)
    noise = jax.random.uniform(jax.random.fold_in(key, 15), (3, MODS, MROWS, COLS), jnp.float32, -3.0, 3.0)
    return levels + noise


def draw_good(key, part):
    pixel = jax.random.randint(jax.random.fold_in(key, 21), (MODS, MROWS, COLS), 0, 16, dtype=jnp.int32)
    row = jax.random.randint(jax.random.fold_in(key, 22), (MODS, MROWS, 1), 0, 32, dtype=jnp.int32)
    return ((pixel != 0) & (row != 0)).astype(jnp.int32)


def draw_bounds(key, part):
    width = COLS // BANDS
    base = jnp.arange(1, BANDS, dtype=jnp.int32) * width
    random_shift = jax.random.randint(jax.random.fold_in(key, 31), (MODS, BANDS - 1), -(width // 4), width // 4 + 1, dtype=jnp.int32)
    return base[None, :] + random_shift


def block_scale(key, extent, shards, low, top_value):
    factor_of, own = 1.0, jax.random.fold_in(key, 6)
    for dim, shards_of in shards:
        steps = jnp.exp(jax.random.uniform(jax.random.fold_in(own, dim), (shards_of,), jnp.float32, low / len(shards), top_value / len(shards)))
        factor_of = factor_of * jnp.repeat(steps, extent[dim] // shards_of).reshape([-1 if axis == dim else 1 for axis in range(len(extent))])
    return factor_of


def setup_inputs(seed: int = 0) -> dict:
    seeds = jax.random.split(jax.random.key(seed), 7)
    return {
        "raw": draw_raw(jax.random.fold_in(seeds[6], 71), 0),
        "pedestal": draw_pedestal(jax.random.fold_in(seeds[6], 71), 0),
        "gain": jnp.clip(jnp.exp(math.log(64.0) - 1.3862944 * jax.random.uniform(seeds[2], (3, MODS, MROWS, COLS), jnp.float32) ** block_scale(seeds[2], (3, MODS, MROWS, COLS), ((2, 32),), -0.2, 0.2)), 16.0, 64.0).astype(jnp.bfloat16),
        "good": draw_good(jax.random.fold_in(seeds[6], 71), 0),
        "bounds": draw_bounds(jax.random.fold_in(seeds[6], 71), 0),
        "table": draw_table(jax.random.fold_in(seeds[6], 71), 0),
    }


precise_variant = lax.Precision.HIGHEST

def cycle_onehot(slot, row_pos, col_pos, mrows, slot_rows):
    ypos = slot // SLOT_C * mrows + row_pos
    xpos = slot % SLOT_C * COLS + col_pos
    dy_two = 2 * ypos + 1 - slot_rows * mrows
    dx_two = 2 * xpos + 1 - SLOT_C * COLS
    dist = dy_two[:, None] * dy_two[:, None] + dx_two[None, :] * dx_two[None, :]
    levels = jnp.arange(CYCLES, dtype=jnp.int32)
    lows = (2 * CYCLE_W * levels) ** 2
    cycle = lax.optimization_barrier(jnp.sum((dist[None] >= lows[:, None, None]).astype(jnp.int32), axis=0)) - 1
    hits = (cycle[None] == levels[:, None, None]).astype(jnp.float32)
    return hits.reshape(CYCLES, -1)

def calibrate(raw, pedestal, gain, good, bounds):
    code = raw // 2048
    counts_adc = (raw % 2048).astype(jnp.float32)
    base = jnp.where(code == 0, pedestal[0], jnp.where(code == 1, pedestal[1], pedestal[2]))
    gain_factor = gain.astype(jnp.float32)
    scale = jnp.where(code == 0, gain_factor[0], jnp.where(code == 1, gain_factor[1], gain_factor[2]))
    weight_factor = good.astype(jnp.float32)
    energy = weight_factor * (counts_adc - base) / scale
    columns = jnp.arange(raw.shape[-1], dtype=jnp.int32)
    band = lax.optimization_barrier(jnp.sum((columns[None, :, None] >= bounds[:, None, :]).astype(jnp.int32), axis=2))
    member_entry = (band[:, :, None] == jnp.arange(BANDS, dtype=jnp.int32)[None, None, :]).astype(jnp.float32)
    totals = jnp.einsum('fmrc,mcb->fmrb', energy, member_entry, precision=precise_variant)
    present_flag = jnp.einsum('tlg,tgd->tld', weight_factor, member_entry, precision=precise_variant)
    level = totals / jnp.maximum(present_flag, 1.0)
    spread = jnp.einsum('fmrb,mcb->fmrc', level, member_entry, precision=precise_variant)
    return (weight_factor * (energy - spread)).astype(jnp.bfloat16)

def laplace(padded):
    center = padded[..., 1:-1, 1:-1]
    return 4.0 * center - padded[..., :-2, 1:-1] - padded[..., 2:, 1:-1] - padded[..., 1:-1, :-2] - padded[..., 1:-1, 2:]

def reference(raw, pedestal, gain, good, bounds, table):
    corrected = lax.map(lambda single: calibrate(single[None], pedestal, gain, good, bounds)[0], raw)
    frame = jnp.zeros(corrected.shape, jnp.bfloat16).at[:, table].set(corrected)
    placed_good = jnp.zeros(good.shape, jnp.float32).at[table].set(good.astype(jnp.float32))
    row_pos = jnp.arange(MROWS, dtype=jnp.int32)
    col_pos = jnp.arange(COLS, dtype=jnp.int32)

    def moments(slot):
        hits = cycle_onehot(slot, row_pos, col_pos, MROWS, SLOT_R)
        values = lax.dynamic_index_in_dim(frame, slot, 1, keepdims=False).reshape(FRAMES, -1).astype(jnp.float32)
        weight_factor = lax.dynamic_index_in_dim(placed_good, slot, 0, keepdims=False).reshape(1, -1)
        first = jnp.einsum('fp,kp->fk', values, hits, precision=precise_variant)
        second = jnp.einsum('fp,kp->fk', values * values, hits, precision=precise_variant)
        present_flag = jnp.einsum('fp,kp->fk', weight_factor, hits, precision=precise_variant)[0]
        return (first, second, present_flag)
    first, second, present_flag = lax.map(moments, jnp.arange(MODS, dtype=jnp.int32))
    first = lax.optimization_barrier(jnp.sum(first, axis=0))
    second = lax.optimization_barrier(jnp.sum(second, axis=0))
    present_flag = lax.optimization_barrier(jnp.sum(present_flag, axis=0))
    cycle_average = first / present_flag[None, :]
    cycle_rms = jnp.sqrt(second / present_flag[None, :] + 1e-06)

    def outputs(slot):
        hits = cycle_onehot(slot, row_pos, col_pos, MROWS, SLOT_R)
        values = lax.dynamic_index_in_dim(frame, slot, 1, keepdims=False).reshape(FRAMES, -1).astype(jnp.float32)
        pixel_mean = jnp.einsum('fk,kp->fp', cycle_average, hits, precision=precise_variant)
        pixel_rms = jnp.einsum('fk,kp->fp', cycle_rms, hits, precision=precise_variant)
        score = ((values - pixel_mean) / pixel_rms).reshape(FRAMES, MROWS, COLS)
        padded = jnp.pad(score, ((0, 0), (1, 1), (1, 1)))
        return (score.astype(jnp.bfloat16), laplace(padded).astype(jnp.bfloat16))
    snr, curvature = lax.map(outputs, jnp.arange(MODS, dtype=jnp.int32))
    return (jnp.swapaxes(snr, 0, 1), jnp.swapaxes(curvature, 0, 1))
```

```python
import jax
import jax.numpy as jnp
from jax import lax
from jax.sharding import PartitionSpec as P

COLS = 1024
BANDS = 8
SLOT_C = 4
CYCLES = 32
CYCLE_W = 64


precise_variant = lax.Precision.HIGHEST


def padded_2(block, sides, width):
    for axis, dim in sides:
        count = lax.axis_size(axis)
        forward = [(i, i + 1) for i in range(count - 1)]
        backward = [(target, source) for source, target in forward]
        low = lax.ppermute(
            lax.slice_in_dim(block, block.shape[dim] - width, None, axis=dim), axis, forward
        )
        high = lax.ppermute(lax.slice_in_dim(block, 0, width, axis=dim), axis, backward)
        block = jnp.concatenate([low, block, high], axis=dim)
    return block


def cycle_index(dist):
    levels = jnp.arange(1, CYCLES, dtype=jnp.int32)
    lows = (2 * CYCLE_W * levels) ** 2
    return jnp.sum((dist[..., None] >= lows).astype(jnp.int32), axis=-1)


def cycle_onehot(slot, row_pos, col_pos, mrows, slot_rows):
    ypos = slot // SLOT_C * mrows + row_pos
    xpos = slot % SLOT_C * COLS + col_pos
    dy_two = 2 * ypos + 1 - slot_rows * mrows
    dx_two = 2 * xpos + 1 - SLOT_C * COLS
    dist = dy_two[:, None] * dy_two[:, None] + dx_two[None, :] * dx_two[None, :]
    levels = jnp.arange(CYCLES, dtype=jnp.int32)
    lows = (2 * CYCLE_W * levels) ** 2
    cycle = jnp.sum((dist[None] >= lows[:, None, None]).astype(jnp.int32), axis=0) - 1
    hits = (cycle[None] == levels[:, None, None]).astype(jnp.float32)
    return hits.reshape(CYCLES, -1)


def calibrate(raw, pedestal, gain, good, bounds):
    code = raw // 2048
    counts_adc = (raw % 2048).astype(jnp.float32)
    base = jnp.where(code == 0, pedestal[0], jnp.where(code == 1, pedestal[1], pedestal[2]))
    gain_factor = gain.astype(jnp.float32)
    scale = jnp.where(
        code == 0, gain_factor[0], jnp.where(code == 1, gain_factor[1], gain_factor[2])
    )
    weight_factor = good.astype(jnp.float32)
    energy = weight_factor * (counts_adc - base) / scale
    columns = jnp.arange(raw.shape[-1], dtype=jnp.int32)
    band = jnp.sum((columns[None, :, None] >= bounds[:, None, :]).astype(jnp.int32), axis=2)
    member_entry = (band[:, :, None] == jnp.arange(BANDS, dtype=jnp.int32)[None, None, :]).astype(
        jnp.float32
    )
    totals = jnp.einsum("fmrc,mcb->fmrb", energy, member_entry, precision=precise_variant)
    present_flag = jnp.einsum(
        "tlg,tgd->tld", weight_factor, member_entry, precision=precise_variant
    )
    level = totals / jnp.maximum(present_flag, 1.0)
    spread = jnp.einsum("fmrb,mcb->fmrc", level, member_entry, precision=precise_variant)
    return (weight_factor * (energy - spread)).astype(jnp.bfloat16)


def laplace(padded):
    center = padded[..., 1:-1, 1:-1]
    return (
        4.0 * center
        - padded[..., :-2, 1:-1]
        - padded[..., 2:, 1:-1]
        - padded[..., 1:-1, :-2]
        - padded[..., 1:-1, 2:]
    )


def local_present(good, table, row_src, mrows, slot_rows):
    n_peak = lax.axis_size("peak")
    width = good.shape[2] // n_peak
    start = lax.axis_index("peak") * width
    part = lax.dynamic_slice_in_dim(good, start, width, axis=2)
    col = start + jnp.arange(width, dtype=jnp.int32)
    ypos = (table // SLOT_C)[:, None] * mrows + row_src[None, :]
    xpos = (table % SLOT_C)[:, None] * COLS + col[None, :]
    dy_two = 2 * ypos + 1 - slot_rows * mrows
    dx_two = 2 * xpos + 1 - SLOT_C * COLS
    dist = dy_two[:, :, None] * dy_two[:, :, None] + dx_two[:, None, :] * dx_two[:, None, :]
    cycle = cycle_index(dist)
    levels = jnp.arange(CYCLES, dtype=jnp.int32)
    hit = jnp.where(cycle[..., None] == levels, part[..., None], 0)
    return jnp.sum(hit, axis=(0, 1, 2)).astype(jnp.float32)


def cycle_stats(first, second, present_flag):
    cycle_average = first / present_flag[None, :]
    cycle_rms = jnp.sqrt(second / present_flag[None, :] + 1e-06)
    return (cycle_average, cycle_rms)


def body(raw, pedestal, gain, good, bounds, table):
    frame_dev, mods, row_dev, cols = raw.shape
    n_calib = lax.axis_size("calib")
    n_peak = lax.axis_size("peak")
    mrows = row_dev * n_calib
    slot_rows = mods // SLOT_C
    width_here = cols // n_peak
    frames_all = frame_dev * n_peak
    row_src = lax.axis_index("calib") * row_dev + jnp.arange(row_dev, dtype=jnp.int32)
    corrected = calibrate(raw, pedestal, gain, good, bounds)
    present_part = local_present(good, table, row_src, mrows, slot_rows)
    indices = jnp.arange(mods, dtype=jnp.int32)
    slot_module = jnp.sum(
        jnp.where(table[None, :] == indices[:, None], indices[None, :], 0), axis=1
    )
    ordered = jnp.take(corrected, slot_module, axis=1)
    send = ordered.reshape(frame_dev, mods, row_dev, n_peak, width_here)
    send = jnp.transpose(send, (1, 3, 0, 2, 4)).reshape(mods * n_peak, frame_dev, row_dev, width_here)
    got = lax.all_to_all(send, ("calib", "peak"), 0, 0, tiled=True)
    got = got.reshape(n_calib, n_peak, frame_dev, row_dev, width_here)
    frame = jnp.transpose(got, (1, 2, 0, 3, 4)).reshape(frames_all, mrows, width_here)
    slot = lax.axis_index("calib")
    col_dst = lax.axis_index("peak") * width_here + jnp.arange(width_here, dtype=jnp.int32)
    hits = cycle_onehot(slot, jnp.arange(mrows, dtype=jnp.int32), col_dst, mrows, slot_rows)
    values = frame.reshape(frames_all, -1).astype(jnp.float32)
    first = jnp.einsum("fp,kp->fk", values, hits, precision=precise_variant)
    second = jnp.einsum("fp,kp->fk", values * values, hits, precision=precise_variant)
    first, second, present_flag = lax.psum((first, second, present_part), ("calib", "peak"))
    cycle_average, cycle_rms = cycle_stats(first, second, present_flag)
    pixel_mean = jnp.einsum("fk,kp->fp", cycle_average, hits, precision=precise_variant)
    pixel_rms = jnp.einsum("fk,kp->fp", cycle_rms, hits, precision=precise_variant)
    score = ((values - pixel_mean) / pixel_rms).reshape(frames_all, mrows, width_here)
    padded = padded_2(score, (("peak", 2),), 1)
    padded = jnp.pad(padded, ((0, 0), (1, 1), (0, 0)))
    bent = laplace(padded)
    return (score.astype(jnp.bfloat16)[:, None], bent.astype(jnp.bfloat16)[:, None])


def solution(mesh):
    in_specs = (
        P("peak", None, "calib", None),
        P(None, None, "calib", None),
        P(None, None, "calib", None),
        P(None, "calib", None),
        P(),
        P(),
    )
    out_specs = (P(None, "calib", None, "peak"), P(None, "calib", None, "peak"))
    return jax.shard_map(body, mesh=mesh, in_specs=in_specs, out_specs=out_specs, check_vma=False)
```

```python
import jax
import jax.numpy as jnp
from jax import lax
from jax.sharding import PartitionSpec as P
from jax.experimental import pallas as pl
from jax.experimental.pallas import tpu as pltpu

COLS = 1024
BANDS = 8
SLOT_C = 4
CYCLES = 32
CYCLE_W = 64


precise_variant = lax.Precision.HIGHEST


def padded_2(block, sides, width):
    for axis, dim in sides:
        count = lax.axis_size(axis)
        forward = [(i, i + 1) for i in range(count - 1)]
        backward = [(target, source) for source, target in forward]
        low = lax.ppermute(
            lax.slice_in_dim(block, block.shape[dim] - width, None, axis=dim), axis, forward
        )
        high = lax.ppermute(lax.slice_in_dim(block, 0, width, axis=dim), axis, backward)
        block = jnp.concatenate([low, block, high], axis=dim)
    return block


def cycle_index(dist):
    levels = jnp.arange(1, CYCLES, dtype=jnp.int32)
    lows = (2 * CYCLE_W * levels) ** 2
    return jnp.sum((dist[..., None] >= lows).astype(jnp.int32), axis=-1)


def cycle_onehot(slot, row_pos, col_pos, mrows, slot_rows):
    ypos = slot // SLOT_C * mrows + row_pos
    xpos = slot % SLOT_C * COLS + col_pos
    dy_two = 2 * ypos + 1 - slot_rows * mrows
    dx_two = 2 * xpos + 1 - SLOT_C * COLS
    dist = dy_two[:, None] * dy_two[:, None] + dx_two[None, :] * dx_two[None, :]
    levels = jnp.arange(CYCLES, dtype=jnp.int32)
    lows = (2 * CYCLE_W * levels) ** 2
    cycle = jnp.sum((dist[None] >= lows[:, None, None]).astype(jnp.int32), axis=0) - 1
    hits = (cycle[None] == levels[:, None, None]).astype(jnp.float32)
    return hits.reshape(CYCLES, -1)


def calibrate(raw, pedestal, gain, good, bounds):
    code = raw // 2048
    counts_adc = (raw % 2048).astype(jnp.float32)
    base = jnp.where(code == 0, pedestal[0], jnp.where(code == 1, pedestal[1], pedestal[2]))
    gain_factor = gain.astype(jnp.float32)
    scale = jnp.where(
        code == 0, gain_factor[0], jnp.where(code == 1, gain_factor[1], gain_factor[2])
    )
    weight_factor = good.astype(jnp.float32)
    energy = weight_factor * (counts_adc - base) / scale
    columns = jnp.arange(raw.shape[-1], dtype=jnp.int32)
    band = jnp.sum((columns[None, :, None] >= bounds[:, None, :]).astype(jnp.int32), axis=2)
    member_entry = (band[:, :, None] == jnp.arange(BANDS, dtype=jnp.int32)[None, None, :]).astype(
        jnp.float32
    )
    totals = jnp.einsum("fmrc,mcb->fmrb", energy, member_entry, precision=precise_variant)
    present_flag = jnp.einsum(
        "tlg,tgd->tld", weight_factor, member_entry, precision=precise_variant
    )
    level = totals / jnp.maximum(present_flag, 1.0)
    spread = jnp.einsum("fmrb,mcb->fmrc", level, member_entry, precision=precise_variant)
    return (weight_factor * (energy - spread)).astype(jnp.bfloat16)


def laplace(padded):
    center = padded[..., 1:-1, 1:-1]
    return (
        4.0 * center
        - padded[..., :-2, 1:-1]
        - padded[..., 2:, 1:-1]
        - padded[..., 1:-1, :-2]
        - padded[..., 1:-1, 2:]
    )


def local_present(good, table, row_src, mrows, slot_rows):
    n_peak = lax.axis_size("peak")
    width = good.shape[2] // n_peak
    start = lax.axis_index("peak") * width
    part = lax.dynamic_slice_in_dim(good, start, width, axis=2)
    col = start + jnp.arange(width, dtype=jnp.int32)
    ypos = (table // SLOT_C)[:, None] * mrows + row_src[None, :]
    xpos = (table % SLOT_C)[:, None] * COLS + col[None, :]
    dy_two = 2 * ypos + 1 - slot_rows * mrows
    dx_two = 2 * xpos + 1 - SLOT_C * COLS
    dist = dy_two[:, :, None] * dy_two[:, :, None] + dx_two[:, None, :] * dx_two[:, None, :]
    cycle = cycle_index(dist)
    levels = jnp.arange(CYCLES, dtype=jnp.int32)
    hit = jnp.where(cycle[..., None] == levels, part[..., None], 0)
    return jnp.sum(hit, axis=(0, 1, 2)).astype(jnp.float32)


def gather_sum_kernel(n_calib, n_peak, x_ref, o_ref, buf, send_sem, recv_sem):
    total = n_calib * n_peak
    me = lax.axis_index("calib") * n_peak + lax.axis_index("peak")
    buf[total - 1] = x_ref[...]
    barrier = pltpu.get_barrier_semaphore()

    def peer_of(step):
        peer = lax.rem(me + step, total)
        return (peer // n_peak, peer % n_peak)

    def greet(step, carry):
        pl.semaphore_signal(
            barrier, inc=1, device_id=peer_of(step), device_id_type=pl.DeviceIdType.MESH
        )
        return carry

    lax.fori_loop(1, total, greet, 0)
    pl.semaphore_wait(barrier, total - 1)

    def send(step, carry):
        pltpu.make_async_remote_copy(
            src_ref=x_ref,
            dst_ref=buf.at[total - 1 - step],
            send_sem=send_sem,
            recv_sem=recv_sem,
            device_id=peer_of(step),
            device_id_type=pl.DeviceIdType.MESH,
        ).start()
        return carry

    lax.fori_loop(1, total, send, 0)
    every = pltpu.make_async_remote_copy(
        src_ref=buf.at[pl.ds(0, total - 1)],
        dst_ref=buf.at[pl.ds(0, total - 1)],
        send_sem=send_sem,
        recv_sem=recv_sem,
        device_id=peer_of(1),
        device_id_type=pl.DeviceIdType.MESH,
    )
    every.wait_send()
    every.wait_recv()

    def add(source, acc):
        return acc + buf[lax.rem(source - me - 1 + 2 * total, total)]

    o_ref[...] = lax.fori_loop(0, total, add, jnp.zeros(x_ref.shape, x_ref.dtype))


def gather_sum(x):
    n_calib = lax.axis_size("calib")
    n_peak = lax.axis_size("peak")
    return pl.pallas_call(
        lambda *refs: gather_sum_kernel(n_calib, n_peak, *refs),
        out_shape=jax.ShapeDtypeStruct(x.shape, x.dtype),
        in_specs=[pl.BlockSpec(memory_space=pltpu.VMEM)],
        out_specs=pl.BlockSpec(memory_space=pltpu.VMEM),
        scratch_shapes=[
            pltpu.VMEM((n_calib * n_peak,) + x.shape, x.dtype),
            pltpu.SemaphoreType.DMA,
            pltpu.SemaphoreType.DMA,
        ],
        compiler_params=pltpu.CompilerParams(collective_id=0, has_side_effects=True),
    )(x)


def cycle_stats(first, second, present_flag):
    cycle_average = first / present_flag[None, :]
    cycle_rms = jnp.sqrt(second / present_flag[None, :] + 1e-06)
    return (cycle_average, cycle_rms)


def body(raw, pedestal, gain, good, bounds, table):
    frame_dev, mods, row_dev, cols = raw.shape
    n_calib = lax.axis_size("calib")
    n_peak = lax.axis_size("peak")
    mrows = row_dev * n_calib
    slot_rows = mods // SLOT_C
    width_here = cols // n_peak
    frames_all = frame_dev * n_peak
    row_src = lax.axis_index("calib") * row_dev + jnp.arange(row_dev, dtype=jnp.int32)
    corrected = calibrate(raw, pedestal, gain, good, bounds)
    present_part = local_present(good, table, row_src, mrows, slot_rows)
    indices = jnp.arange(mods, dtype=jnp.int32)
    slot_module = jnp.sum(
        jnp.where(table[None, :] == indices[:, None], indices[None, :], 0), axis=1
    )
    ordered = jnp.take(corrected, slot_module, axis=1)
    send = ordered.reshape(frame_dev, mods, row_dev, n_peak, width_here)
    send = jnp.transpose(send, (1, 3, 0, 2, 4)).reshape(mods * n_peak, frame_dev, row_dev, width_here)
    got = lax.all_to_all(send, ("calib", "peak"), 0, 0, tiled=True)
    got = got.reshape(n_calib, n_peak, frame_dev, row_dev, width_here)
    frame = jnp.transpose(got, (1, 2, 0, 3, 4)).reshape(frames_all, mrows, width_here)
    slot = lax.axis_index("calib")
    col_dst = lax.axis_index("peak") * width_here + jnp.arange(width_here, dtype=jnp.int32)
    hits = cycle_onehot(slot, jnp.arange(mrows, dtype=jnp.int32), col_dst, mrows, slot_rows)
    values = frame.reshape(frames_all, -1).astype(jnp.float32)
    first = jnp.einsum("fp,kp->fk", values, hits, precision=precise_variant)
    second = jnp.einsum("fp,kp->fk", values * values, hits, precision=precise_variant)
    lanes = 128
    packed = jnp.concatenate(
        [
            first,
            second,
            jnp.zeros((frames_all, CYCLES), jnp.float32).at[0].set(present_part),
            jnp.zeros((frames_all, lanes - 3 * CYCLES), jnp.float32),
        ],
        axis=1,
    )
    summed = gather_sum(packed)
    first = summed[:, :CYCLES]
    second = summed[:, CYCLES : 2 * CYCLES]
    present_flag = summed[0, 2 * CYCLES : 3 * CYCLES]
    cycle_average, cycle_rms = cycle_stats(first, second, present_flag)
    pixel_mean = jnp.einsum("fk,kp->fp", cycle_average, hits, precision=precise_variant)
    pixel_rms = jnp.einsum("fk,kp->fp", cycle_rms, hits, precision=precise_variant)
    score = ((values - pixel_mean) / pixel_rms).reshape(frames_all, mrows, width_here)
    padded = padded_2(score, (("peak", 2),), 1)
    padded = jnp.pad(padded, ((0, 0), (1, 1), (0, 0)))
    bent = laplace(padded)
    return (score.astype(jnp.bfloat16)[:, None], bent.astype(jnp.bfloat16)[:, None])


def solution(mesh):
    in_specs = (
        P("peak", None, "calib", None),
        P(None, None, "calib", None),
        P(None, None, "calib", None),
        P(None, "calib", None),
        P(),
        P(),
    )
    out_specs = (P(None, "calib", None, "peak"), P(None, "calib", None, "peak"))
    return jax.shard_map(body, mesh=mesh, in_specs=in_specs, out_specs=out_specs, check_vma=False)
```

```python
import jax
import jax.numpy as jnp
from jax import lax
from jax.sharding import PartitionSpec as P
from jax.experimental import pallas as pl
from jax.experimental.pallas import tpu as pltpu

COLS = 1024
BANDS = 8
SLOT_C = 4
CYCLES = 32
CYCLE_W = 64


precise_variant = lax.Precision.HIGHEST


def padded_2(block, sides, width):
    for axis, dim in sides:
        count = lax.axis_size(axis)
        forward = [(i, i + 1) for i in range(count - 1)]
        backward = [(target, source) for source, target in forward]
        low = lax.ppermute(
            lax.slice_in_dim(block, block.shape[dim] - width, None, axis=dim), axis, forward
        )
        high = lax.ppermute(lax.slice_in_dim(block, 0, width, axis=dim), axis, backward)
        block = jnp.concatenate([low, block, high], axis=dim)
    return block


def cycle_index(dist):
    levels = jnp.arange(1, CYCLES, dtype=jnp.int32)
    lows = (2 * CYCLE_W * levels) ** 2
    return jnp.sum((dist[..., None] >= lows).astype(jnp.int32), axis=-1)


def cycle_onehot(slot, row_pos, col_pos, mrows, slot_rows):
    ypos = slot // SLOT_C * mrows + row_pos
    xpos = slot % SLOT_C * COLS + col_pos
    dy_two = 2 * ypos + 1 - slot_rows * mrows
    dx_two = 2 * xpos + 1 - SLOT_C * COLS
    dist = dy_two[:, None] * dy_two[:, None] + dx_two[None, :] * dx_two[None, :]
    levels = jnp.arange(CYCLES, dtype=jnp.int32)
    lows = (2 * CYCLE_W * levels) ** 2
    cycle = jnp.sum((dist[None] >= lows[:, None, None]).astype(jnp.int32), axis=0) - 1
    hits = (cycle[None] == levels[:, None, None]).astype(jnp.float32)
    return hits.reshape(CYCLES, -1)


def calibrate(raw, pedestal, gain, good, bounds):
    code = raw // 2048
    counts_adc = (raw % 2048).astype(jnp.float32)
    base = jnp.where(code == 0, pedestal[0], jnp.where(code == 1, pedestal[1], pedestal[2]))
    gain_factor = gain.astype(jnp.float32)
    scale = jnp.where(
        code == 0, gain_factor[0], jnp.where(code == 1, gain_factor[1], gain_factor[2])
    )
    weight_factor = good.astype(jnp.float32)
    energy = weight_factor * (counts_adc - base) / scale
    columns = jnp.arange(raw.shape[-1], dtype=jnp.int32)
    band = jnp.sum((columns[None, :, None] >= bounds[:, None, :]).astype(jnp.int32), axis=2)
    member_entry = (band[:, :, None] == jnp.arange(BANDS, dtype=jnp.int32)[None, None, :]).astype(
        jnp.float32
    )
    totals = jnp.einsum("fmrc,mcb->fmrb", energy, member_entry, precision=precise_variant)
    present_flag = jnp.einsum(
        "tlg,tgd->tld", weight_factor, member_entry, precision=precise_variant
    )
    level = totals / jnp.maximum(present_flag, 1.0)
    spread = jnp.einsum("fmrb,mcb->fmrc", level, member_entry, precision=precise_variant)
    return (weight_factor * (energy - spread)).astype(jnp.bfloat16)


def calibrate_kernel(table_ref, bounds_ref, raw_ref, ped_ref, gain_ref, good_ref, out_ref):
    module = pl.program_id(0)
    raw = raw_ref[...]
    code = raw // 2048
    counts_adc = (raw % 2048).astype(jnp.float32)
    base = jnp.where(code == 0, ped_ref[0], jnp.where(code == 1, ped_ref[1], ped_ref[2]))
    scale = jnp.where(
        code == 0,
        gain_ref[0].astype(jnp.float32),
        jnp.where(code == 1, gain_ref[1].astype(jnp.float32), gain_ref[2].astype(jnp.float32)),
    )
    weight_factor = good_ref[...].astype(jnp.float32)
    energy = weight_factor * (counts_adc - base) / scale
    cols = raw.shape[-1]
    columns = lax.broadcasted_iota(jnp.int32, (1, cols), 1)
    band = jnp.zeros((1, cols), jnp.int32)
    for j in range(BANDS - 1):
        band = band + (columns >= bounds_ref[module * (BANDS - 1) + j]).astype(jnp.int32)
    spread = jnp.zeros(energy.shape, jnp.float32)
    for b in range(BANDS):
        member = band == b
        totals = jnp.sum(jnp.where(member, energy, 0.0), axis=-1, keepdims=True)
        present = jnp.sum(jnp.where(member, weight_factor, 0.0), axis=-1, keepdims=True)
        spread = jnp.where(member, totals / jnp.maximum(present, 1.0), spread)
    corrected = (weight_factor * (energy - spread)).astype(jnp.bfloat16)
    quarters = out_ref.shape[0]
    width = cols // quarters
    for q in range(quarters):
        out_ref[q] = corrected[:, :, q * width : (q + 1) * width]


def calibrate_send(raw, pedestal, gain, good, bounds, table, n_peak):
    frame_dev, mods, row_dev, cols = raw.shape
    width = cols // n_peak
    grid_spec = pltpu.PrefetchScalarGridSpec(
        num_scalar_prefetch=2,
        grid=(mods,),
        in_specs=[
            pl.BlockSpec((frame_dev, None, row_dev, cols), lambda m, t, b: (0, m, 0, 0)),
            pl.BlockSpec((3, None, row_dev, cols), lambda m, t, b: (0, m, 0, 0)),
            pl.BlockSpec((3, None, row_dev, cols), lambda m, t, b: (0, m, 0, 0)),
            pl.BlockSpec((None, row_dev, cols), lambda m, t, b: (m, 0, 0)),
        ],
        out_specs=pl.BlockSpec(
            (None, n_peak, frame_dev, row_dev, width), lambda m, t, b: (t[m], 0, 0, 0, 0)
        ),
    )
    return pl.pallas_call(
        calibrate_kernel,
        grid_spec=grid_spec,
        out_shape=jax.ShapeDtypeStruct((mods, n_peak, frame_dev, row_dev, width), jnp.bfloat16),
    )(table, bounds.reshape(-1), raw, pedestal, gain, good)


def laplace(padded):
    center = padded[..., 1:-1, 1:-1]
    return (
        4.0 * center
        - padded[..., :-2, 1:-1]
        - padded[..., 2:, 1:-1]
        - padded[..., 1:-1, :-2]
        - padded[..., 1:-1, 2:]
    )


def local_present(good, table, row_src, mrows, slot_rows):
    n_peak = lax.axis_size("peak")
    width = good.shape[2] // n_peak
    start = lax.axis_index("peak") * width
    part = lax.dynamic_slice_in_dim(good, start, width, axis=2)
    col = start + jnp.arange(width, dtype=jnp.int32)
    ypos = (table // SLOT_C)[:, None] * mrows + row_src[None, :]
    xpos = (table % SLOT_C)[:, None] * COLS + col[None, :]
    dy_two = 2 * ypos + 1 - slot_rows * mrows
    dx_two = 2 * xpos + 1 - SLOT_C * COLS
    dist = dy_two[:, :, None] * dy_two[:, :, None] + dx_two[:, None, :] * dx_two[:, None, :]
    cycle = cycle_index(dist)
    levels = jnp.arange(CYCLES, dtype=jnp.int32)
    hit = jnp.where(cycle[..., None] == levels, part[..., None], 0)
    return jnp.sum(hit, axis=(0, 1, 2)).astype(jnp.float32)


def gather_sum_kernel(n_calib, n_peak, x_ref, o_ref, buf, send_sem, recv_sem):
    total = n_calib * n_peak
    me = lax.axis_index("calib") * n_peak + lax.axis_index("peak")
    buf[total - 1] = x_ref[...]
    barrier = pltpu.get_barrier_semaphore()

    def peer_of(step):
        peer = lax.rem(me + step, total)
        return (peer // n_peak, peer % n_peak)

    def greet(step, carry):
        pl.semaphore_signal(
            barrier, inc=1, device_id=peer_of(step), device_id_type=pl.DeviceIdType.MESH
        )
        return carry

    lax.fori_loop(1, total, greet, 0)
    pl.semaphore_wait(barrier, total - 1)

    def send(step, carry):
        pltpu.make_async_remote_copy(
            src_ref=x_ref,
            dst_ref=buf.at[total - 1 - step],
            send_sem=send_sem,
            recv_sem=recv_sem,
            device_id=peer_of(step),
            device_id_type=pl.DeviceIdType.MESH,
        ).start()
        return carry

    lax.fori_loop(1, total, send, 0)
    every = pltpu.make_async_remote_copy(
        src_ref=buf.at[pl.ds(0, total - 1)],
        dst_ref=buf.at[pl.ds(0, total - 1)],
        send_sem=send_sem,
        recv_sem=recv_sem,
        device_id=peer_of(1),
        device_id_type=pl.DeviceIdType.MESH,
    )
    every.wait_send()
    every.wait_recv()

    def add(source, acc):
        return acc + buf[lax.rem(source - me - 1 + 2 * total, total)]

    o_ref[...] = lax.fori_loop(0, total, add, jnp.zeros(x_ref.shape, x_ref.dtype))


def gather_sum(x):
    n_calib = lax.axis_size("calib")
    n_peak = lax.axis_size("peak")
    return pl.pallas_call(
        lambda *refs: gather_sum_kernel(n_calib, n_peak, *refs),
        out_shape=jax.ShapeDtypeStruct(x.shape, x.dtype),
        in_specs=[pl.BlockSpec(memory_space=pltpu.VMEM)],
        out_specs=pl.BlockSpec(memory_space=pltpu.VMEM),
        scratch_shapes=[
            pltpu.VMEM((n_calib * n_peak,) + x.shape, x.dtype),
            pltpu.SemaphoreType.DMA,
            pltpu.SemaphoreType.DMA,
        ],
        compiler_params=pltpu.CompilerParams(collective_id=0, has_side_effects=True),
    )(x)


def cycle_stats(first, second, present_flag):
    cycle_average = first / present_flag[None, :]
    cycle_rms = jnp.sqrt(second / present_flag[None, :] + 1e-06)
    return (cycle_average, cycle_rms)


def body(raw, pedestal, gain, good, bounds, table):
    frame_dev, mods, row_dev, cols = raw.shape
    n_calib = lax.axis_size("calib")
    n_peak = lax.axis_size("peak")
    mrows = row_dev * n_calib
    slot_rows = mods // SLOT_C
    width_here = cols // n_peak
    frames_all = frame_dev * n_peak
    row_src = lax.axis_index("calib") * row_dev + jnp.arange(row_dev, dtype=jnp.int32)
    send = calibrate_send(raw, pedestal, gain, good, bounds, table, n_peak)
    send = send.reshape(mods * n_peak, frame_dev, row_dev, width_here)
    present_part = local_present(good, table, row_src, mrows, slot_rows)
    got = lax.all_to_all(send, ("calib", "peak"), 0, 0, tiled=True)
    got = got.reshape(n_calib, n_peak, frame_dev, row_dev, width_here)
    frame = jnp.transpose(got, (1, 2, 0, 3, 4)).reshape(frames_all, mrows, width_here)
    slot = lax.axis_index("calib")
    col_dst = lax.axis_index("peak") * width_here + jnp.arange(width_here, dtype=jnp.int32)
    hits = cycle_onehot(slot, jnp.arange(mrows, dtype=jnp.int32), col_dst, mrows, slot_rows)
    values = frame.reshape(frames_all, -1).astype(jnp.float32)
    first = jnp.einsum("fp,kp->fk", values, hits, precision=precise_variant)
    second = jnp.einsum("fp,kp->fk", values * values, hits, precision=precise_variant)
    lanes = 128
    packed = jnp.concatenate(
        [
            first,
            second,
            jnp.zeros((frames_all, CYCLES), jnp.float32).at[0].set(present_part),
            jnp.zeros((frames_all, lanes - 3 * CYCLES), jnp.float32),
        ],
        axis=1,
    )
    summed = gather_sum(packed)
    first = summed[:, :CYCLES]
    second = summed[:, CYCLES : 2 * CYCLES]
    present_flag = summed[0, 2 * CYCLES : 3 * CYCLES]
    cycle_average, cycle_rms = cycle_stats(first, second, present_flag)
    pixel_mean = jnp.einsum("fk,kp->fp", cycle_average, hits, precision=precise_variant)
    pixel_rms = jnp.einsum("fk,kp->fp", cycle_rms, hits, precision=precise_variant)
    score = ((values - pixel_mean) / pixel_rms).reshape(frames_all, mrows, width_here)
    padded = padded_2(score, (("peak", 2),), 1)
    padded = jnp.pad(padded, ((0, 0), (1, 1), (0, 0)))
    bent = laplace(padded)
    return (score.astype(jnp.bfloat16)[:, None], bent.astype(jnp.bfloat16)[:, None])


def solution(mesh):
    in_specs = (
        P("peak", None, "calib", None),
        P(None, None, "calib", None),
        P(None, None, "calib", None),
        P(None, "calib", None),
        P(),
        P(),
    )
    out_specs = (P(None, "calib", None, "peak"), P(None, "calib", None, "peak"))
    return jax.shard_map(body, mesh=mesh, in_specs=in_specs, out_specs=out_specs, check_vma=False)
```

```python
import jax
import jax.numpy as jnp
from jax import lax
from jax.sharding import PartitionSpec as P
from jax.experimental import pallas as pl
from jax.experimental.pallas import tpu as pltpu

COLS = 1024
BANDS = 8
SLOT_C = 4
CYCLES = 32
CYCLE_W = 64


precise_variant = lax.Precision.HIGHEST


def padded_2(block, sides, width):
    for axis, dim in sides:
        count = lax.axis_size(axis)
        forward = [(i, i + 1) for i in range(count - 1)]
        backward = [(target, source) for source, target in forward]
        low = lax.ppermute(
            lax.slice_in_dim(block, block.shape[dim] - width, None, axis=dim), axis, forward
        )
        high = lax.ppermute(lax.slice_in_dim(block, 0, width, axis=dim), axis, backward)
        block = jnp.concatenate([low, block, high], axis=dim)
    return block


def cycle_index(dist):
    levels = jnp.arange(1, CYCLES, dtype=jnp.int32)
    lows = (2 * CYCLE_W * levels) ** 2
    return jnp.sum((dist[..., None] >= lows).astype(jnp.int32), axis=-1)


def cycle_onehot(slot, row_pos, col_pos, mrows, slot_rows):
    ypos = slot // SLOT_C * mrows + row_pos
    xpos = slot % SLOT_C * COLS + col_pos
    dy_two = 2 * ypos + 1 - slot_rows * mrows
    dx_two = 2 * xpos + 1 - SLOT_C * COLS
    dist = dy_two[:, None] * dy_two[:, None] + dx_two[None, :] * dx_two[None, :]
    levels = jnp.arange(CYCLES, dtype=jnp.int32)
    lows = (2 * CYCLE_W * levels) ** 2
    cycle = jnp.sum((dist[None] >= lows[:, None, None]).astype(jnp.int32), axis=0) - 1
    hits = (cycle[None] == levels[:, None, None]).astype(jnp.float32)
    return hits.reshape(CYCLES, -1)


def calibrate(raw, pedestal, gain, good, bounds):
    code = raw // 2048
    counts_adc = (raw % 2048).astype(jnp.float32)
    base = jnp.where(code == 0, pedestal[0], jnp.where(code == 1, pedestal[1], pedestal[2]))
    gain_factor = gain.astype(jnp.float32)
    scale = jnp.where(
        code == 0, gain_factor[0], jnp.where(code == 1, gain_factor[1], gain_factor[2])
    )
    weight_factor = good.astype(jnp.float32)
    energy = weight_factor * (counts_adc - base) / scale
    columns = jnp.arange(raw.shape[-1], dtype=jnp.int32)
    band = jnp.sum((columns[None, :, None] >= bounds[:, None, :]).astype(jnp.int32), axis=2)
    member_entry = (band[:, :, None] == jnp.arange(BANDS, dtype=jnp.int32)[None, None, :]).astype(
        jnp.float32
    )
    totals = jnp.einsum("fmrc,mcb->fmrb", energy, member_entry, precision=precise_variant)
    present_flag = jnp.einsum(
        "tlg,tgd->tld", weight_factor, member_entry, precision=precise_variant
    )
    level = totals / jnp.maximum(present_flag, 1.0)
    spread = jnp.einsum("fmrb,mcb->fmrc", level, member_entry, precision=precise_variant)
    return (weight_factor * (energy - spread)).astype(jnp.bfloat16)


def calibrate_kernel(table_ref, bounds_ref, raw_ref, ped_ref, gain_ref, good_ref, out_ref):
    module = pl.program_id(0)
    raw = raw_ref[...]
    code = raw // 2048
    counts_adc = (raw % 2048).astype(jnp.float32)
    base = jnp.where(code == 0, ped_ref[0], jnp.where(code == 1, ped_ref[1], ped_ref[2]))
    scale = jnp.where(
        code == 0,
        gain_ref[0].astype(jnp.float32),
        jnp.where(code == 1, gain_ref[1].astype(jnp.float32), gain_ref[2].astype(jnp.float32)),
    )
    weight_factor = good_ref[...].astype(jnp.float32)
    energy = weight_factor * (counts_adc - base) / scale
    cols = raw.shape[-1]
    columns = lax.broadcasted_iota(jnp.int32, (1, cols), 1)
    band = jnp.zeros((1, cols), jnp.int32)
    for j in range(BANDS - 1):
        band = band + (columns >= bounds_ref[module * (BANDS - 1) + j]).astype(jnp.int32)
    spread = jnp.zeros(energy.shape, jnp.float32)
    for b in range(BANDS):
        member = band == b
        totals = jnp.sum(jnp.where(member, energy, 0.0), axis=-1, keepdims=True)
        present = jnp.sum(jnp.where(member, weight_factor, 0.0), axis=-1, keepdims=True)
        spread = jnp.where(member, totals / jnp.maximum(present, 1.0), spread)
    corrected = (weight_factor * (energy - spread)).astype(jnp.bfloat16)
    quarters = out_ref.shape[0]
    width = cols // quarters
    for q in range(quarters):
        out_ref[q] = corrected[:, :, q * width : (q + 1) * width]


def calibrate_send(raw, pedestal, gain, good, bounds, table, n_peak):
    frame_dev, mods, row_dev, cols = raw.shape
    width = cols // n_peak
    grid_spec = pltpu.PrefetchScalarGridSpec(
        num_scalar_prefetch=2,
        grid=(mods,),
        in_specs=[
            pl.BlockSpec((frame_dev, None, row_dev, cols), lambda m, t, b: (0, m, 0, 0)),
            pl.BlockSpec((3, None, row_dev, cols), lambda m, t, b: (0, m, 0, 0)),
            pl.BlockSpec((3, None, row_dev, cols), lambda m, t, b: (0, m, 0, 0)),
            pl.BlockSpec((None, row_dev, cols), lambda m, t, b: (m, 0, 0)),
        ],
        out_specs=pl.BlockSpec(
            (None, n_peak, frame_dev, row_dev, width), lambda m, t, b: (t[m], 0, 0, 0, 0)
        ),
    )
    return pl.pallas_call(
        calibrate_kernel,
        grid_spec=grid_spec,
        out_shape=jax.ShapeDtypeStruct((mods, n_peak, frame_dev, row_dev, width), jnp.bfloat16),
    )(table, bounds.reshape(-1), raw, pedestal, gain, good)


def laplace(padded):
    center = padded[..., 1:-1, 1:-1]
    return (
        4.0 * center
        - padded[..., :-2, 1:-1]
        - padded[..., 2:, 1:-1]
        - padded[..., 1:-1, :-2]
        - padded[..., 1:-1, 2:]
    )


def local_present(good, table, row_src, mrows, slot_rows):
    n_peak = lax.axis_size("peak")
    width = good.shape[2] // n_peak
    start = lax.axis_index("peak") * width
    part = lax.dynamic_slice_in_dim(good, start, width, axis=2)
    col = start + jnp.arange(width, dtype=jnp.int32)
    ypos = (table // SLOT_C)[:, None] * mrows + row_src[None, :]
    xpos = (table % SLOT_C)[:, None] * COLS + col[None, :]
    dy_two = 2 * ypos + 1 - slot_rows * mrows
    dx_two = 2 * xpos + 1 - SLOT_C * COLS
    dist = dy_two[:, :, None] * dy_two[:, :, None] + dx_two[:, None, :] * dx_two[:, None, :]
    cycle = cycle_index(dist)
    levels = jnp.arange(CYCLES, dtype=jnp.int32)
    hit = jnp.where(cycle[..., None] == levels, part[..., None], 0)
    return jnp.sum(hit, axis=(0, 1, 2)).astype(jnp.float32)


def gather_sum_kernel(n_calib, n_peak, x_ref, o_ref, buf, send_sem, recv_sem):
    total = n_calib * n_peak
    me = lax.axis_index("calib") * n_peak + lax.axis_index("peak")
    buf[total - 1] = x_ref[...]
    barrier = pltpu.get_barrier_semaphore()

    def peer_of(step):
        peer = lax.rem(me + step, total)
        return (peer // n_peak, peer % n_peak)

    def greet(step, carry):
        pl.semaphore_signal(
            barrier, inc=1, device_id=peer_of(step), device_id_type=pl.DeviceIdType.MESH
        )
        return carry

    lax.fori_loop(1, total, greet, 0)
    pl.semaphore_wait(barrier, total - 1)

    def send(step, carry):
        pltpu.make_async_remote_copy(
            src_ref=x_ref,
            dst_ref=buf.at[total - 1 - step],
            send_sem=send_sem,
            recv_sem=recv_sem,
            device_id=peer_of(step),
            device_id_type=pl.DeviceIdType.MESH,
        ).start()
        return carry

    lax.fori_loop(1, total, send, 0)
    every = pltpu.make_async_remote_copy(
        src_ref=buf.at[pl.ds(0, total - 1)],
        dst_ref=buf.at[pl.ds(0, total - 1)],
        send_sem=send_sem,
        recv_sem=recv_sem,
        device_id=peer_of(1),
        device_id_type=pl.DeviceIdType.MESH,
    )
    every.wait_send()
    every.wait_recv()

    def add(source, acc):
        return acc + buf[lax.rem(source - me - 1 + 2 * total, total)]

    o_ref[...] = lax.fori_loop(0, total, add, jnp.zeros(x_ref.shape, x_ref.dtype))


def gather_sum(x):
    n_calib = lax.axis_size("calib")
    n_peak = lax.axis_size("peak")
    return pl.pallas_call(
        lambda *refs: gather_sum_kernel(n_calib, n_peak, *refs),
        out_shape=jax.ShapeDtypeStruct(x.shape, x.dtype),
        in_specs=[pl.BlockSpec(memory_space=pltpu.VMEM)],
        out_specs=pl.BlockSpec(memory_space=pltpu.VMEM),
        scratch_shapes=[
            pltpu.VMEM((n_calib * n_peak,) + x.shape, x.dtype),
            pltpu.SemaphoreType.DMA,
            pltpu.SemaphoreType.DMA,
        ],
        compiler_params=pltpu.CompilerParams(collective_id=0, has_side_effects=True),
    )(x)


def cycle_stats(first, second, present_flag):
    cycle_average = first / present_flag[None, :]
    cycle_rms = jnp.sqrt(second / present_flag[None, :] + 1e-06)
    return (cycle_average, cycle_rms)


def body(raw, pedestal, gain, good, bounds, table):
    frame_dev, mods, row_dev, cols = raw.shape
    n_calib = lax.axis_size("calib")
    n_peak = lax.axis_size("peak")
    mrows = row_dev * n_calib
    slot_rows = mods // SLOT_C
    width_here = cols // n_peak
    frames_all = frame_dev * n_peak
    row_src = lax.axis_index("calib") * row_dev + jnp.arange(row_dev, dtype=jnp.int32)
    send = calibrate_send(raw, pedestal, gain, good, bounds, table, n_peak)
    send = send.reshape(mods * n_peak, frame_dev, row_dev, width_here)
    present_part = local_present(good, table, row_src, mrows, slot_rows)
    got = lax.all_to_all(send, ("calib", "peak"), 0, 0, tiled=True)
    got = got.reshape(n_calib, n_peak, frame_dev, row_dev, width_here)
    frame = jnp.transpose(got, (1, 2, 0, 3, 4)).reshape(frames_all, mrows, width_here)
    slot = lax.axis_index("calib")
    col_dst = lax.axis_index("peak") * width_here + jnp.arange(width_here, dtype=jnp.int32)
    hits = cycle_onehot(slot, jnp.arange(mrows, dtype=jnp.int32), col_dst, mrows, slot_rows)
    hits = hits.astype(jnp.bfloat16)
    pixels = frame.reshape(frames_all, -1)
    values = pixels.astype(jnp.float32)
    square = values * values
    square_top = lax.reduce_precision(square, exponent_bits=8, mantissa_bits=7)
    square_hi = square_top.astype(jnp.bfloat16)
    square_lo = (square - square_top).astype(jnp.bfloat16)
    stacked = jnp.concatenate([pixels, square_hi, square_lo], axis=0)
    sums = jnp.einsum("fp,kp->fk", stacked, hits, preferred_element_type=jnp.float32)
    first = sums[:frames_all]
    second = sums[frames_all : 2 * frames_all] + sums[2 * frames_all :]
    lanes = 128
    packed = jnp.concatenate(
        [
            first,
            second,
            jnp.zeros((frames_all, CYCLES), jnp.float32).at[0].set(present_part),
            jnp.zeros((frames_all, lanes - 3 * CYCLES), jnp.float32),
        ],
        axis=1,
    )
    summed = gather_sum(packed)
    first = summed[:, :CYCLES]
    second = summed[:, CYCLES : 2 * CYCLES]
    present_flag = summed[0, 2 * CYCLES : 3 * CYCLES]
    cycle_average, cycle_rms = cycle_stats(first, second, present_flag)
    table_f32 = jnp.concatenate([cycle_average, cycle_rms], axis=0)
    top_1 = lax.reduce_precision(table_f32, exponent_bits=8, mantissa_bits=7)
    rest = table_f32 - top_1
    top_2 = lax.reduce_precision(rest, exponent_bits=8, mantissa_bits=7)
    piece_1 = top_1.astype(jnp.bfloat16)
    piece_2 = top_2.astype(jnp.bfloat16)
    piece_3 = (rest - top_2).astype(jnp.bfloat16)
    pieces = jnp.concatenate([piece_1, piece_2, piece_3], axis=1)
    hits_3 = jnp.concatenate([hits, hits, hits], axis=0)
    lookup = jnp.einsum("fk,kp->fp", pieces, hits_3, preferred_element_type=jnp.float32)
    pixel_mean = lookup[:frames_all]
    pixel_rms = lookup[frames_all:]
    score = ((values - pixel_mean) / pixel_rms).reshape(frames_all, mrows, width_here)
    padded = padded_2(score, (("peak", 2),), 1)
    padded = jnp.pad(padded, ((0, 0), (1, 1), (0, 0)))
    bent = laplace(padded)
    return (score.astype(jnp.bfloat16)[:, None], bent.astype(jnp.bfloat16)[:, None])


def solution(mesh):
    in_specs = (
        P("peak", None, "calib", None),
        P(None, None, "calib", None),
        P(None, None, "calib", None),
        P(None, "calib", None),
        P(),
        P(),
    )
    out_specs = (P(None, "calib", None, "peak"), P(None, "calib", None, "peak"))
    return jax.shard_map(body, mesh=mesh, in_specs=in_specs, out_specs=out_specs, check_vma=False)
```

```python
import jax
import jax.numpy as jnp
from jax import lax
from jax.sharding import PartitionSpec as P
from jax.experimental import pallas as pl
from jax.experimental.pallas import tpu as pltpu

COLS = 1024
BANDS = 8
SLOT_C = 4
CYCLES = 32
CYCLE_W = 64


precise_variant = lax.Precision.HIGHEST


def padded_2(block, sides, width):
    for axis, dim in sides:
        count = lax.axis_size(axis)
        forward = [(i, i + 1) for i in range(count - 1)]
        backward = [(target, source) for source, target in forward]
        low = lax.ppermute(
            lax.slice_in_dim(block, block.shape[dim] - width, None, axis=dim), axis, forward
        )
        high = lax.ppermute(lax.slice_in_dim(block, 0, width, axis=dim), axis, backward)
        block = jnp.concatenate([low, block, high], axis=dim)
    return block


def cycle_index(dist):
    levels = jnp.arange(1, CYCLES, dtype=jnp.int32)
    lows = (2 * CYCLE_W * levels) ** 2
    return jnp.sum((dist[..., None] >= lows).astype(jnp.int32), axis=-1)


def cycle_onehot(slot, row_pos, col_pos, mrows, slot_rows):
    ypos = slot // SLOT_C * mrows + row_pos
    xpos = slot % SLOT_C * COLS + col_pos
    dy_two = 2 * ypos + 1 - slot_rows * mrows
    dx_two = 2 * xpos + 1 - SLOT_C * COLS
    dist = dy_two[:, None] * dy_two[:, None] + dx_two[None, :] * dx_two[None, :]
    levels = jnp.arange(CYCLES, dtype=jnp.int32)
    lows = (2 * CYCLE_W * levels) ** 2
    cycle = jnp.sum((dist[None] >= lows[:, None, None]).astype(jnp.int32), axis=0) - 1
    hits = (cycle[None] == levels[:, None, None]).astype(jnp.float32)
    return hits.reshape(CYCLES, -1)


def calibrate(raw, pedestal, gain, good, bounds):
    code = raw // 2048
    counts_adc = (raw % 2048).astype(jnp.float32)
    base = jnp.where(code == 0, pedestal[0], jnp.where(code == 1, pedestal[1], pedestal[2]))
    gain_factor = gain.astype(jnp.float32)
    scale = jnp.where(
        code == 0, gain_factor[0], jnp.where(code == 1, gain_factor[1], gain_factor[2])
    )
    weight_factor = good.astype(jnp.float32)
    energy = weight_factor * (counts_adc - base) / scale
    columns = jnp.arange(raw.shape[-1], dtype=jnp.int32)
    band = jnp.sum((columns[None, :, None] >= bounds[:, None, :]).astype(jnp.int32), axis=2)
    member_entry = (band[:, :, None] == jnp.arange(BANDS, dtype=jnp.int32)[None, None, :]).astype(
        jnp.float32
    )
    totals = jnp.einsum("fmrc,mcb->fmrb", energy, member_entry, precision=precise_variant)
    present_flag = jnp.einsum(
        "tlg,tgd->tld", weight_factor, member_entry, precision=precise_variant
    )
    level = totals / jnp.maximum(present_flag, 1.0)
    spread = jnp.einsum("fmrb,mcb->fmrc", level, member_entry, precision=precise_variant)
    return (weight_factor * (energy - spread)).astype(jnp.bfloat16)


def calibrate_kernel(table_ref, bounds_ref, raw_ref, ped_ref, gain_ref, good_ref, out_ref):
    module = pl.program_id(0)
    raw = raw_ref[...]
    code = raw // 2048
    counts_adc = (raw % 2048).astype(jnp.float32)
    base = jnp.where(code == 0, ped_ref[0], jnp.where(code == 1, ped_ref[1], ped_ref[2]))
    scale = jnp.where(
        code == 0,
        gain_ref[0].astype(jnp.float32),
        jnp.where(code == 1, gain_ref[1].astype(jnp.float32), gain_ref[2].astype(jnp.float32)),
    )
    weight_factor = good_ref[...].astype(jnp.float32)
    energy = weight_factor * (counts_adc - base) / scale
    cols = raw.shape[-1]
    columns = lax.broadcasted_iota(jnp.int32, (1, cols), 1)
    band = jnp.zeros((1, cols), jnp.int32)
    for j in range(BANDS - 1):
        band = band + (columns >= bounds_ref[module * (BANDS - 1) + j]).astype(jnp.int32)
    spread = jnp.zeros(energy.shape, jnp.float32)
    for b in range(BANDS):
        member = band == b
        totals = jnp.sum(jnp.where(member, energy, 0.0), axis=-1, keepdims=True)
        present = jnp.sum(jnp.where(member, weight_factor, 0.0), axis=-1, keepdims=True)
        spread = jnp.where(member, totals / jnp.maximum(present, 1.0), spread)
    corrected = (weight_factor * (energy - spread)).astype(jnp.bfloat16)
    quarters = out_ref.shape[0]
    width = cols // quarters
    for q in range(quarters):
        out_ref[q] = corrected[:, :, q * width : (q + 1) * width]


def calibrate_send(raw, pedestal, gain, good, bounds, table, n_peak):
    frame_dev, mods, row_dev, cols = raw.shape
    width = cols // n_peak
    grid_spec = pltpu.PrefetchScalarGridSpec(
        num_scalar_prefetch=2,
        grid=(mods,),
        in_specs=[
            pl.BlockSpec((frame_dev, None, row_dev, cols), lambda m, t, b: (0, m, 0, 0)),
            pl.BlockSpec((3, None, row_dev, cols), lambda m, t, b: (0, m, 0, 0)),
            pl.BlockSpec((3, None, row_dev, cols), lambda m, t, b: (0, m, 0, 0)),
            pl.BlockSpec((None, row_dev, cols), lambda m, t, b: (m, 0, 0)),
        ],
        out_specs=pl.BlockSpec(
            (None, n_peak, frame_dev, row_dev, width), lambda m, t, b: (t[m], 0, 0, 0, 0)
        ),
    )
    return pl.pallas_call(
        calibrate_kernel,
        grid_spec=grid_spec,
        out_shape=jax.ShapeDtypeStruct((mods, n_peak, frame_dev, row_dev, width), jnp.bfloat16),
    )(table, bounds.reshape(-1), raw, pedestal, gain, good)


def laplace(padded):
    center = padded[..., 1:-1, 1:-1]
    return (
        4.0 * center
        - padded[..., :-2, 1:-1]
        - padded[..., 2:, 1:-1]
        - padded[..., 1:-1, :-2]
        - padded[..., 1:-1, 2:]
    )


def local_present(good, table, row_src, mrows, slot_rows):
    n_peak = lax.axis_size("peak")
    width = good.shape[2] // n_peak
    start = lax.axis_index("peak") * width
    part = lax.dynamic_slice_in_dim(good, start, width, axis=2)
    col = start + jnp.arange(width, dtype=jnp.int32)
    ypos = (table // SLOT_C)[:, None] * mrows + row_src[None, :]
    xpos = (table % SLOT_C)[:, None] * COLS + col[None, :]
    dy_two = 2 * ypos + 1 - slot_rows * mrows
    dx_two = 2 * xpos + 1 - SLOT_C * COLS
    dist = dy_two[:, :, None] * dy_two[:, :, None] + dx_two[:, None, :] * dx_two[:, None, :]
    cycle = cycle_index(dist)
    levels = jnp.arange(CYCLES, dtype=jnp.int32)
    hit = jnp.where(cycle[..., None] == levels, part[..., None], 0)
    return jnp.sum(hit, axis=(0, 1, 2)).astype(jnp.float32)


def gather_sum_kernel(n_calib, n_peak, x_ref, o_ref, buf, send_sem, recv_sem):
    total = n_calib * n_peak
    me = lax.axis_index("calib") * n_peak + lax.axis_index("peak")
    buf[total - 1] = x_ref[...]
    barrier = pltpu.get_barrier_semaphore()

    def peer_of(step):
        peer = lax.rem(me + step, total)
        return (peer // n_peak, peer % n_peak)

    def greet(step, carry):
        pl.semaphore_signal(
            barrier, inc=1, device_id=peer_of(step), device_id_type=pl.DeviceIdType.MESH
        )
        return carry

    lax.fori_loop(1, total, greet, 0)
    pl.semaphore_wait(barrier, total - 1)

    def send(step, carry):
        pltpu.make_async_remote_copy(
            src_ref=x_ref,
            dst_ref=buf.at[total - 1 - step],
            send_sem=send_sem,
            recv_sem=recv_sem,
            device_id=peer_of(step),
            device_id_type=pl.DeviceIdType.MESH,
        ).start()
        return carry

    lax.fori_loop(1, total, send, 0)
    every = pltpu.make_async_remote_copy(
        src_ref=buf.at[pl.ds(0, total - 1)],
        dst_ref=buf.at[pl.ds(0, total - 1)],
        send_sem=send_sem,
        recv_sem=recv_sem,
        device_id=peer_of(1),
        device_id_type=pl.DeviceIdType.MESH,
    )
    every.wait_send()
    every.wait_recv()

    def add(source, acc):
        return acc + buf[lax.rem(source - me - 1 + 2 * total, total)]

    o_ref[...] = lax.fori_loop(0, total, add, jnp.zeros(x_ref.shape, x_ref.dtype))


def gather_sum(x):
    n_calib = lax.axis_size("calib")
    n_peak = lax.axis_size("peak")
    return pl.pallas_call(
        lambda *refs: gather_sum_kernel(n_calib, n_peak, *refs),
        out_shape=jax.ShapeDtypeStruct(x.shape, x.dtype),
        in_specs=[pl.BlockSpec(memory_space=pltpu.VMEM)],
        out_specs=pl.BlockSpec(memory_space=pltpu.VMEM),
        scratch_shapes=[
            pltpu.VMEM((n_calib * n_peak,) + x.shape, x.dtype),
            pltpu.SemaphoreType.DMA,
            pltpu.SemaphoreType.DMA,
        ],
        compiler_params=pltpu.CompilerParams(collective_id=0, has_side_effects=True),
    )(x)


def cycle_stats(first, second, present_flag):
    cycle_average = first / present_flag[None, :]
    cycle_rms = jnp.sqrt(second / present_flag[None, :] + 1e-06)
    return (cycle_average, cycle_rms)


def body(raw, pedestal, gain, good, bounds, table):
    frame_dev, mods, row_dev, cols = raw.shape
    n_calib = lax.axis_size("calib")
    n_peak = lax.axis_size("peak")
    mrows = row_dev * n_calib
    slot_rows = mods // SLOT_C
    width_here = cols // n_peak
    frames_all = frame_dev * n_peak
    row_src = lax.axis_index("calib") * row_dev + jnp.arange(row_dev, dtype=jnp.int32)
    send = calibrate_send(raw, pedestal, gain, good, bounds, table, n_peak)
    send = send.reshape(mods * n_peak, frame_dev, row_dev, width_here)
    present_part = local_present(good, table, row_src, mrows, slot_rows)
    got = lax.all_to_all(send, ("calib", "peak"), 0, 0, tiled=True)
    got = got.reshape(n_calib, n_peak, frame_dev, row_dev, width_here)
    frame = jnp.transpose(got, (1, 2, 0, 3, 4)).reshape(frames_all, mrows, width_here)
    slot = lax.axis_index("calib")
    fwd = [(i, i + 1) for i in range(n_peak - 1)]
    bwd = [(i + 1, i) for i in range(n_peak - 1)]
    from_left = lax.ppermute(frame[:, :, width_here - 1 :], "peak", fwd)
    from_right = lax.ppermute(frame[:, :, :1], "peak", bwd)
    edge_values = jnp.concatenate([from_left, from_right], axis=2).astype(jnp.float32)
    peak_start = lax.axis_index("peak") * width_here
    edge_cols = jnp.stack([peak_start - 1, peak_start + width_here])
    col_dst = lax.axis_index("peak") * width_here + jnp.arange(width_here, dtype=jnp.int32)
    hits = cycle_onehot(slot, jnp.arange(mrows, dtype=jnp.int32), col_dst, mrows, slot_rows)
    hits = hits.astype(jnp.bfloat16)
    pixels = frame.reshape(frames_all, -1)
    values = pixels.astype(jnp.float32)
    square = values * values
    square_top = lax.reduce_precision(square, exponent_bits=8, mantissa_bits=7)
    square_hi = square_top.astype(jnp.bfloat16)
    square_lo = (square - square_top).astype(jnp.bfloat16)
    stacked = jnp.concatenate([pixels, square_hi, square_lo], axis=0)
    sums = jnp.einsum("fp,kp->fk", stacked, hits, preferred_element_type=jnp.float32)
    first = sums[:frames_all]
    second = sums[frames_all : 2 * frames_all] + sums[2 * frames_all :]
    lanes = 128
    packed = jnp.concatenate(
        [
            first,
            second,
            jnp.zeros((frames_all, CYCLES), jnp.float32).at[0].set(present_part),
            jnp.zeros((frames_all, lanes - 3 * CYCLES), jnp.float32),
        ],
        axis=1,
    )
    summed = gather_sum(packed)
    first = summed[:, :CYCLES]
    second = summed[:, CYCLES : 2 * CYCLES]
    present_flag = summed[0, 2 * CYCLES : 3 * CYCLES]
    cycle_average, cycle_rms = cycle_stats(first, second, present_flag)
    table_f32 = jnp.concatenate([cycle_average, cycle_rms], axis=0)
    top_1 = lax.reduce_precision(table_f32, exponent_bits=8, mantissa_bits=7)
    rest = table_f32 - top_1
    top_2 = lax.reduce_precision(rest, exponent_bits=8, mantissa_bits=7)
    piece_1 = top_1.astype(jnp.bfloat16)
    piece_2 = top_2.astype(jnp.bfloat16)
    piece_3 = (rest - top_2).astype(jnp.bfloat16)
    pieces = jnp.concatenate([piece_1, piece_2, piece_3], axis=1)
    hits_3 = jnp.concatenate([hits, hits, hits], axis=0)
    lookup = jnp.einsum("fk,kp->fp", pieces, hits_3, preferred_element_type=jnp.float32)
    pixel_mean = lookup[:frames_all]
    pixel_rms = lookup[frames_all:]
    score = ((values - pixel_mean) / pixel_rms).reshape(frames_all, mrows, width_here)
    edge_hits = cycle_onehot(slot, jnp.arange(mrows, dtype=jnp.int32), edge_cols, mrows, slot_rows)
    edge_hits = jnp.concatenate([edge_hits] * 3, axis=0).astype(jnp.bfloat16)
    edge_lookup = jnp.einsum("fk,kp->fp", pieces, edge_hits, preferred_element_type=jnp.float32)
    edge_lookup = edge_lookup.reshape(2 * frames_all, mrows, 2)
    edge_score = (edge_values - edge_lookup[:frames_all]) / edge_lookup[frames_all:]
    peak_pos = lax.axis_index("peak")
    left = jnp.where(peak_pos == 0, 0.0, edge_score[:, :, :1])
    right = jnp.where(peak_pos == n_peak - 1, 0.0, edge_score[:, :, 1:])
    zero_row = jnp.zeros((frames_all, 1, width_here), jnp.float32)
    up = jnp.concatenate([zero_row, score[:, :-1]], axis=1)
    down = jnp.concatenate([score[:, 1:], zero_row], axis=1)
    left_nb = jnp.concatenate([left, score[:, :, :-1]], axis=2)
    right_nb = jnp.concatenate([score[:, :, 1:], right], axis=2)
    bent = 4.0 * score - up - down - left_nb - right_nb
    return (score.astype(jnp.bfloat16)[:, None], bent.astype(jnp.bfloat16)[:, None])


def solution(mesh):
    in_specs = (
        P("peak", None, "calib", None),
        P(None, None, "calib", None),
        P(None, None, "calib", None),
        P(None, "calib", None),
        P(),
        P(),
    )
    out_specs = (P(None, "calib", None, "peak"), P(None, "calib", None, "peak"))
    return jax.shard_map(body, mesh=mesh, in_specs=in_specs, out_specs=out_specs, check_vma=False)
```

```python
import jax
import jax.numpy as jnp
from jax import lax
from jax.sharding import PartitionSpec as P
from jax.experimental import pallas as pl
from jax.experimental.pallas import tpu as pltpu

COLS = 1024
BANDS = 8
SLOT_C = 4
CYCLES = 32
CYCLE_W = 64


precise_variant = lax.Precision.HIGHEST


def padded_2(block, sides, width):
    for axis, dim in sides:
        count = lax.axis_size(axis)
        forward = [(i, i + 1) for i in range(count - 1)]
        backward = [(target, source) for source, target in forward]
        low = lax.ppermute(
            lax.slice_in_dim(block, block.shape[dim] - width, None, axis=dim), axis, forward
        )
        high = lax.ppermute(lax.slice_in_dim(block, 0, width, axis=dim), axis, backward)
        block = jnp.concatenate([low, block, high], axis=dim)
    return block


def cycle_index(dist):
    levels = jnp.arange(1, CYCLES, dtype=jnp.int32)
    lows = (2 * CYCLE_W * levels) ** 2
    return jnp.sum((dist[..., None] >= lows).astype(jnp.int32), axis=-1)


def cycle_onehot(slot, row_pos, col_pos, mrows, slot_rows):
    ypos = slot // SLOT_C * mrows + row_pos
    xpos = slot % SLOT_C * COLS + col_pos
    dy_two = 2 * ypos + 1 - slot_rows * mrows
    dx_two = 2 * xpos + 1 - SLOT_C * COLS
    dist = dy_two[:, None] * dy_two[:, None] + dx_two[None, :] * dx_two[None, :]
    levels = jnp.arange(CYCLES, dtype=jnp.int32)
    lows = (2 * CYCLE_W * levels) ** 2
    cycle = jnp.sum((dist[None] >= lows[:, None, None]).astype(jnp.int32), axis=0) - 1
    hits = (cycle[None] == levels[:, None, None]).astype(jnp.float32)
    return hits.reshape(CYCLES, -1)


def calibrate(raw, pedestal, gain, good, bounds):
    code = raw // 2048
    counts_adc = (raw % 2048).astype(jnp.float32)
    base = jnp.where(code == 0, pedestal[0], jnp.where(code == 1, pedestal[1], pedestal[2]))
    gain_factor = gain.astype(jnp.float32)
    scale = jnp.where(
        code == 0, gain_factor[0], jnp.where(code == 1, gain_factor[1], gain_factor[2])
    )
    weight_factor = good.astype(jnp.float32)
    energy = weight_factor * (counts_adc - base) / scale
    columns = jnp.arange(raw.shape[-1], dtype=jnp.int32)
    band = jnp.sum((columns[None, :, None] >= bounds[:, None, :]).astype(jnp.int32), axis=2)
    member_entry = (band[:, :, None] == jnp.arange(BANDS, dtype=jnp.int32)[None, None, :]).astype(
        jnp.float32
    )
    totals = jnp.einsum("fmrc,mcb->fmrb", energy, member_entry, precision=precise_variant)
    present_flag = jnp.einsum(
        "tlg,tgd->tld", weight_factor, member_entry, precision=precise_variant
    )
    level = totals / jnp.maximum(present_flag, 1.0)
    spread = jnp.einsum("fmrb,mcb->fmrc", level, member_entry, precision=precise_variant)
    return (weight_factor * (energy - spread)).astype(jnp.bfloat16)


def calibrate_kernel(table_ref, bounds_ref, raw_ref, ped_ref, gain_ref, good_ref, out_ref):
    module = pl.program_id(0)
    raw = raw_ref[...]
    code = raw // 2048
    counts_adc = (raw % 2048).astype(jnp.float32)
    base = jnp.where(code == 0, ped_ref[0], jnp.where(code == 1, ped_ref[1], ped_ref[2]))
    scale = jnp.where(
        code == 0,
        gain_ref[0].astype(jnp.float32),
        jnp.where(code == 1, gain_ref[1].astype(jnp.float32), gain_ref[2].astype(jnp.float32)),
    )
    weight_factor = good_ref[...].astype(jnp.float32)
    energy = weight_factor * (counts_adc - base) / scale
    cols = raw.shape[-1]
    columns = lax.broadcasted_iota(jnp.int32, (1, cols), 1)
    band = jnp.zeros((1, cols), jnp.int32)
    for j in range(BANDS - 1):
        band = band + (columns >= bounds_ref[module * (BANDS - 1) + j]).astype(jnp.int32)
    spread = jnp.zeros(energy.shape, jnp.float32)
    for b in range(BANDS):
        member = band == b
        totals = jnp.sum(jnp.where(member, energy, 0.0), axis=-1, keepdims=True)
        present = jnp.sum(jnp.where(member, weight_factor, 0.0), axis=-1, keepdims=True)
        spread = jnp.where(member, totals / jnp.maximum(present, 1.0), spread)
    corrected = (weight_factor * (energy - spread)).astype(jnp.bfloat16)
    quarters = out_ref.shape[0]
    width = cols // quarters
    for q in range(quarters):
        out_ref[q] = corrected[:, :, q * width : (q + 1) * width]


def calibrate_send(raw, pedestal, gain, good, bounds, table, n_peak):
    frame_dev, mods, row_dev, cols = raw.shape
    width = cols // n_peak
    grid_spec = pltpu.PrefetchScalarGridSpec(
        num_scalar_prefetch=2,
        grid=(mods,),
        in_specs=[
            pl.BlockSpec((frame_dev, None, row_dev, cols), lambda m, t, b: (0, m, 0, 0)),
            pl.BlockSpec((3, None, row_dev, cols), lambda m, t, b: (0, m, 0, 0)),
            pl.BlockSpec((3, None, row_dev, cols), lambda m, t, b: (0, m, 0, 0)),
            pl.BlockSpec((None, row_dev, cols), lambda m, t, b: (m, 0, 0)),
        ],
        out_specs=pl.BlockSpec(
            (None, n_peak, frame_dev, row_dev, width), lambda m, t, b: (t[m], 0, 0, 0, 0)
        ),
    )
    return pl.pallas_call(
        calibrate_kernel,
        grid_spec=grid_spec,
        out_shape=jax.ShapeDtypeStruct((mods, n_peak, frame_dev, row_dev, width), jnp.bfloat16),
    )(table, bounds.reshape(-1), raw, pedestal, gain, good)


def laplace_kernel(n_peak, score_ref, left_ref, right_ref, snr_ref, bent_ref):
    score = score_ref[...]
    rows, cols = score.shape
    peak_pos = lax.axis_index("peak")
    row_ids = lax.broadcasted_iota(jnp.int32, (rows, cols), 0)
    col_ids = lax.broadcasted_iota(jnp.int32, (rows, cols), 1)
    left_col = jnp.where(peak_pos == 0, 0.0, left_ref[...])
    right_col = jnp.where(peak_pos == n_peak - 1, 0.0, right_ref[...])
    total = 4.0 * score
    for shift in (1, rows - 1):
        moved = pltpu.roll(score, shift, 0)
        source = pltpu.roll(row_ids, shift, 0)
        total = total - jnp.where(jnp.abs(source - row_ids) == 1, moved, 0.0)
    for shift in (1, cols - 1):
        moved = pltpu.roll(score, shift, 1)
        source = pltpu.roll(col_ids, shift, 1)
        near = jnp.where(source == cols - 1, left_col, right_col)
        total = total - jnp.where(jnp.abs(source - col_ids) == 1, moved, near)
    snr_ref[...] = score.astype(snr_ref.dtype)
    bent_ref[...] = total.astype(bent_ref.dtype)


def score_outputs(score, left, right, n_peak):
    frames, rows, cols = score.shape
    block = pl.BlockSpec((None, rows, cols), lambda f: (f, 0, 0))
    edge = pl.BlockSpec((None, rows, 1), lambda f: (f, 0, 0))
    return pl.pallas_call(
        lambda *refs: laplace_kernel(n_peak, *refs),
        grid=(frames,),
        in_specs=[block, edge, edge],
        out_specs=[block, block],
        out_shape=[jax.ShapeDtypeStruct(score.shape, jnp.bfloat16)] * 2,
    )(score, left, right)


def laplace(padded):
    center = padded[..., 1:-1, 1:-1]
    return (
        4.0 * center
        - padded[..., :-2, 1:-1]
        - padded[..., 2:, 1:-1]
        - padded[..., 1:-1, :-2]
        - padded[..., 1:-1, 2:]
    )


def local_present(good, table, row_src, mrows, slot_rows):
    n_peak = lax.axis_size("peak")
    width = good.shape[2] // n_peak
    start = lax.axis_index("peak") * width
    part = lax.dynamic_slice_in_dim(good, start, width, axis=2)
    col = start + jnp.arange(width, dtype=jnp.int32)
    ypos = (table // SLOT_C)[:, None] * mrows + row_src[None, :]
    xpos = (table % SLOT_C)[:, None] * COLS + col[None, :]
    dy_two = 2 * ypos + 1 - slot_rows * mrows
    dx_two = 2 * xpos + 1 - SLOT_C * COLS
    dist = dy_two[:, :, None] * dy_two[:, :, None] + dx_two[:, None, :] * dx_two[:, None, :]
    cycle = cycle_index(dist)
    levels = jnp.arange(CYCLES, dtype=jnp.int32)
    hit = jnp.where(cycle[..., None] == levels, part[..., None], 0)
    return jnp.sum(hit, axis=(0, 1, 2)).astype(jnp.float32)


def gather_sum_kernel(n_calib, n_peak, x_ref, o_ref, buf, send_sem, recv_sem):
    total = n_calib * n_peak
    me = lax.axis_index("calib") * n_peak + lax.axis_index("peak")
    buf[total - 1] = x_ref[...]
    barrier = pltpu.get_barrier_semaphore()

    def peer_of(step):
        peer = lax.rem(me + step, total)
        return (peer // n_peak, peer % n_peak)

    def greet(step, carry):
        pl.semaphore_signal(
            barrier, inc=1, device_id=peer_of(step), device_id_type=pl.DeviceIdType.MESH
        )
        return carry

    lax.fori_loop(1, total, greet, 0)
    pl.semaphore_wait(barrier, total - 1)

    def send(step, carry):
        pltpu.make_async_remote_copy(
            src_ref=x_ref,
            dst_ref=buf.at[total - 1 - step],
            send_sem=send_sem,
            recv_sem=recv_sem,
            device_id=peer_of(step),
            device_id_type=pl.DeviceIdType.MESH,
        ).start()
        return carry

    lax.fori_loop(1, total, send, 0)
    every = pltpu.make_async_remote_copy(
        src_ref=buf.at[pl.ds(0, total - 1)],
        dst_ref=buf.at[pl.ds(0, total - 1)],
        send_sem=send_sem,
        recv_sem=recv_sem,
        device_id=peer_of(1),
        device_id_type=pl.DeviceIdType.MESH,
    )
    every.wait_send()
    every.wait_recv()

    def add(source, acc):
        return acc + buf[lax.rem(source - me - 1 + 2 * total, total)]

    o_ref[...] = lax.fori_loop(0, total, add, jnp.zeros(x_ref.shape, x_ref.dtype))


def gather_sum(x):
    n_calib = lax.axis_size("calib")
    n_peak = lax.axis_size("peak")
    return pl.pallas_call(
        lambda *refs: gather_sum_kernel(n_calib, n_peak, *refs),
        out_shape=jax.ShapeDtypeStruct(x.shape, x.dtype),
        in_specs=[pl.BlockSpec(memory_space=pltpu.VMEM)],
        out_specs=pl.BlockSpec(memory_space=pltpu.VMEM),
        scratch_shapes=[
            pltpu.VMEM((n_calib * n_peak,) + x.shape, x.dtype),
            pltpu.SemaphoreType.DMA,
            pltpu.SemaphoreType.DMA,
        ],
        compiler_params=pltpu.CompilerParams(collective_id=0, has_side_effects=True),
    )(x)


def cycle_stats(first, second, present_flag):
    cycle_average = first / present_flag[None, :]
    cycle_rms = jnp.sqrt(second / present_flag[None, :] + 1e-06)
    return (cycle_average, cycle_rms)


def body(raw, pedestal, gain, good, bounds, table):
    frame_dev, mods, row_dev, cols = raw.shape
    n_calib = lax.axis_size("calib")
    n_peak = lax.axis_size("peak")
    mrows = row_dev * n_calib
    slot_rows = mods // SLOT_C
    width_here = cols // n_peak
    frames_all = frame_dev * n_peak
    row_src = lax.axis_index("calib") * row_dev + jnp.arange(row_dev, dtype=jnp.int32)
    send = calibrate_send(raw, pedestal, gain, good, bounds, table, n_peak)
    send = send.reshape(mods * n_peak, frame_dev, row_dev, width_here)
    present_part = local_present(good, table, row_src, mrows, slot_rows)
    got = lax.all_to_all(send, ("calib", "peak"), 0, 0, tiled=True)
    got = got.reshape(n_calib, n_peak, frame_dev, row_dev, width_here)
    frame = jnp.transpose(got, (1, 2, 0, 3, 4)).reshape(frames_all, mrows, width_here)
    slot = lax.axis_index("calib")
    col_dst = lax.axis_index("peak") * width_here + jnp.arange(width_here, dtype=jnp.int32)
    hits = cycle_onehot(slot, jnp.arange(mrows, dtype=jnp.int32), col_dst, mrows, slot_rows)
    hits = hits.astype(jnp.bfloat16)
    pixels = frame.reshape(frames_all, -1)
    values = pixels.astype(jnp.float32)
    square = values * values
    square_top = lax.reduce_precision(square, exponent_bits=8, mantissa_bits=7)
    square_hi = square_top.astype(jnp.bfloat16)
    square_lo = (square - square_top).astype(jnp.bfloat16)
    stacked = jnp.concatenate([pixels, square_hi, square_lo], axis=0)
    sums = jnp.einsum("fp,kp->fk", stacked, hits, preferred_element_type=jnp.float32)
    first = sums[:frames_all]
    second = sums[frames_all : 2 * frames_all] + sums[2 * frames_all :]
    lanes = 128
    packed = jnp.concatenate(
        [
            first,
            second,
            jnp.zeros((frames_all, CYCLES), jnp.float32).at[0].set(present_part),
            jnp.zeros((frames_all, lanes - 3 * CYCLES), jnp.float32),
        ],
        axis=1,
    )
    summed = gather_sum(packed)
    first = summed[:, :CYCLES]
    second = summed[:, CYCLES : 2 * CYCLES]
    present_flag = summed[0, 2 * CYCLES : 3 * CYCLES]
    cycle_average, cycle_rms = cycle_stats(first, second, present_flag)
    table_f32 = jnp.concatenate([cycle_average, cycle_rms], axis=0)
    top_1 = lax.reduce_precision(table_f32, exponent_bits=8, mantissa_bits=7)
    rest = table_f32 - top_1
    top_2 = lax.reduce_precision(rest, exponent_bits=8, mantissa_bits=7)
    piece_1 = top_1.astype(jnp.bfloat16)
    piece_2 = top_2.astype(jnp.bfloat16)
    piece_3 = (rest - top_2).astype(jnp.bfloat16)
    pieces = jnp.concatenate([piece_1, piece_2, piece_3], axis=1)
    hits_3 = jnp.concatenate([hits, hits, hits], axis=0)
    lookup = jnp.einsum("fk,kp->fp", pieces, hits_3, preferred_element_type=jnp.float32)
    pixel_mean = lookup[:frames_all]
    pixel_rms = lookup[frames_all:]
    score = ((values - pixel_mean) / pixel_rms).reshape(frames_all, mrows, width_here)
    fwd = [(i, i + 1) for i in range(n_peak - 1)]
    bwd = [(i + 1, i) for i in range(n_peak - 1)]
    left = lax.ppermute(score[:, :, width_here - 1 :], "peak", fwd)
    right = lax.ppermute(score[:, :, :1], "peak", bwd)
    snr, bent = score_outputs(score, left, right, n_peak)
    return (snr[:, None], bent[:, None])


def solution(mesh):
    in_specs = (
        P("peak", None, "calib", None),
        P(None, None, "calib", None),
        P(None, None, "calib", None),
        P(None, "calib", None),
        P(),
        P(),
    )
    out_specs = (P(None, "calib", None, "peak"), P(None, "calib", None, "peak"))
    return jax.shard_map(body, mesh=mesh, in_specs=in_specs, out_specs=out_specs, check_vma=False)
```

```python
import jax
import jax.numpy as jnp
from jax import lax
from jax.sharding import PartitionSpec as P
from jax.experimental import pallas as pl
from jax.experimental.pallas import tpu as pltpu

COLS = 1024
BANDS = 8
SLOT_C = 4
CYCLES = 32
CYCLE_W = 64


precise_variant = lax.Precision.HIGHEST


def padded_2(block, sides, width):
    for axis, dim in sides:
        count = lax.axis_size(axis)
        forward = [(i, i + 1) for i in range(count - 1)]
        backward = [(target, source) for source, target in forward]
        low = lax.ppermute(
            lax.slice_in_dim(block, block.shape[dim] - width, None, axis=dim), axis, forward
        )
        high = lax.ppermute(lax.slice_in_dim(block, 0, width, axis=dim), axis, backward)
        block = jnp.concatenate([low, block, high], axis=dim)
    return block


def cycle_index(dist):
    levels = jnp.arange(1, CYCLES, dtype=jnp.int32)
    lows = (2 * CYCLE_W * levels) ** 2
    return jnp.sum((dist[..., None] >= lows).astype(jnp.int32), axis=-1)


def cycle_onehot(slot, row_pos, col_pos, mrows, slot_rows):
    ypos = slot // SLOT_C * mrows + row_pos
    xpos = slot % SLOT_C * COLS + col_pos
    dy_two = 2 * ypos + 1 - slot_rows * mrows
    dx_two = 2 * xpos + 1 - SLOT_C * COLS
    dist = dy_two[:, None] * dy_two[:, None] + dx_two[None, :] * dx_two[None, :]
    levels = jnp.arange(CYCLES, dtype=jnp.int32)
    lows = (2 * CYCLE_W * levels) ** 2
    cycle = jnp.sum((dist[None] >= lows[:, None, None]).astype(jnp.int32), axis=0) - 1
    hits = (cycle[None] == levels[:, None, None]).astype(jnp.float32)
    return hits.reshape(CYCLES, -1)


def calibrate(raw, pedestal, gain, good, bounds):
    code = raw // 2048
    counts_adc = (raw % 2048).astype(jnp.float32)
    base = jnp.where(code == 0, pedestal[0], jnp.where(code == 1, pedestal[1], pedestal[2]))
    gain_factor = gain.astype(jnp.float32)
    scale = jnp.where(
        code == 0, gain_factor[0], jnp.where(code == 1, gain_factor[1], gain_factor[2])
    )
    weight_factor = good.astype(jnp.float32)
    energy = weight_factor * (counts_adc - base) / scale
    columns = jnp.arange(raw.shape[-1], dtype=jnp.int32)
    band = jnp.sum((columns[None, :, None] >= bounds[:, None, :]).astype(jnp.int32), axis=2)
    member_entry = (band[:, :, None] == jnp.arange(BANDS, dtype=jnp.int32)[None, None, :]).astype(
        jnp.float32
    )
    totals = jnp.einsum("fmrc,mcb->fmrb", energy, member_entry, precision=precise_variant)
    present_flag = jnp.einsum(
        "tlg,tgd->tld", weight_factor, member_entry, precision=precise_variant
    )
    level = totals / jnp.maximum(present_flag, 1.0)
    spread = jnp.einsum("fmrb,mcb->fmrc", level, member_entry, precision=precise_variant)
    return (weight_factor * (energy - spread)).astype(jnp.bfloat16)


def calibrate_kernel(group, table_ref, bounds_ref, raw_ref, ped_ref, gain_ref, good_ref, out_ref):
    step = pl.program_id(0)
    cols = raw_ref.shape[-1]
    columns = lax.broadcasted_iota(jnp.int32, (1, cols), 1)
    quarters = out_ref.shape[1]
    width = cols // quarters
    for inner in range(group):
        module = step * group + inner
        raw = raw_ref[:, inner]
        code = raw // 2048
        counts_adc = (raw % 2048).astype(jnp.float32)
        base = jnp.where(
            code == 0, ped_ref[0, inner], jnp.where(code == 1, ped_ref[1, inner], ped_ref[2, inner])
        )
        scale = jnp.where(
            code == 0,
            gain_ref[0, inner].astype(jnp.float32),
            jnp.where(
                code == 1,
                gain_ref[1, inner].astype(jnp.float32),
                gain_ref[2, inner].astype(jnp.float32),
            ),
        )
        weight_factor = good_ref[inner].astype(jnp.float32)
        energy = weight_factor * (counts_adc - base) / scale
        band = jnp.zeros((1, cols), jnp.int32)
        for j in range(BANDS - 1):
            band = band + (columns >= bounds_ref[module * (BANDS - 1) + j]).astype(jnp.int32)
        spread = jnp.zeros(energy.shape, jnp.float32)
        for b in range(BANDS):
            member = band == b
            totals = jnp.sum(jnp.where(member, energy, 0.0), axis=-1, keepdims=True)
            present = jnp.sum(jnp.where(member, weight_factor, 0.0), axis=-1, keepdims=True)
            spread = jnp.where(member, totals / jnp.maximum(present, 1.0), spread)
        corrected = (weight_factor * (energy - spread)).astype(jnp.bfloat16)
        slot = table_ref[module]
        for q in range(quarters):
            out_ref[slot, q] = corrected[:, :, q * width : (q + 1) * width]


def calibrate_send(raw, pedestal, gain, good, bounds, table, n_peak):
    frame_dev, mods, row_dev, cols = raw.shape
    width = cols // n_peak
    group = 4
    grid_spec = pltpu.PrefetchScalarGridSpec(
        num_scalar_prefetch=2,
        grid=(mods // group,),
        in_specs=[
            pl.BlockSpec((frame_dev, group, row_dev, cols), lambda m, t, b: (0, m, 0, 0)),
            pl.BlockSpec((3, group, row_dev, cols), lambda m, t, b: (0, m, 0, 0)),
            pl.BlockSpec((3, group, row_dev, cols), lambda m, t, b: (0, m, 0, 0)),
            pl.BlockSpec((group, row_dev, cols), lambda m, t, b: (m, 0, 0)),
        ],
        out_specs=pl.BlockSpec(
            (mods, n_peak, frame_dev, row_dev, width), lambda m, t, b: (0, 0, 0, 0, 0)
        ),
    )
    return pl.pallas_call(
        lambda *refs: calibrate_kernel(group, *refs),
        grid_spec=grid_spec,
        out_shape=jax.ShapeDtypeStruct((mods, n_peak, frame_dev, row_dev, width), jnp.bfloat16),
    )(table, bounds.reshape(-1), raw, pedestal, gain, good)


def laplace_kernel(n_peak, score_ref, left_ref, right_ref, snr_ref, bent_ref):
    score = score_ref[...]
    rows, cols = score.shape
    peak_pos = lax.axis_index("peak")
    row_ids = lax.broadcasted_iota(jnp.int32, (rows, cols), 0)
    col_ids = lax.broadcasted_iota(jnp.int32, (rows, cols), 1)
    left_col = jnp.where(peak_pos == 0, 0.0, left_ref[...])
    right_col = jnp.where(peak_pos == n_peak - 1, 0.0, right_ref[...])
    total = 4.0 * score
    for shift in (1, rows - 1):
        moved = pltpu.roll(score, shift, 0)
        source = pltpu.roll(row_ids, shift, 0)
        total = total - jnp.where(jnp.abs(source - row_ids) == 1, moved, 0.0)
    for shift in (1, cols - 1):
        moved = pltpu.roll(score, shift, 1)
        source = pltpu.roll(col_ids, shift, 1)
        near = jnp.where(source == cols - 1, left_col, right_col)
        total = total - jnp.where(jnp.abs(source - col_ids) == 1, moved, near)
    snr_ref[...] = score.astype(snr_ref.dtype)
    bent_ref[...] = total.astype(bent_ref.dtype)


def score_outputs(score, left, right, n_peak):
    frames, rows, cols = score.shape
    block = pl.BlockSpec((None, rows, cols), lambda f: (f, 0, 0))
    edge = pl.BlockSpec((None, rows, 1), lambda f: (f, 0, 0))
    return pl.pallas_call(
        lambda *refs: laplace_kernel(n_peak, *refs),
        grid=(frames,),
        in_specs=[block, edge, edge],
        out_specs=[block, block],
        out_shape=[jax.ShapeDtypeStruct(score.shape, jnp.bfloat16)] * 2,
    )(score, left, right)


def laplace(padded):
    center = padded[..., 1:-1, 1:-1]
    return (
        4.0 * center
        - padded[..., :-2, 1:-1]
        - padded[..., 2:, 1:-1]
        - padded[..., 1:-1, :-2]
        - padded[..., 1:-1, 2:]
    )


def local_present(good, table, row_src, mrows, slot_rows):
    n_peak = lax.axis_size("peak")
    width = good.shape[2] // n_peak
    start = lax.axis_index("peak") * width
    part = lax.dynamic_slice_in_dim(good, start, width, axis=2)
    col = start + jnp.arange(width, dtype=jnp.int32)
    ypos = (table // SLOT_C)[:, None] * mrows + row_src[None, :]
    xpos = (table % SLOT_C)[:, None] * COLS + col[None, :]
    dy_two = 2 * ypos + 1 - slot_rows * mrows
    dx_two = 2 * xpos + 1 - SLOT_C * COLS
    dist = dy_two[:, :, None] * dy_two[:, :, None] + dx_two[:, None, :] * dx_two[:, None, :]
    cycle = cycle_index(dist)
    levels = jnp.arange(CYCLES, dtype=jnp.int32)
    hit = jnp.where(cycle[..., None] == levels, part[..., None], 0)
    return jnp.sum(hit, axis=(0, 1, 2)).astype(jnp.float32)


def gather_sum_kernel(n_calib, n_peak, x_ref, o_ref, buf, send_sem, recv_sem):
    total = n_calib * n_peak
    me = lax.axis_index("calib") * n_peak + lax.axis_index("peak")
    buf[total - 1] = x_ref[...]
    barrier = pltpu.get_barrier_semaphore()

    def peer_of(step):
        peer = lax.rem(me + step, total)
        return (peer // n_peak, peer % n_peak)

    def greet(step, carry):
        pl.semaphore_signal(
            barrier, inc=1, device_id=peer_of(step), device_id_type=pl.DeviceIdType.MESH
        )
        return carry

    lax.fori_loop(1, total, greet, 0)
    pl.semaphore_wait(barrier, total - 1)

    def send(step, carry):
        pltpu.make_async_remote_copy(
            src_ref=x_ref,
            dst_ref=buf.at[total - 1 - step],
            send_sem=send_sem,
            recv_sem=recv_sem,
            device_id=peer_of(step),
            device_id_type=pl.DeviceIdType.MESH,
        ).start()
        return carry

    lax.fori_loop(1, total, send, 0)
    every = pltpu.make_async_remote_copy(
        src_ref=buf.at[pl.ds(0, total - 1)],
        dst_ref=buf.at[pl.ds(0, total - 1)],
        send_sem=send_sem,
        recv_sem=recv_sem,
        device_id=peer_of(1),
        device_id_type=pl.DeviceIdType.MESH,
    )
    every.wait_send()
    every.wait_recv()

    def add(source, acc):
        return acc + buf[lax.rem(source - me - 1 + 2 * total, total)]

    o_ref[...] = lax.fori_loop(0, total, add, jnp.zeros(x_ref.shape, x_ref.dtype))


def gather_sum(x):
    n_calib = lax.axis_size("calib")
    n_peak = lax.axis_size("peak")
    return pl.pallas_call(
        lambda *refs: gather_sum_kernel(n_calib, n_peak, *refs),
        out_shape=jax.ShapeDtypeStruct(x.shape, x.dtype),
        in_specs=[pl.BlockSpec(memory_space=pltpu.VMEM)],
        out_specs=pl.BlockSpec(memory_space=pltpu.VMEM),
        scratch_shapes=[
            pltpu.VMEM((n_calib * n_peak,) + x.shape, x.dtype),
            pltpu.SemaphoreType.DMA,
            pltpu.SemaphoreType.DMA,
        ],
        compiler_params=pltpu.CompilerParams(collective_id=0, has_side_effects=True),
    )(x)


def cycle_stats(first, second, present_flag):
    cycle_average = first / present_flag[None, :]
    cycle_rms = jnp.sqrt(second / present_flag[None, :] + 1e-06)
    return (cycle_average, cycle_rms)


def body(raw, pedestal, gain, good, bounds, table):
    frame_dev, mods, row_dev, cols = raw.shape
    n_calib = lax.axis_size("calib")
    n_peak = lax.axis_size("peak")
    mrows = row_dev * n_calib
    slot_rows = mods // SLOT_C
    width_here = cols // n_peak
    frames_all = frame_dev * n_peak
    row_src = lax.axis_index("calib") * row_dev + jnp.arange(row_dev, dtype=jnp.int32)
    send = calibrate_send(raw, pedestal, gain, good, bounds, table, n_peak)
    send = send.reshape(mods * n_peak, frame_dev, row_dev, width_here)
    present_part = local_present(good, table, row_src, mrows, slot_rows)
    got = lax.all_to_all(send, ("calib", "peak"), 0, 0, tiled=True)
    got = got.reshape(n_calib, n_peak, frame_dev, row_dev, width_here)
    frame = jnp.transpose(got, (1, 2, 0, 3, 4)).reshape(frames_all, mrows, width_here)
    slot = lax.axis_index("calib")
    col_dst = lax.axis_index("peak") * width_here + jnp.arange(width_here, dtype=jnp.int32)
    hits = cycle_onehot(slot, jnp.arange(mrows, dtype=jnp.int32), col_dst, mrows, slot_rows)
    hits = hits.astype(jnp.bfloat16)
    pixels = frame.reshape(frames_all, -1)
    values = pixels.astype(jnp.float32)
    square = values * values
    square_top = lax.reduce_precision(square, exponent_bits=8, mantissa_bits=7)
    square_hi = square_top.astype(jnp.bfloat16)
    square_lo = (square - square_top).astype(jnp.bfloat16)
    stacked = jnp.concatenate([pixels, square_hi, square_lo], axis=0)
    sums = jnp.einsum("fp,kp->fk", stacked, hits, preferred_element_type=jnp.float32)
    first = sums[:frames_all]
    second = sums[frames_all : 2 * frames_all] + sums[2 * frames_all :]
    lanes = 128
    packed = jnp.concatenate(
        [
            first,
            second,
            jnp.zeros((frames_all, CYCLES), jnp.float32).at[0].set(present_part),
            jnp.zeros((frames_all, lanes - 3 * CYCLES), jnp.float32),
        ],
        axis=1,
    )
    summed = gather_sum(packed)
    first = summed[:, :CYCLES]
    second = summed[:, CYCLES : 2 * CYCLES]
    present_flag = summed[0, 2 * CYCLES : 3 * CYCLES]
    cycle_average, cycle_rms = cycle_stats(first, second, present_flag)
    table_f32 = jnp.concatenate([cycle_average, cycle_rms], axis=0)
    top_1 = lax.reduce_precision(table_f32, exponent_bits=8, mantissa_bits=7)
    rest = table_f32 - top_1
    top_2 = lax.reduce_precision(rest, exponent_bits=8, mantissa_bits=7)
    piece_1 = top_1.astype(jnp.bfloat16)
    piece_2 = top_2.astype(jnp.bfloat16)
    piece_3 = (rest - top_2).astype(jnp.bfloat16)
    pieces = jnp.concatenate([piece_1, piece_2, piece_3], axis=1)
    hits_3 = jnp.concatenate([hits, hits, hits], axis=0)
    lookup = jnp.einsum("fk,kp->fp", pieces, hits_3, preferred_element_type=jnp.float32)
    pixel_mean = lookup[:frames_all]
    pixel_rms = lookup[frames_all:]
    score = ((values - pixel_mean) / pixel_rms).reshape(frames_all, mrows, width_here)
    fwd = [(i, i + 1) for i in range(n_peak - 1)]
    bwd = [(i + 1, i) for i in range(n_peak - 1)]
    left = lax.ppermute(score[:, :, width_here - 1 :], "peak", fwd)
    right = lax.ppermute(score[:, :, :1], "peak", bwd)
    snr, bent = score_outputs(score, left, right, n_peak)
    return (snr[:, None], bent[:, None])


def solution(mesh):
    in_specs = (
        P("peak", None, "calib", None),
        P(None, None, "calib", None),
        P(None, None, "calib", None),
        P(None, "calib", None),
        P(),
        P(),
    )
    out_specs = (P(None, "calib", None, "peak"), P(None, "calib", None, "peak"))
    return jax.shard_map(body, mesh=mesh, in_specs=in_specs, out_specs=out_specs, check_vma=False)
```

```python
import jax
import jax.numpy as jnp
from jax import lax
from jax.sharding import PartitionSpec as P
from jax.experimental import pallas as pl
from jax.experimental.pallas import tpu as pltpu

COLS = 1024
BANDS = 8
SLOT_C = 4
CYCLES = 32
CYCLE_W = 64


precise_variant = lax.Precision.HIGHEST


def padded_2(block, sides, width):
    for axis, dim in sides:
        count = lax.axis_size(axis)
        forward = [(i, i + 1) for i in range(count - 1)]
        backward = [(target, source) for source, target in forward]
        low = lax.ppermute(
            lax.slice_in_dim(block, block.shape[dim] - width, None, axis=dim), axis, forward
        )
        high = lax.ppermute(lax.slice_in_dim(block, 0, width, axis=dim), axis, backward)
        block = jnp.concatenate([low, block, high], axis=dim)
    return block


def cycle_index(dist):
    levels = jnp.arange(1, CYCLES, dtype=jnp.int32)
    lows = (2 * CYCLE_W * levels) ** 2
    return jnp.sum((dist[..., None] >= lows).astype(jnp.int32), axis=-1)


def cycle_onehot(slot, row_pos, col_pos, mrows, slot_rows):
    ypos = slot // SLOT_C * mrows + row_pos
    xpos = slot % SLOT_C * COLS + col_pos
    dy_two = 2 * ypos + 1 - slot_rows * mrows
    dx_two = 2 * xpos + 1 - SLOT_C * COLS
    dist = dy_two[:, None] * dy_two[:, None] + dx_two[None, :] * dx_two[None, :]
    levels = jnp.arange(CYCLES, dtype=jnp.int32)
    lows = (2 * CYCLE_W * levels) ** 2
    cycle = jnp.sum((dist[None] >= lows[:, None, None]).astype(jnp.int32), axis=0) - 1
    hits = (cycle[None] == levels[:, None, None]).astype(jnp.float32)
    return hits.reshape(CYCLES, -1)


def calibrate(raw, pedestal, gain, good, bounds):
    code = raw // 2048
    counts_adc = (raw % 2048).astype(jnp.float32)
    base = jnp.where(code == 0, pedestal[0], jnp.where(code == 1, pedestal[1], pedestal[2]))
    gain_factor = gain.astype(jnp.float32)
    scale = jnp.where(
        code == 0, gain_factor[0], jnp.where(code == 1, gain_factor[1], gain_factor[2])
    )
    weight_factor = good.astype(jnp.float32)
    energy = weight_factor * (counts_adc - base) / scale
    columns = jnp.arange(raw.shape[-1], dtype=jnp.int32)
    band = jnp.sum((columns[None, :, None] >= bounds[:, None, :]).astype(jnp.int32), axis=2)
    member_entry = (band[:, :, None] == jnp.arange(BANDS, dtype=jnp.int32)[None, None, :]).astype(
        jnp.float32
    )
    totals = jnp.einsum("fmrc,mcb->fmrb", energy, member_entry, precision=precise_variant)
    present_flag = jnp.einsum(
        "tlg,tgd->tld", weight_factor, member_entry, precision=precise_variant
    )
    level = totals / jnp.maximum(present_flag, 1.0)
    spread = jnp.einsum("fmrb,mcb->fmrc", level, member_entry, precision=precise_variant)
    return (weight_factor * (energy - spread)).astype(jnp.bfloat16)


def calibrate_kernel(group, table_ref, bounds_ref, raw_ref, ped_ref, gain_ref, good_ref, out_ref):
    step = pl.program_id(0)
    cols = raw_ref.shape[-1]
    columns = lax.broadcasted_iota(jnp.int32, (1, cols), 1)
    quarters = out_ref.shape[1]
    width = cols // quarters
    for inner in range(group):
        module = step * group + inner
        raw = raw_ref[:, inner]
        code = raw // 2048
        counts_adc = (raw % 2048).astype(jnp.float32)
        base = jnp.where(
            code == 0, ped_ref[0, inner], jnp.where(code == 1, ped_ref[1, inner], ped_ref[2, inner])
        )
        scale = jnp.where(
            code == 0,
            gain_ref[0, inner].astype(jnp.float32),
            jnp.where(
                code == 1,
                gain_ref[1, inner].astype(jnp.float32),
                gain_ref[2, inner].astype(jnp.float32),
            ),
        )
        weight_factor = good_ref[inner].astype(jnp.float32)
        energy = weight_factor * (counts_adc - base) / scale
        band = jnp.zeros((1, cols), jnp.int32)
        for j in range(BANDS - 1):
            band = band + (columns >= bounds_ref[module * (BANDS - 1) + j]).astype(jnp.int32)
        spread = jnp.zeros(energy.shape, jnp.float32)
        for b in range(BANDS):
            member = band == b
            totals = jnp.sum(jnp.where(member, energy, 0.0), axis=-1, keepdims=True)
            present = jnp.sum(jnp.where(member, weight_factor, 0.0), axis=-1, keepdims=True)
            spread = jnp.where(member, totals / jnp.maximum(present, 1.0), spread)
        corrected = (weight_factor * (energy - spread)).astype(jnp.bfloat16)
        slot = table_ref[module]
        for q in range(quarters):
            out_ref[slot, q] = corrected[:, :, q * width : (q + 1) * width]


def calibrate_send(raw, pedestal, gain, good, bounds, table, n_peak):
    frame_dev, mods, row_dev, cols = raw.shape
    width = cols // n_peak
    group = 4
    grid_spec = pltpu.PrefetchScalarGridSpec(
        num_scalar_prefetch=2,
        grid=(mods // group,),
        in_specs=[
            pl.BlockSpec((frame_dev, group, row_dev, cols), lambda m, t, b: (0, m, 0, 0)),
            pl.BlockSpec((3, group, row_dev, cols), lambda m, t, b: (0, m, 0, 0)),
            pl.BlockSpec((3, group, row_dev, cols), lambda m, t, b: (0, m, 0, 0)),
            pl.BlockSpec((group, row_dev, cols), lambda m, t, b: (m, 0, 0)),
        ],
        out_specs=pl.BlockSpec(
            (mods, n_peak, frame_dev, row_dev, width), lambda m, t, b: (0, 0, 0, 0, 0)
        ),
    )
    return pl.pallas_call(
        lambda *refs: calibrate_kernel(group, *refs),
        grid_spec=grid_spec,
        out_shape=jax.ShapeDtypeStruct((mods, n_peak, frame_dev, row_dev, width), jnp.bfloat16),
    )(table, bounds.reshape(-1), raw, pedestal, gain, good)


def score_kernel(n_peak, levels, low_ref, mean_ref, rms_ref, frame_ref, cycle_ref, left_ref, right_ref, snr_ref, bent_ref):
    frame_pos = pl.program_id(0)
    cycle = cycle_ref[...]
    values = frame_ref[...].astype(jnp.float32)
    rows, cols = values.shape
    tops = mean_ref.shape[1] - 1
    pixel_mean = jnp.zeros((rows, cols), jnp.float32)
    pixel_rms = jnp.ones((rows, cols), jnp.float32)
    for j in range(levels):
        level = jnp.minimum(low_ref[0] + j, tops)
        hit = cycle == level
        pixel_mean = jnp.where(hit, mean_ref[frame_pos, level], pixel_mean)
        pixel_rms = jnp.where(hit, rms_ref[frame_pos, level], pixel_rms)
    score = (values - pixel_mean) / pixel_rms
    peak_pos = lax.axis_index("peak")
    row_ids = lax.broadcasted_iota(jnp.int32, (rows, cols), 0)
    col_ids = lax.broadcasted_iota(jnp.int32, (rows, cols), 1)
    left_col = jnp.where(peak_pos == 0, 0.0, left_ref[...])
    right_col = jnp.where(peak_pos == n_peak - 1, 0.0, right_ref[...])
    total = 4.0 * score
    for shift in (1, rows - 1):
        moved = pltpu.roll(score, shift, 0)
        source = pltpu.roll(row_ids, shift, 0)
        total = total - jnp.where(jnp.abs(source - row_ids) == 1, moved, 0.0)
    for shift in (1, cols - 1):
        moved = pltpu.roll(score, shift, 1)
        source = pltpu.roll(col_ids, shift, 1)
        near = jnp.where(source == cols - 1, left_col, right_col)
        total = total - jnp.where(jnp.abs(source - col_ids) == 1, moved, near)
    snr_ref[...] = score.astype(snr_ref.dtype)
    bent_ref[...] = total.astype(bent_ref.dtype)


def score_outputs(frame, cycle, cycle_average, cycle_rms, left, right, n_peak):
    frames, rows, cols = frame.shape
    span = (rows * rows + cols * cols) ** 0.5
    levels = min(CYCLES, int(span // CYCLE_W) + 3)
    low = jnp.min(cycle).reshape(1)
    block = pl.BlockSpec((None, rows, cols), lambda f, *_: (f, 0, 0))
    edge = pl.BlockSpec((None, rows, 1), lambda f, *_: (f, 0, 0))
    grid_spec = pltpu.PrefetchScalarGridSpec(
        num_scalar_prefetch=3,
        grid=(frames,),
        in_specs=[block, pl.BlockSpec((rows, cols), lambda f, *_: (0, 0)), edge, edge],
        out_specs=[block, block],
    )
    return pl.pallas_call(
        lambda *refs: score_kernel(n_peak, levels, *refs),
        grid_spec=grid_spec,
        out_shape=[jax.ShapeDtypeStruct(frame.shape, jnp.bfloat16)] * 2,
    )(low, cycle_average, cycle_rms, frame, cycle, left, right)


def laplace(padded):
    center = padded[..., 1:-1, 1:-1]
    return (
        4.0 * center
        - padded[..., :-2, 1:-1]
        - padded[..., 2:, 1:-1]
        - padded[..., 1:-1, :-2]
        - padded[..., 1:-1, 2:]
    )


def local_present(good, table, row_src, mrows, slot_rows):
    n_peak = lax.axis_size("peak")
    width = good.shape[2] // n_peak
    start = lax.axis_index("peak") * width
    part = lax.dynamic_slice_in_dim(good, start, width, axis=2)
    col = start + jnp.arange(width, dtype=jnp.int32)
    ypos = (table // SLOT_C)[:, None] * mrows + row_src[None, :]
    xpos = (table % SLOT_C)[:, None] * COLS + col[None, :]
    dy_two = 2 * ypos + 1 - slot_rows * mrows
    dx_two = 2 * xpos + 1 - SLOT_C * COLS
    dist = dy_two[:, :, None] * dy_two[:, :, None] + dx_two[:, None, :] * dx_two[:, None, :]
    cycle = cycle_index(dist)
    levels = jnp.arange(CYCLES, dtype=jnp.int32)
    hit = jnp.where(cycle[..., None] == levels, part[..., None], 0)
    return jnp.sum(hit, axis=(0, 1, 2)).astype(jnp.float32)


def gather_sum_kernel(n_calib, n_peak, x_ref, o_ref, buf, send_sem, recv_sem):
    total = n_calib * n_peak
    me = lax.axis_index("calib") * n_peak + lax.axis_index("peak")
    buf[total - 1] = x_ref[...]
    barrier = pltpu.get_barrier_semaphore()

    def peer_of(step):
        peer = lax.rem(me + step, total)
        return (peer // n_peak, peer % n_peak)

    def greet(step, carry):
        pl.semaphore_signal(
            barrier, inc=1, device_id=peer_of(step), device_id_type=pl.DeviceIdType.MESH
        )
        return carry

    lax.fori_loop(1, total, greet, 0)
    pl.semaphore_wait(barrier, total - 1)

    def send(step, carry):
        pltpu.make_async_remote_copy(
            src_ref=x_ref,
            dst_ref=buf.at[total - 1 - step],
            send_sem=send_sem,
            recv_sem=recv_sem,
            device_id=peer_of(step),
            device_id_type=pl.DeviceIdType.MESH,
        ).start()
        return carry

    lax.fori_loop(1, total, send, 0)
    every = pltpu.make_async_remote_copy(
        src_ref=buf.at[pl.ds(0, total - 1)],
        dst_ref=buf.at[pl.ds(0, total - 1)],
        send_sem=send_sem,
        recv_sem=recv_sem,
        device_id=peer_of(1),
        device_id_type=pl.DeviceIdType.MESH,
    )
    every.wait_send()
    every.wait_recv()

    def add(source, acc):
        return acc + buf[lax.rem(source - me - 1 + 2 * total, total)]

    o_ref[...] = lax.fori_loop(0, total, add, jnp.zeros(x_ref.shape, x_ref.dtype))


def gather_sum(x):
    n_calib = lax.axis_size("calib")
    n_peak = lax.axis_size("peak")
    return pl.pallas_call(
        lambda *refs: gather_sum_kernel(n_calib, n_peak, *refs),
        out_shape=jax.ShapeDtypeStruct(x.shape, x.dtype),
        in_specs=[pl.BlockSpec(memory_space=pltpu.VMEM)],
        out_specs=pl.BlockSpec(memory_space=pltpu.VMEM),
        scratch_shapes=[
            pltpu.VMEM((n_calib * n_peak,) + x.shape, x.dtype),
            pltpu.SemaphoreType.DMA,
            pltpu.SemaphoreType.DMA,
        ],
        compiler_params=pltpu.CompilerParams(collective_id=0, has_side_effects=True),
    )(x)


def cycle_stats(first, second, present_flag):
    cycle_average = first / present_flag[None, :]
    cycle_rms = jnp.sqrt(second / present_flag[None, :] + 1e-06)
    return (cycle_average, cycle_rms)


def body(raw, pedestal, gain, good, bounds, table):
    frame_dev, mods, row_dev, cols = raw.shape
    n_calib = lax.axis_size("calib")
    n_peak = lax.axis_size("peak")
    mrows = row_dev * n_calib
    slot_rows = mods // SLOT_C
    width_here = cols // n_peak
    frames_all = frame_dev * n_peak
    row_src = lax.axis_index("calib") * row_dev + jnp.arange(row_dev, dtype=jnp.int32)
    send = calibrate_send(raw, pedestal, gain, good, bounds, table, n_peak)
    send = send.reshape(mods * n_peak, frame_dev, row_dev, width_here)
    present_part = local_present(good, table, row_src, mrows, slot_rows)
    got = lax.all_to_all(send, ("calib", "peak"), 0, 0, tiled=True)
    got = got.reshape(n_calib, n_peak, frame_dev, row_dev, width_here)
    frame = jnp.transpose(got, (1, 2, 0, 3, 4)).reshape(frames_all, mrows, width_here)
    slot = lax.axis_index("calib")
    col_dst = lax.axis_index("peak") * width_here + jnp.arange(width_here, dtype=jnp.int32)
    ypos = slot // SLOT_C * mrows + jnp.arange(mrows, dtype=jnp.int32)
    xpos = slot % SLOT_C * COLS + col_dst
    dy_two = 2 * ypos + 1 - slot_rows * mrows
    dx_two = 2 * xpos + 1 - SLOT_C * COLS
    cycle = cycle_index(dy_two[:, None] * dy_two[:, None] + dx_two[None, :] * dx_two[None, :])
    levels = jnp.arange(CYCLES, dtype=jnp.int32)
    hits = (cycle.reshape(1, -1) == levels[:, None]).astype(jnp.bfloat16)
    pixels = frame.reshape(frames_all, -1)
    values = pixels.astype(jnp.float32)
    square = values * values
    square_top = lax.reduce_precision(square, exponent_bits=8, mantissa_bits=7)
    square_hi = square_top.astype(jnp.bfloat16)
    square_lo = (square - square_top).astype(jnp.bfloat16)
    stacked = jnp.concatenate([pixels, square_hi, square_lo], axis=0)
    sums = jnp.einsum("fp,kp->fk", stacked, hits, preferred_element_type=jnp.float32)
    first = sums[:frames_all]
    second = sums[frames_all : 2 * frames_all] + sums[2 * frames_all :]
    lanes = 128
    packed = jnp.concatenate(
        [
            first,
            second,
            jnp.zeros((frames_all, CYCLES), jnp.float32).at[0].set(present_part),
            jnp.zeros((frames_all, lanes - 3 * CYCLES), jnp.float32),
        ],
        axis=1,
    )
    summed = gather_sum(packed)
    first = summed[:, :CYCLES]
    second = summed[:, CYCLES : 2 * CYCLES]
    present_flag = summed[0, 2 * CYCLES : 3 * CYCLES]
    cycle_average, cycle_rms = cycle_stats(first, second, present_flag)
    edge_cycle = jnp.stack([cycle[:, width_here - 1], cycle[:, 0]], axis=1)
    edge_values = jnp.stack([frame[:, :, width_here - 1], frame[:, :, 0]], axis=2)
    edge_mean = jnp.take(cycle_average, edge_cycle, axis=1)
    edge_rms = jnp.take(cycle_rms, edge_cycle, axis=1)
    edge_score = (edge_values.astype(jnp.float32) - edge_mean) / edge_rms
    fwd = [(i, i + 1) for i in range(n_peak - 1)]
    bwd = [(i + 1, i) for i in range(n_peak - 1)]
    left = lax.ppermute(edge_score[:, :, :1], "peak", fwd)
    right = lax.ppermute(edge_score[:, :, 1:], "peak", bwd)
    snr, bent = score_outputs(frame, cycle, cycle_average, cycle_rms, left, right, n_peak)
    return (snr[:, None], bent[:, None])


def solution(mesh):
    in_specs = (
        P("peak", None, "calib", None),
        P(None, None, "calib", None),
        P(None, None, "calib", None),
        P(None, "calib", None),
        P(),
        P(),
    )
    out_specs = (P(None, "calib", None, "peak"), P(None, "calib", None, "peak"))
    return jax.shard_map(body, mesh=mesh, in_specs=in_specs, out_specs=out_specs, check_vma=False)
```

```python
import jax
import jax.numpy as jnp
from jax import lax
from jax.sharding import PartitionSpec as P
from jax.experimental import pallas as pl
from jax.experimental.pallas import tpu as pltpu

COLS = 1024
BANDS = 8
SLOT_C = 4
CYCLES = 32
CYCLE_W = 64


precise_variant = lax.Precision.HIGHEST


def padded_2(block, sides, width):
    for axis, dim in sides:
        count = lax.axis_size(axis)
        forward = [(i, i + 1) for i in range(count - 1)]
        backward = [(target, source) for source, target in forward]
        low = lax.ppermute(
            lax.slice_in_dim(block, block.shape[dim] - width, None, axis=dim), axis, forward
        )
        high = lax.ppermute(lax.slice_in_dim(block, 0, width, axis=dim), axis, backward)
        block = jnp.concatenate([low, block, high], axis=dim)
    return block


def cycle_index(dist):
    levels = jnp.arange(1, CYCLES, dtype=jnp.int32)
    lows = (2 * CYCLE_W * levels) ** 2
    return jnp.sum((dist[..., None] >= lows).astype(jnp.int32), axis=-1)


def cycle_onehot(slot, row_pos, col_pos, mrows, slot_rows):
    ypos = slot // SLOT_C * mrows + row_pos
    xpos = slot % SLOT_C * COLS + col_pos
    dy_two = 2 * ypos + 1 - slot_rows * mrows
    dx_two = 2 * xpos + 1 - SLOT_C * COLS
    dist = dy_two[:, None] * dy_two[:, None] + dx_two[None, :] * dx_two[None, :]
    levels = jnp.arange(CYCLES, dtype=jnp.int32)
    lows = (2 * CYCLE_W * levels) ** 2
    cycle = jnp.sum((dist[None] >= lows[:, None, None]).astype(jnp.int32), axis=0) - 1
    hits = (cycle[None] == levels[:, None, None]).astype(jnp.float32)
    return hits.reshape(CYCLES, -1)


def calibrate(raw, pedestal, gain, good, bounds):
    code = raw // 2048
    counts_adc = (raw % 2048).astype(jnp.float32)
    base = jnp.where(code == 0, pedestal[0], jnp.where(code == 1, pedestal[1], pedestal[2]))
    gain_factor = gain.astype(jnp.float32)
    scale = jnp.where(
        code == 0, gain_factor[0], jnp.where(code == 1, gain_factor[1], gain_factor[2])
    )
    weight_factor = good.astype(jnp.float32)
    energy = weight_factor * (counts_adc - base) / scale
    columns = jnp.arange(raw.shape[-1], dtype=jnp.int32)
    band = jnp.sum((columns[None, :, None] >= bounds[:, None, :]).astype(jnp.int32), axis=2)
    member_entry = (band[:, :, None] == jnp.arange(BANDS, dtype=jnp.int32)[None, None, :]).astype(
        jnp.float32
    )
    totals = jnp.einsum("fmrc,mcb->fmrb", energy, member_entry, precision=precise_variant)
    present_flag = jnp.einsum(
        "tlg,tgd->tld", weight_factor, member_entry, precision=precise_variant
    )
    level = totals / jnp.maximum(present_flag, 1.0)
    spread = jnp.einsum("fmrb,mcb->fmrc", level, member_entry, precision=precise_variant)
    return (weight_factor * (energy - spread)).astype(jnp.bfloat16)


def calibrate_kernel(group, table_ref, bounds_ref, raw_ref, ped_ref, gain_ref, good_ref, out_ref):
    step = pl.program_id(0)
    cols = raw_ref.shape[-1]
    columns = lax.broadcasted_iota(jnp.int32, (1, cols), 1)
    quarters = out_ref.shape[1]
    width = cols // quarters
    for inner in range(group):
        module = step * group + inner
        raw = raw_ref[:, inner]
        code = raw // 2048
        counts_adc = (raw % 2048).astype(jnp.float32)
        base = jnp.where(
            code == 0, ped_ref[0, inner], jnp.where(code == 1, ped_ref[1, inner], ped_ref[2, inner])
        )
        scale = jnp.where(
            code == 0,
            gain_ref[0, inner].astype(jnp.float32),
            jnp.where(
                code == 1,
                gain_ref[1, inner].astype(jnp.float32),
                gain_ref[2, inner].astype(jnp.float32),
            ),
        )
        weight_factor = good_ref[inner].astype(jnp.float32)
        energy = weight_factor * (counts_adc - base) / scale
        band = jnp.zeros((1, cols), jnp.int32)
        for j in range(BANDS - 1):
            band = band + (columns >= bounds_ref[module * (BANDS - 1) + j]).astype(jnp.int32)
        spread = jnp.zeros(energy.shape, jnp.float32)
        for b in range(BANDS):
            member = band == b
            totals = jnp.sum(jnp.where(member, energy, 0.0), axis=-1, keepdims=True)
            present = jnp.sum(jnp.where(member, weight_factor, 0.0), axis=-1, keepdims=True)
            spread = jnp.where(member, totals / jnp.maximum(present, 1.0), spread)
        corrected = (weight_factor * (energy - spread)).astype(jnp.bfloat16)
        slot = table_ref[module]
        for q in range(quarters):
            out_ref[slot, q] = corrected[:, :, q * width : (q + 1) * width]


def calibrate_send(raw, pedestal, gain, good, bounds, table, n_peak):
    frame_dev, mods, row_dev, cols = raw.shape
    width = cols // n_peak
    group = 8
    grid_spec = pltpu.PrefetchScalarGridSpec(
        num_scalar_prefetch=2,
        grid=(mods // group,),
        in_specs=[
            pl.BlockSpec((frame_dev, group, row_dev, cols), lambda m, t, b: (0, m, 0, 0)),
            pl.BlockSpec((3, group, row_dev, cols), lambda m, t, b: (0, m, 0, 0)),
            pl.BlockSpec((3, group, row_dev, cols), lambda m, t, b: (0, m, 0, 0)),
            pl.BlockSpec((group, row_dev, cols), lambda m, t, b: (m, 0, 0)),
        ],
        out_specs=pl.BlockSpec(
            (mods, n_peak, frame_dev, row_dev, width), lambda m, t, b: (0, 0, 0, 0, 0)
        ),
    )
    return pl.pallas_call(
        lambda *refs: calibrate_kernel(group, *refs),
        grid_spec=grid_spec,
        out_shape=jax.ShapeDtypeStruct((mods, n_peak, frame_dev, row_dev, width), jnp.bfloat16),
    )(table, bounds.reshape(-1), raw, pedestal, gain, good)


def score_kernel(n_peak, levels, low_ref, mean_ref, rms_ref, frame_ref, cycle_ref, left_ref, right_ref, snr_ref, bent_ref):
    frame_pos = pl.program_id(0)
    cycle = cycle_ref[...]
    values = frame_ref[...].astype(jnp.float32)
    rows, cols = values.shape
    tops = mean_ref.shape[1] - 1
    pixel_mean = jnp.zeros((rows, cols), jnp.float32)
    pixel_rms = jnp.ones((rows, cols), jnp.float32)
    for j in range(levels):
        level = jnp.minimum(low_ref[0] + j, tops)
        hit = cycle == level
        pixel_mean = jnp.where(hit, mean_ref[frame_pos, level], pixel_mean)
        pixel_rms = jnp.where(hit, rms_ref[frame_pos, level], pixel_rms)
    score = (values - pixel_mean) / pixel_rms
    peak_pos = lax.axis_index("peak")
    row_ids = lax.broadcasted_iota(jnp.int32, (rows, cols), 0)
    col_ids = lax.broadcasted_iota(jnp.int32, (rows, cols), 1)
    left_col = jnp.where(peak_pos == 0, 0.0, left_ref[...])
    right_col = jnp.where(peak_pos == n_peak - 1, 0.0, right_ref[...])
    total = 4.0 * score
    for shift in (1, rows - 1):
        moved = pltpu.roll(score, shift, 0)
        source = pltpu.roll(row_ids, shift, 0)
        total = total - jnp.where(jnp.abs(source - row_ids) == 1, moved, 0.0)
    for shift in (1, cols - 1):
        moved = pltpu.roll(score, shift, 1)
        source = pltpu.roll(col_ids, shift, 1)
        near = jnp.where(source == cols - 1, left_col, right_col)
        total = total - jnp.where(jnp.abs(source - col_ids) == 1, moved, near)
    snr_ref[...] = score.astype(snr_ref.dtype)
    bent_ref[...] = total.astype(bent_ref.dtype)


def score_outputs(frame, cycle, cycle_average, cycle_rms, left, right, n_peak):
    frames, rows, cols = frame.shape
    span = (rows * rows + cols * cols) ** 0.5
    levels = min(CYCLES, int(span // CYCLE_W) + 3)
    low = jnp.min(cycle).reshape(1)
    block = pl.BlockSpec((None, rows, cols), lambda f, *_: (f, 0, 0))
    edge = pl.BlockSpec((None, rows, 1), lambda f, *_: (f, 0, 0))
    grid_spec = pltpu.PrefetchScalarGridSpec(
        num_scalar_prefetch=3,
        grid=(frames,),
        in_specs=[block, pl.BlockSpec((rows, cols), lambda f, *_: (0, 0)), edge, edge],
        out_specs=[block, block],
    )
    return pl.pallas_call(
        lambda *refs: score_kernel(n_peak, levels, *refs),
        grid_spec=grid_spec,
        out_shape=[jax.ShapeDtypeStruct(frame.shape, jnp.bfloat16)] * 2,
    )(low, cycle_average, cycle_rms, frame, cycle, left, right)


def laplace(padded):
    center = padded[..., 1:-1, 1:-1]
    return (
        4.0 * center
        - padded[..., :-2, 1:-1]
        - padded[..., 2:, 1:-1]
        - padded[..., 1:-1, :-2]
        - padded[..., 1:-1, 2:]
    )


def local_present(good, table, row_src, mrows, slot_rows):
    n_peak = lax.axis_size("peak")
    width = good.shape[2] // n_peak
    start = lax.axis_index("peak") * width
    part = lax.dynamic_slice_in_dim(good, start, width, axis=2)
    col = start + jnp.arange(width, dtype=jnp.int32)
    ypos = (table // SLOT_C)[:, None] * mrows + row_src[None, :]
    xpos = (table % SLOT_C)[:, None] * COLS + col[None, :]
    dy_two = 2 * ypos + 1 - slot_rows * mrows
    dx_two = 2 * xpos + 1 - SLOT_C * COLS
    dist = dy_two[:, :, None] * dy_two[:, :, None] + dx_two[:, None, :] * dx_two[:, None, :]
    cycle = cycle_index(dist)
    levels = jnp.arange(CYCLES, dtype=jnp.int32)
    hit = jnp.where(cycle[..., None] == levels, part[..., None], 0)
    return jnp.sum(hit, axis=(0, 1, 2)).astype(jnp.float32)


def gather_sum_kernel(n_calib, n_peak, x_ref, o_ref, buf, send_sem, recv_sem):
    total = n_calib * n_peak
    me = lax.axis_index("calib") * n_peak + lax.axis_index("peak")
    buf[total - 1] = x_ref[...]
    barrier = pltpu.get_barrier_semaphore()

    def peer_of(step):
        peer = lax.rem(me + step, total)
        return (peer // n_peak, peer % n_peak)

    def greet(step, carry):
        pl.semaphore_signal(
            barrier, inc=1, device_id=peer_of(step), device_id_type=pl.DeviceIdType.MESH
        )
        return carry

    lax.fori_loop(1, total, greet, 0)
    pl.semaphore_wait(barrier, total - 1)

    def send(step, carry):
        pltpu.make_async_remote_copy(
            src_ref=x_ref,
            dst_ref=buf.at[total - 1 - step],
            send_sem=send_sem,
            recv_sem=recv_sem,
            device_id=peer_of(step),
            device_id_type=pl.DeviceIdType.MESH,
        ).start()
        return carry

    lax.fori_loop(1, total, send, 0)
    every = pltpu.make_async_remote_copy(
        src_ref=buf.at[pl.ds(0, total - 1)],
        dst_ref=buf.at[pl.ds(0, total - 1)],
        send_sem=send_sem,
        recv_sem=recv_sem,
        device_id=peer_of(1),
        device_id_type=pl.DeviceIdType.MESH,
    )
    every.wait_send()
    every.wait_recv()

    def add(source, acc):
        return acc + buf[lax.rem(source - me - 1 + 2 * total, total)]

    o_ref[...] = lax.fori_loop(0, total, add, jnp.zeros(x_ref.shape, x_ref.dtype))


def gather_sum(x):
    n_calib = lax.axis_size("calib")
    n_peak = lax.axis_size("peak")
    return pl.pallas_call(
        lambda *refs: gather_sum_kernel(n_calib, n_peak, *refs),
        out_shape=jax.ShapeDtypeStruct(x.shape, x.dtype),
        in_specs=[pl.BlockSpec(memory_space=pltpu.VMEM)],
        out_specs=pl.BlockSpec(memory_space=pltpu.VMEM),
        scratch_shapes=[
            pltpu.VMEM((n_calib * n_peak,) + x.shape, x.dtype),
            pltpu.SemaphoreType.DMA,
            pltpu.SemaphoreType.DMA,
        ],
        compiler_params=pltpu.CompilerParams(collective_id=0, has_side_effects=True),
    )(x)


def cycle_stats(first, second, present_flag):
    cycle_average = first / present_flag[None, :]
    cycle_rms = jnp.sqrt(second / present_flag[None, :] + 1e-06)
    return (cycle_average, cycle_rms)


def body(raw, pedestal, gain, good, bounds, table):
    frame_dev, mods, row_dev, cols = raw.shape
    n_calib = lax.axis_size("calib")
    n_peak = lax.axis_size("peak")
    mrows = row_dev * n_calib
    slot_rows = mods // SLOT_C
    width_here = cols // n_peak
    frames_all = frame_dev * n_peak
    row_src = lax.axis_index("calib") * row_dev + jnp.arange(row_dev, dtype=jnp.int32)
    send = calibrate_send(raw, pedestal, gain, good, bounds, table, n_peak)
    send = send.reshape(mods * n_peak, frame_dev, row_dev, width_here)
    present_part = local_present(good, table, row_src, mrows, slot_rows)
    got = lax.all_to_all(send, ("calib", "peak"), 0, 0, tiled=True)
    got = got.reshape(n_calib, n_peak, frame_dev, row_dev, width_here)
    frame = jnp.transpose(got, (1, 2, 0, 3, 4)).reshape(frames_all, mrows, width_here)
    slot = lax.axis_index("calib")
    col_dst = lax.axis_index("peak") * width_here + jnp.arange(width_here, dtype=jnp.int32)
    ypos = slot // SLOT_C * mrows + jnp.arange(mrows, dtype=jnp.int32)
    xpos = slot % SLOT_C * COLS + col_dst
    dy_two = 2 * ypos + 1 - slot_rows * mrows
    dx_two = 2 * xpos + 1 - SLOT_C * COLS
    cycle = cycle_index(dy_two[:, None] * dy_two[:, None] + dx_two[None, :] * dx_two[None, :])
    levels = jnp.arange(CYCLES, dtype=jnp.int32)
    hits = (cycle.reshape(1, -1) == levels[:, None]).astype(jnp.bfloat16)
    pixels = frame.reshape(frames_all, -1)
    values = pixels.astype(jnp.float32)
    square = values * values
    square_top = lax.reduce_precision(square, exponent_bits=8, mantissa_bits=7)
    square_hi = square_top.astype(jnp.bfloat16)
    square_lo = (square - square_top).astype(jnp.bfloat16)
    stacked = jnp.concatenate([pixels, square_hi, square_lo], axis=0)
    sums = jnp.einsum("fp,kp->fk", stacked, hits, preferred_element_type=jnp.float32)
    first = sums[:frames_all]
    second = sums[frames_all : 2 * frames_all] + sums[2 * frames_all :]
    lanes = 128
    packed = jnp.concatenate(
        [
            first,
            second,
            jnp.zeros((frames_all, CYCLES), jnp.float32).at[0].set(present_part),
            jnp.zeros((frames_all, lanes - 3 * CYCLES), jnp.float32),
        ],
        axis=1,
    )
    summed = gather_sum(packed)
    first = summed[:, :CYCLES]
    second = summed[:, CYCLES : 2 * CYCLES]
    present_flag = summed[0, 2 * CYCLES : 3 * CYCLES]
    cycle_average, cycle_rms = cycle_stats(first, second, present_flag)
    edge_cycle = jnp.stack([cycle[:, width_here - 1], cycle[:, 0]], axis=1)
    edge_values = jnp.stack([frame[:, :, width_here - 1], frame[:, :, 0]], axis=2)
    edge_hits = (edge_cycle.reshape(1, -1) == levels[:, None]).astype(jnp.float32)
    edge_table = jnp.einsum(
        "fk,kp->fp",
        jnp.concatenate([cycle_average, cycle_rms], axis=0),
        edge_hits,
        precision=precise_variant,
    ).reshape(2 * frames_all, mrows, 2)
    edge_mean = edge_table[:frames_all]
    edge_rms = edge_table[frames_all:]
    edge_score = (edge_values.astype(jnp.float32) - edge_mean) / edge_rms
    fwd = [(i, i + 1) for i in range(n_peak - 1)]
    bwd = [(i + 1, i) for i in range(n_peak - 1)]
    left = lax.ppermute(edge_score[:, :, :1], "peak", fwd)
    right = lax.ppermute(edge_score[:, :, 1:], "peak", bwd)
    snr, bent = score_outputs(frame, cycle, cycle_average, cycle_rms, left, right, n_peak)
    return (snr[:, None], bent[:, None])


def solution(mesh):
    in_specs = (
        P("peak", None, "calib", None),
        P(None, None, "calib", None),
        P(None, None, "calib", None),
        P(None, "calib", None),
        P(),
        P(),
    )
    out_specs = (P(None, "calib", None, "peak"), P(None, "calib", None, "peak"))
    return jax.shard_map(body, mesh=mesh, in_specs=in_specs, out_specs=out_specs, check_vma=False)
```

```python
import jax
import jax.numpy as jnp
from jax import lax
from jax.sharding import PartitionSpec as P
from jax.experimental import pallas as pl
from jax.experimental.pallas import tpu as pltpu

COLS = 1024
BANDS = 8
SLOT_C = 4
CYCLES = 32
CYCLE_W = 64


precise_variant = lax.Precision.HIGHEST


def padded_2(block, sides, width):
    for axis, dim in sides:
        count = lax.axis_size(axis)
        forward = [(i, i + 1) for i in range(count - 1)]
        backward = [(target, source) for source, target in forward]
        low = lax.ppermute(
            lax.slice_in_dim(block, block.shape[dim] - width, None, axis=dim), axis, forward
        )
        high = lax.ppermute(lax.slice_in_dim(block, 0, width, axis=dim), axis, backward)
        block = jnp.concatenate([low, block, high], axis=dim)
    return block


def cycle_index(dist):
    levels = jnp.arange(1, CYCLES, dtype=jnp.int32)
    lows = (2 * CYCLE_W * levels) ** 2
    return jnp.sum((dist[..., None] >= lows).astype(jnp.int32), axis=-1)


def cycle_onehot(slot, row_pos, col_pos, mrows, slot_rows):
    ypos = slot // SLOT_C * mrows + row_pos
    xpos = slot % SLOT_C * COLS + col_pos
    dy_two = 2 * ypos + 1 - slot_rows * mrows
    dx_two = 2 * xpos + 1 - SLOT_C * COLS
    dist = dy_two[:, None] * dy_two[:, None] + dx_two[None, :] * dx_two[None, :]
    levels = jnp.arange(CYCLES, dtype=jnp.int32)
    lows = (2 * CYCLE_W * levels) ** 2
    cycle = jnp.sum((dist[None] >= lows[:, None, None]).astype(jnp.int32), axis=0) - 1
    hits = (cycle[None] == levels[:, None, None]).astype(jnp.float32)
    return hits.reshape(CYCLES, -1)


def calibrate(raw, pedestal, gain, good, bounds):
    code = raw // 2048
    counts_adc = (raw % 2048).astype(jnp.float32)
    base = jnp.where(code == 0, pedestal[0], jnp.where(code == 1, pedestal[1], pedestal[2]))
    gain_factor = gain.astype(jnp.float32)
    scale = jnp.where(
        code == 0, gain_factor[0], jnp.where(code == 1, gain_factor[1], gain_factor[2])
    )
    weight_factor = good.astype(jnp.float32)
    energy = weight_factor * (counts_adc - base) / scale
    columns = jnp.arange(raw.shape[-1], dtype=jnp.int32)
    band = jnp.sum((columns[None, :, None] >= bounds[:, None, :]).astype(jnp.int32), axis=2)
    member_entry = (band[:, :, None] == jnp.arange(BANDS, dtype=jnp.int32)[None, None, :]).astype(
        jnp.float32
    )
    totals = jnp.einsum("fmrc,mcb->fmrb", energy, member_entry, precision=precise_variant)
    present_flag = jnp.einsum(
        "tlg,tgd->tld", weight_factor, member_entry, precision=precise_variant
    )
    level = totals / jnp.maximum(present_flag, 1.0)
    spread = jnp.einsum("fmrb,mcb->fmrc", level, member_entry, precision=precise_variant)
    return (weight_factor * (energy - spread)).astype(jnp.bfloat16)


def calibrate_kernel(group, table_ref, bounds_ref, raw_ref, ped_ref, gain_ref, good_ref, out_ref):
    step = pl.program_id(0)
    cols = raw_ref.shape[-1]
    columns = lax.broadcasted_iota(jnp.int32, (1, cols), 1)
    quarters = out_ref.shape[1]
    width = cols // quarters
    for inner in range(group):
        module = step * group + inner
        raw = raw_ref[:, inner]
        code = raw // 2048
        counts_adc = (raw % 2048).astype(jnp.float32)
        base = jnp.where(
            code == 0, ped_ref[0, inner], jnp.where(code == 1, ped_ref[1, inner], ped_ref[2, inner])
        )
        scale = jnp.where(
            code == 0,
            gain_ref[0, inner].astype(jnp.float32),
            jnp.where(
                code == 1,
                gain_ref[1, inner].astype(jnp.float32),
                gain_ref[2, inner].astype(jnp.float32),
            ),
        )
        weight_factor = good_ref[inner].astype(jnp.float32)
        energy = weight_factor * (counts_adc - base) / scale
        band = jnp.zeros((1, cols), jnp.int32)
        for j in range(BANDS - 1):
            band = band + (columns >= bounds_ref[module * (BANDS - 1) + j]).astype(jnp.int32)
        spread = jnp.zeros(energy.shape, jnp.float32)
        for b in range(BANDS):
            member = band == b
            totals = jnp.sum(jnp.where(member, energy, 0.0), axis=-1, keepdims=True)
            present = jnp.sum(jnp.where(member, weight_factor, 0.0), axis=-1, keepdims=True)
            spread = jnp.where(member, totals / jnp.maximum(present, 1.0), spread)
        corrected = (weight_factor * (energy - spread)).astype(jnp.bfloat16)
        slot = table_ref[module]
        for q in range(quarters):
            out_ref[slot, q] = corrected[:, :, q * width : (q + 1) * width]


def calibrate_send(raw, pedestal, gain, good, bounds, table, n_peak):
    frame_dev, mods, row_dev, cols = raw.shape
    width = cols // n_peak
    group = 8
    grid_spec = pltpu.PrefetchScalarGridSpec(
        num_scalar_prefetch=2,
        grid=(mods // group,),
        in_specs=[
            pl.BlockSpec((frame_dev, group, row_dev, cols), lambda m, t, b: (0, m, 0, 0)),
            pl.BlockSpec((3, group, row_dev, cols), lambda m, t, b: (0, m, 0, 0)),
            pl.BlockSpec((3, group, row_dev, cols), lambda m, t, b: (0, m, 0, 0)),
            pl.BlockSpec((group, row_dev, cols), lambda m, t, b: (m, 0, 0)),
        ],
        out_specs=pl.BlockSpec(
            (mods, n_peak, frame_dev, row_dev, width), lambda m, t, b: (0, 0, 0, 0, 0)
        ),
    )
    return pl.pallas_call(
        lambda *refs: calibrate_kernel(group, *refs),
        grid_spec=grid_spec,
        out_shape=jax.ShapeDtypeStruct((mods, n_peak, frame_dev, row_dev, width), jnp.bfloat16),
    )(table, bounds.reshape(-1), raw, pedestal, gain, good)


def score_kernel(n_peak, levels, low_ref, mean_ref, rms_ref, frame_ref, cycle_ref, left_ref, right_ref, snr_ref, bent_ref):
    frame_pos = pl.program_id(0)
    cycle = cycle_ref[...]
    values = frame_ref[...].astype(jnp.float32)
    rows, cols = values.shape
    tops = mean_ref.shape[1] - 1
    pixel_mean = jnp.zeros((rows, cols), jnp.float32)
    pixel_rms = jnp.ones((rows, cols), jnp.float32)
    for j in range(levels):
        level = jnp.minimum(low_ref[0] + j, tops)
        hit = cycle == level
        pixel_mean = jnp.where(hit, mean_ref[frame_pos, level], pixel_mean)
        pixel_rms = jnp.where(hit, rms_ref[frame_pos, level], pixel_rms)
    score = (values - pixel_mean) / pixel_rms
    peak_pos = lax.axis_index("peak")
    row_ids = lax.broadcasted_iota(jnp.int32, (rows, cols), 0)
    col_ids = lax.broadcasted_iota(jnp.int32, (rows, cols), 1)
    left_col = jnp.where(peak_pos == 0, 0.0, left_ref[...])
    right_col = jnp.where(peak_pos == n_peak - 1, 0.0, right_ref[...])
    total = 4.0 * score
    for shift in (1, rows - 1):
        moved = pltpu.roll(score, shift, 0)
        source = pltpu.roll(row_ids, shift, 0)
        total = total - jnp.where(jnp.abs(source - row_ids) == 1, moved, 0.0)
    for shift in (1, cols - 1):
        moved = pltpu.roll(score, shift, 1)
        source = pltpu.roll(col_ids, shift, 1)
        near = jnp.where(source == cols - 1, left_col, right_col)
        total = total - jnp.where(jnp.abs(source - col_ids) == 1, moved, near)
    snr_ref[...] = score.astype(snr_ref.dtype)
    bent_ref[...] = total.astype(bent_ref.dtype)


def score_outputs(frame, cycle, cycle_average, cycle_rms, left, right, n_peak):
    frames, rows, cols = frame.shape
    span = (rows * rows + cols * cols) ** 0.5
    levels = min(CYCLES, int(span // CYCLE_W) + 3)
    low = jnp.min(cycle).reshape(1)
    block = pl.BlockSpec((None, rows, cols), lambda f, *_: (f, 0, 0))
    edge = pl.BlockSpec((None, rows, 1), lambda f, *_: (f, 0, 0))
    grid_spec = pltpu.PrefetchScalarGridSpec(
        num_scalar_prefetch=3,
        grid=(frames,),
        in_specs=[block, pl.BlockSpec((rows, cols), lambda f, *_: (0, 0)), edge, edge],
        out_specs=[block, block],
    )
    return pl.pallas_call(
        lambda *refs: score_kernel(n_peak, levels, *refs),
        grid_spec=grid_spec,
        out_shape=[jax.ShapeDtypeStruct(frame.shape, jnp.bfloat16)] * 2,
    )(low, cycle_average, cycle_rms, frame, cycle, left, right)


def laplace(padded):
    center = padded[..., 1:-1, 1:-1]
    return (
        4.0 * center
        - padded[..., :-2, 1:-1]
        - padded[..., 2:, 1:-1]
        - padded[..., 1:-1, :-2]
        - padded[..., 1:-1, 2:]
    )


def local_present(good, table, row_src, mrows, slot_rows):
    n_peak = lax.axis_size("peak")
    width = good.shape[2] // n_peak
    start = lax.axis_index("peak") * width
    part = lax.dynamic_slice_in_dim(good, start, width, axis=2)
    col = start + jnp.arange(width, dtype=jnp.int32)
    ypos = (table // SLOT_C)[:, None] * mrows + row_src[None, :]
    xpos = (table % SLOT_C)[:, None] * COLS + col[None, :]
    dy_two = 2 * ypos + 1 - slot_rows * mrows
    dx_two = 2 * xpos + 1 - SLOT_C * COLS
    dist = dy_two[:, :, None] * dy_two[:, :, None] + dx_two[:, None, :] * dx_two[:, None, :]
    cycle = cycle_index(dist)
    levels = jnp.arange(CYCLES, dtype=jnp.int32)
    hit = jnp.where(cycle[..., None] == levels, part[..., None], 0)
    return jnp.sum(hit, axis=(0, 1, 2)).astype(jnp.float32)


def gather_sum_kernel(
    n_calib, n_peak, x_ref, o_ref, near, far, partial, near_send, near_recv, far_send, far_recv
):
    my_calib = lax.axis_index("calib")
    my_peak = lax.axis_index("peak")
    near[n_peak - 1] = x_ref[...]
    barrier = pltpu.get_barrier_semaphore()

    def peak_peer(step):
        return (my_calib, lax.rem(my_peak + step, n_peak))

    def calib_peer(step):
        return (lax.rem(my_calib + step, n_calib), my_peak)

    def greet_peak(step, carry):
        pl.semaphore_signal(
            barrier, inc=1, device_id=peak_peer(step), device_id_type=pl.DeviceIdType.MESH
        )
        return carry

    def greet_calib(step, carry):
        pl.semaphore_signal(
            barrier, inc=1, device_id=calib_peer(step), device_id_type=pl.DeviceIdType.MESH
        )
        return carry

    lax.fori_loop(1, n_peak, greet_peak, 0)
    lax.fori_loop(1, n_calib, greet_calib, 0)
    pl.semaphore_wait(barrier, n_peak - 1 + n_calib - 1)

    def send_near(step, carry):
        pltpu.make_async_remote_copy(
            src_ref=x_ref,
            dst_ref=near.at[n_peak - 1 - step],
            send_sem=near_send,
            recv_sem=near_recv,
            device_id=peak_peer(step),
            device_id_type=pl.DeviceIdType.MESH,
        ).start()
        return carry

    lax.fori_loop(1, n_peak, send_near, 0)
    every_near = pltpu.make_async_remote_copy(
        src_ref=near.at[pl.ds(0, n_peak - 1)],
        dst_ref=near.at[pl.ds(0, n_peak - 1)],
        send_sem=near_send,
        recv_sem=near_recv,
        device_id=peak_peer(1),
        device_id_type=pl.DeviceIdType.MESH,
    )
    every_near.wait_send()
    every_near.wait_recv()

    def add_near(source, acc):
        return acc + near[lax.rem(source - my_peak - 1 + 2 * n_peak, n_peak)]

    partial[...] = lax.fori_loop(0, n_peak, add_near, jnp.zeros(x_ref.shape, x_ref.dtype))
    far[n_calib - 1] = partial[...]

    def send_far(step, carry):
        pltpu.make_async_remote_copy(
            src_ref=partial,
            dst_ref=far.at[n_calib - 1 - step],
            send_sem=far_send,
            recv_sem=far_recv,
            device_id=calib_peer(step),
            device_id_type=pl.DeviceIdType.MESH,
        ).start()
        return carry

    lax.fori_loop(1, n_calib, send_far, 0)
    every_far = pltpu.make_async_remote_copy(
        src_ref=far.at[pl.ds(0, n_calib - 1)],
        dst_ref=far.at[pl.ds(0, n_calib - 1)],
        send_sem=far_send,
        recv_sem=far_recv,
        device_id=calib_peer(1),
        device_id_type=pl.DeviceIdType.MESH,
    )
    every_far.wait_send()
    every_far.wait_recv()

    def add_far(source, acc):
        return acc + far[lax.rem(source - my_calib - 1 + 2 * n_calib, n_calib)]

    o_ref[...] = lax.fori_loop(0, n_calib, add_far, jnp.zeros(x_ref.shape, x_ref.dtype))


def gather_sum(x):
    n_calib = lax.axis_size("calib")
    n_peak = lax.axis_size("peak")
    return pl.pallas_call(
        lambda *refs: gather_sum_kernel(n_calib, n_peak, *refs),
        out_shape=jax.ShapeDtypeStruct(x.shape, x.dtype),
        in_specs=[pl.BlockSpec(memory_space=pltpu.VMEM)],
        out_specs=pl.BlockSpec(memory_space=pltpu.VMEM),
        scratch_shapes=[
            pltpu.VMEM((n_peak,) + x.shape, x.dtype),
            pltpu.VMEM((n_calib,) + x.shape, x.dtype),
            pltpu.VMEM(x.shape, x.dtype),
            pltpu.SemaphoreType.DMA,
            pltpu.SemaphoreType.DMA,
            pltpu.SemaphoreType.DMA,
            pltpu.SemaphoreType.DMA,
        ],
        compiler_params=pltpu.CompilerParams(collective_id=0, has_side_effects=True),
    )(x)


def cycle_stats(first, second, present_flag):
    cycle_average = first / present_flag[None, :]
    cycle_rms = jnp.sqrt(second / present_flag[None, :] + 1e-06)
    return (cycle_average, cycle_rms)


def body(raw, pedestal, gain, good, bounds, table):
    frame_dev, mods, row_dev, cols = raw.shape
    n_calib = lax.axis_size("calib")
    n_peak = lax.axis_size("peak")
    mrows = row_dev * n_calib
    slot_rows = mods // SLOT_C
    width_here = cols // n_peak
    frames_all = frame_dev * n_peak
    row_src = lax.axis_index("calib") * row_dev + jnp.arange(row_dev, dtype=jnp.int32)
    send = calibrate_send(raw, pedestal, gain, good, bounds, table, n_peak)
    send = send.reshape(mods * n_peak, frame_dev, row_dev, width_here)
    present_part = local_present(good, table, row_src, mrows, slot_rows)
    got = lax.all_to_all(send, ("calib", "peak"), 0, 0, tiled=True)
    got = got.reshape(n_calib, n_peak, frame_dev, row_dev, width_here)
    frame = jnp.transpose(got, (1, 2, 0, 3, 4)).reshape(frames_all, mrows, width_here)
    slot = lax.axis_index("calib")
    col_dst = lax.axis_index("peak") * width_here + jnp.arange(width_here, dtype=jnp.int32)
    ypos = slot // SLOT_C * mrows + jnp.arange(mrows, dtype=jnp.int32)
    xpos = slot % SLOT_C * COLS + col_dst
    dy_two = 2 * ypos + 1 - slot_rows * mrows
    dx_two = 2 * xpos + 1 - SLOT_C * COLS
    cycle = cycle_index(dy_two[:, None] * dy_two[:, None] + dx_two[None, :] * dx_two[None, :])
    levels = jnp.arange(CYCLES, dtype=jnp.int32)
    hits = (cycle.reshape(1, -1) == levels[:, None]).astype(jnp.bfloat16)
    pixels = frame.reshape(frames_all, -1)
    values = pixels.astype(jnp.float32)
    square = values * values
    square_top = lax.reduce_precision(square, exponent_bits=8, mantissa_bits=7)
    square_hi = square_top.astype(jnp.bfloat16)
    square_lo = (square - square_top).astype(jnp.bfloat16)
    stacked = jnp.concatenate([pixels, square_hi, square_lo], axis=0)
    sums = jnp.einsum("fp,kp->fk", stacked, hits, preferred_element_type=jnp.float32)
    first = sums[:frames_all]
    second = sums[frames_all : 2 * frames_all] + sums[2 * frames_all :]
    lanes = 128
    packed = jnp.concatenate(
        [
            first,
            second,
            jnp.zeros((frames_all, CYCLES), jnp.float32).at[0].set(present_part),
            jnp.zeros((frames_all, lanes - 3 * CYCLES), jnp.float32),
        ],
        axis=1,
    )
    summed = gather_sum(packed)
    first = summed[:, :CYCLES]
    second = summed[:, CYCLES : 2 * CYCLES]
    present_flag = summed[0, 2 * CYCLES : 3 * CYCLES]
    cycle_average, cycle_rms = cycle_stats(first, second, present_flag)
    edge_cycle = jnp.stack([cycle[:, width_here - 1], cycle[:, 0]], axis=1)
    edge_values = jnp.stack([frame[:, :, width_here - 1], frame[:, :, 0]], axis=2)
    edge_hits = (edge_cycle.reshape(1, -1) == levels[:, None]).astype(jnp.float32)
    edge_table = jnp.einsum(
        "fk,kp->fp",
        jnp.concatenate([cycle_average, cycle_rms], axis=0),
        edge_hits,
        precision=precise_variant,
    ).reshape(2 * frames_all, mrows, 2)
    edge_mean = edge_table[:frames_all]
    edge_rms = edge_table[frames_all:]
    edge_score = (edge_values.astype(jnp.float32) - edge_mean) / edge_rms
    fwd = [(i, i + 1) for i in range(n_peak - 1)]
    bwd = [(i + 1, i) for i in range(n_peak - 1)]
    left = lax.ppermute(edge_score[:, :, :1], "peak", fwd)
    right = lax.ppermute(edge_score[:, :, 1:], "peak", bwd)
    snr, bent = score_outputs(frame, cycle, cycle_average, cycle_rms, left, right, n_peak)
    return (snr[:, None], bent[:, None])


def solution(mesh):
    in_specs = (
        P("peak", None, "calib", None),
        P(None, None, "calib", None),
        P(None, None, "calib", None),
        P(None, "calib", None),
        P(),
        P(),
    )
    out_specs = (P(None, "calib", None, "peak"), P(None, "calib", None, "peak"))
    return jax.shard_map(body, mesh=mesh, in_specs=in_specs, out_specs=out_specs, check_vma=False)
```

```python
import jax
import jax.numpy as jnp
from jax import lax
from jax.sharding import PartitionSpec as P
from jax.experimental import pallas as pl
from jax.experimental.pallas import tpu as pltpu

COLS = 1024
BANDS = 8
SLOT_C = 4
CYCLES = 32
CYCLE_W = 64


precise_variant = lax.Precision.HIGHEST


def padded_2(block, sides, width):
    for axis, dim in sides:
        count = lax.axis_size(axis)
        forward = [(i, i + 1) for i in range(count - 1)]
        backward = [(target, source) for source, target in forward]
        low = lax.ppermute(
            lax.slice_in_dim(block, block.shape[dim] - width, None, axis=dim), axis, forward
        )
        high = lax.ppermute(lax.slice_in_dim(block, 0, width, axis=dim), axis, backward)
        block = jnp.concatenate([low, block, high], axis=dim)
    return block


def cycle_index(dist):
    levels = jnp.arange(1, CYCLES, dtype=jnp.int32)
    lows = (2 * CYCLE_W * levels) ** 2
    return jnp.sum((dist[..., None] >= lows).astype(jnp.int32), axis=-1)


def cycle_onehot(slot, row_pos, col_pos, mrows, slot_rows):
    ypos = slot // SLOT_C * mrows + row_pos
    xpos = slot % SLOT_C * COLS + col_pos
    dy_two = 2 * ypos + 1 - slot_rows * mrows
    dx_two = 2 * xpos + 1 - SLOT_C * COLS
    dist = dy_two[:, None] * dy_two[:, None] + dx_two[None, :] * dx_two[None, :]
    levels = jnp.arange(CYCLES, dtype=jnp.int32)
    lows = (2 * CYCLE_W * levels) ** 2
    cycle = jnp.sum((dist[None] >= lows[:, None, None]).astype(jnp.int32), axis=0) - 1
    hits = (cycle[None] == levels[:, None, None]).astype(jnp.float32)
    return hits.reshape(CYCLES, -1)


def calibrate(raw, pedestal, gain, good, bounds):
    code = raw // 2048
    counts_adc = (raw % 2048).astype(jnp.float32)
    base = jnp.where(code == 0, pedestal[0], jnp.where(code == 1, pedestal[1], pedestal[2]))
    gain_factor = gain.astype(jnp.float32)
    scale = jnp.where(
        code == 0, gain_factor[0], jnp.where(code == 1, gain_factor[1], gain_factor[2])
    )
    weight_factor = good.astype(jnp.float32)
    energy = weight_factor * (counts_adc - base) / scale
    columns = jnp.arange(raw.shape[-1], dtype=jnp.int32)
    band = jnp.sum((columns[None, :, None] >= bounds[:, None, :]).astype(jnp.int32), axis=2)
    member_entry = (band[:, :, None] == jnp.arange(BANDS, dtype=jnp.int32)[None, None, :]).astype(
        jnp.float32
    )
    totals = jnp.einsum("fmrc,mcb->fmrb", energy, member_entry, precision=precise_variant)
    present_flag = jnp.einsum(
        "tlg,tgd->tld", weight_factor, member_entry, precision=precise_variant
    )
    level = totals / jnp.maximum(present_flag, 1.0)
    spread = jnp.einsum("fmrb,mcb->fmrc", level, member_entry, precision=precise_variant)
    return (weight_factor * (energy - spread)).astype(jnp.bfloat16)


def calibrate_kernel(group, table_ref, bounds_ref, raw_ref, ped_ref, gain_ref, good_ref, out_ref):
    step = pl.program_id(0)
    cols = raw_ref.shape[-1]
    columns = lax.broadcasted_iota(jnp.int32, (1, cols), 1)
    quarters = out_ref.shape[1]
    width = cols // quarters
    for inner in range(group):
        module = step * group + inner
        raw = raw_ref[:, inner]
        code = raw // 2048
        counts_adc = (raw % 2048).astype(jnp.float32)
        base = jnp.where(
            code == 0, ped_ref[0, inner], jnp.where(code == 1, ped_ref[1, inner], ped_ref[2, inner])
        )
        scale = jnp.where(
            code == 0,
            gain_ref[0, inner].astype(jnp.float32),
            jnp.where(
                code == 1,
                gain_ref[1, inner].astype(jnp.float32),
                gain_ref[2, inner].astype(jnp.float32),
            ),
        )
        weight_factor = good_ref[inner].astype(jnp.float32)
        energy = weight_factor * (counts_adc - base) / scale
        band = jnp.zeros((1, cols), jnp.int32)
        for j in range(BANDS - 1):
            band = band + (columns >= bounds_ref[module * (BANDS - 1) + j]).astype(jnp.int32)
        spread = jnp.zeros(energy.shape, jnp.float32)
        for b in range(BANDS):
            member = band == b
            totals = jnp.sum(jnp.where(member, energy, 0.0), axis=-1, keepdims=True)
            present = jnp.sum(jnp.where(member, weight_factor, 0.0), axis=-1, keepdims=True)
            spread = jnp.where(member, totals / jnp.maximum(present, 1.0), spread)
        corrected = (weight_factor * (energy - spread)).astype(jnp.bfloat16)
        slot = table_ref[module]
        for q in range(quarters):
            out_ref[slot, q] = corrected[:, :, q * width : (q + 1) * width]


def calibrate_send(raw, pedestal, gain, good, bounds, table, n_peak):
    frame_dev, mods, row_dev, cols = raw.shape
    width = cols // n_peak
    group = 8
    grid_spec = pltpu.PrefetchScalarGridSpec(
        num_scalar_prefetch=2,
        grid=(mods // group,),
        in_specs=[
            pl.BlockSpec((frame_dev, group, row_dev, cols), lambda m, t, b: (0, m, 0, 0)),
            pl.BlockSpec((3, group, row_dev, cols), lambda m, t, b: (0, m, 0, 0)),
            pl.BlockSpec((3, group, row_dev, cols), lambda m, t, b: (0, m, 0, 0)),
            pl.BlockSpec((group, row_dev, cols), lambda m, t, b: (m, 0, 0)),
        ],
        out_specs=pl.BlockSpec(
            (mods, n_peak, frame_dev, row_dev, width), lambda m, t, b: (0, 0, 0, 0, 0)
        ),
    )
    return pl.pallas_call(
        lambda *refs: calibrate_kernel(group, *refs),
        grid_spec=grid_spec,
        out_shape=jax.ShapeDtypeStruct((mods, n_peak, frame_dev, row_dev, width), jnp.bfloat16),
    )(table, bounds.reshape(-1), raw, pedestal, gain, good)


def score_kernel(n_peak, levels, low_ref, mean_ref, rms_ref, frame_ref, cycle_ref, left_ref, right_ref, snr_ref, bent_ref):
    frame_pos = pl.program_id(0) * pl.num_programs(1) + pl.program_id(1)
    cycle = cycle_ref[...]
    rows, cols = cycle.shape
    values = frame_ref[...].astype(jnp.float32).reshape(rows, cols)
    tops = mean_ref.shape[1] - 1
    pixel_mean = jnp.zeros((rows, cols), jnp.float32)
    pixel_rms = jnp.ones((rows, cols), jnp.float32)
    for j in range(levels):
        level = jnp.minimum(low_ref[0] + j, tops)
        hit = cycle == level
        pixel_mean = jnp.where(hit, mean_ref[frame_pos, level], pixel_mean)
        pixel_rms = jnp.where(hit, rms_ref[frame_pos, level], pixel_rms)
    score = (values - pixel_mean) / pixel_rms
    peak_pos = lax.axis_index("peak")
    row_ids = lax.broadcasted_iota(jnp.int32, (rows, cols), 0)
    col_ids = lax.broadcasted_iota(jnp.int32, (rows, cols), 1)
    left_col = jnp.where(peak_pos == 0, 0.0, left_ref[...])
    right_col = jnp.where(peak_pos == n_peak - 1, 0.0, right_ref[...])
    total = 4.0 * score
    for shift in (1, rows - 1):
        moved = pltpu.roll(score, shift, 0)
        source = pltpu.roll(row_ids, shift, 0)
        total = total - jnp.where(jnp.abs(source - row_ids) == 1, moved, 0.0)
    for shift in (1, cols - 1):
        moved = pltpu.roll(score, shift, 1)
        source = pltpu.roll(col_ids, shift, 1)
        near = jnp.where(source == cols - 1, left_col, right_col)
        total = total - jnp.where(jnp.abs(source - col_ids) == 1, moved, near)
    snr_ref[...] = score.astype(snr_ref.dtype)
    bent_ref[...] = total.astype(bent_ref.dtype)


def score_outputs(got, cycle, cycle_average, cycle_rms, left, right, n_peak):
    n_calib, _, frame_dev, row_dev, cols = got.shape
    rows, _ = cycle.shape
    frames = n_peak * frame_dev
    span = (rows * rows + cols * cols) ** 0.5
    levels = min(CYCLES, int(span // CYCLE_W) + 3)
    low = jnp.min(cycle).reshape(1)
    source = pl.BlockSpec((n_calib, None, None, row_dev, cols), lambda p, f, *_: (0, p, f, 0, 0))
    block = pl.BlockSpec((None, rows, cols), lambda p, f, *_: (p * frame_dev + f, 0, 0))
    edge = pl.BlockSpec((None, rows, 1), lambda p, f, *_: (p * frame_dev + f, 0, 0))
    grid_spec = pltpu.PrefetchScalarGridSpec(
        num_scalar_prefetch=3,
        grid=(n_peak, frame_dev),
        in_specs=[source, pl.BlockSpec((rows, cols), lambda p, f, *_: (0, 0)), edge, edge],
        out_specs=[block, block],
    )
    return pl.pallas_call(
        lambda *refs: score_kernel(n_peak, levels, *refs),
        grid_spec=grid_spec,
        out_shape=[jax.ShapeDtypeStruct((frames, rows, cols), jnp.bfloat16)] * 2,
    )(low, cycle_average, cycle_rms, got, cycle, left, right)


def laplace(padded):
    center = padded[..., 1:-1, 1:-1]
    return (
        4.0 * center
        - padded[..., :-2, 1:-1]
        - padded[..., 2:, 1:-1]
        - padded[..., 1:-1, :-2]
        - padded[..., 1:-1, 2:]
    )


def local_present(good, table, row_src, mrows, slot_rows):
    n_peak = lax.axis_size("peak")
    width = good.shape[2] // n_peak
    start = lax.axis_index("peak") * width
    part = lax.dynamic_slice_in_dim(good, start, width, axis=2)
    col = start + jnp.arange(width, dtype=jnp.int32)
    ypos = (table // SLOT_C)[:, None] * mrows + row_src[None, :]
    xpos = (table % SLOT_C)[:, None] * COLS + col[None, :]
    dy_two = 2 * ypos + 1 - slot_rows * mrows
    dx_two = 2 * xpos + 1 - SLOT_C * COLS
    dist = dy_two[:, :, None] * dy_two[:, :, None] + dx_two[:, None, :] * dx_two[:, None, :]
    cycle = cycle_index(dist)
    levels = jnp.arange(CYCLES, dtype=jnp.int32)
    hit = jnp.where(cycle[..., None] == levels, part[..., None], 0)
    return jnp.sum(hit, axis=(0, 1, 2)).astype(jnp.float32)


def gather_sum_kernel(
    n_calib, n_peak, x_ref, o_ref, near, far, partial, near_send, near_recv, far_send, far_recv
):
    my_calib = lax.axis_index("calib")
    my_peak = lax.axis_index("peak")
    near[n_peak - 1] = x_ref[...]
    barrier = pltpu.get_barrier_semaphore()

    def peak_peer(step):
        return (my_calib, lax.rem(my_peak + step, n_peak))

    def calib_peer(step):
        return (lax.rem(my_calib + step, n_calib), my_peak)

    def greet_peak(step, carry):
        pl.semaphore_signal(
            barrier, inc=1, device_id=peak_peer(step), device_id_type=pl.DeviceIdType.MESH
        )
        return carry

    def greet_calib(step, carry):
        pl.semaphore_signal(
            barrier, inc=1, device_id=calib_peer(step), device_id_type=pl.DeviceIdType.MESH
        )
        return carry

    lax.fori_loop(1, n_peak, greet_peak, 0)
    lax.fori_loop(1, n_calib, greet_calib, 0)
    pl.semaphore_wait(barrier, n_peak - 1 + n_calib - 1)

    def send_near(step, carry):
        pltpu.make_async_remote_copy(
            src_ref=x_ref,
            dst_ref=near.at[n_peak - 1 - step],
            send_sem=near_send,
            recv_sem=near_recv,
            device_id=peak_peer(step),
            device_id_type=pl.DeviceIdType.MESH,
        ).start()
        return carry

    lax.fori_loop(1, n_peak, send_near, 0)
    every_near = pltpu.make_async_remote_copy(
        src_ref=near.at[pl.ds(0, n_peak - 1)],
        dst_ref=near.at[pl.ds(0, n_peak - 1)],
        send_sem=near_send,
        recv_sem=near_recv,
        device_id=peak_peer(1),
        device_id_type=pl.DeviceIdType.MESH,
    )
    every_near.wait_send()
    every_near.wait_recv()

    def add_near(source, acc):
        return acc + near[lax.rem(source - my_peak - 1 + 2 * n_peak, n_peak)]

    partial[...] = lax.fori_loop(0, n_peak, add_near, jnp.zeros(x_ref.shape, x_ref.dtype))
    far[n_calib - 1] = partial[...]

    def send_far(step, carry):
        pltpu.make_async_remote_copy(
            src_ref=partial,
            dst_ref=far.at[n_calib - 1 - step],
            send_sem=far_send,
            recv_sem=far_recv,
            device_id=calib_peer(step),
            device_id_type=pl.DeviceIdType.MESH,
        ).start()
        return carry

    lax.fori_loop(1, n_calib, send_far, 0)
    every_far = pltpu.make_async_remote_copy(
        src_ref=far.at[pl.ds(0, n_calib - 1)],
        dst_ref=far.at[pl.ds(0, n_calib - 1)],
        send_sem=far_send,
        recv_sem=far_recv,
        device_id=calib_peer(1),
        device_id_type=pl.DeviceIdType.MESH,
    )
    every_far.wait_send()
    every_far.wait_recv()

    def add_far(source, acc):
        return acc + far[lax.rem(source - my_calib - 1 + 2 * n_calib, n_calib)]

    o_ref[...] = lax.fori_loop(0, n_calib, add_far, jnp.zeros(x_ref.shape, x_ref.dtype))


def gather_sum(x):
    n_calib = lax.axis_size("calib")
    n_peak = lax.axis_size("peak")
    return pl.pallas_call(
        lambda *refs: gather_sum_kernel(n_calib, n_peak, *refs),
        out_shape=jax.ShapeDtypeStruct(x.shape, x.dtype),
        in_specs=[pl.BlockSpec(memory_space=pltpu.VMEM)],
        out_specs=pl.BlockSpec(memory_space=pltpu.VMEM),
        scratch_shapes=[
            pltpu.VMEM((n_peak,) + x.shape, x.dtype),
            pltpu.VMEM((n_calib,) + x.shape, x.dtype),
            pltpu.VMEM(x.shape, x.dtype),
            pltpu.SemaphoreType.DMA,
            pltpu.SemaphoreType.DMA,
            pltpu.SemaphoreType.DMA,
            pltpu.SemaphoreType.DMA,
        ],
        compiler_params=pltpu.CompilerParams(collective_id=0, has_side_effects=True),
    )(x)


def cycle_stats(first, second, present_flag):
    cycle_average = first / present_flag[None, :]
    cycle_rms = jnp.sqrt(second / present_flag[None, :] + 1e-06)
    return (cycle_average, cycle_rms)


def body(raw, pedestal, gain, good, bounds, table):
    frame_dev, mods, row_dev, cols = raw.shape
    n_calib = lax.axis_size("calib")
    n_peak = lax.axis_size("peak")
    mrows = row_dev * n_calib
    slot_rows = mods // SLOT_C
    width_here = cols // n_peak
    frames_all = frame_dev * n_peak
    row_src = lax.axis_index("calib") * row_dev + jnp.arange(row_dev, dtype=jnp.int32)
    send = calibrate_send(raw, pedestal, gain, good, bounds, table, n_peak)
    send = send.reshape(mods * n_peak, frame_dev, row_dev, width_here)
    present_part = local_present(good, table, row_src, mrows, slot_rows)
    got = lax.all_to_all(send, ("calib", "peak"), 0, 0, tiled=True)
    got = got.reshape(n_calib, n_peak, frame_dev, row_dev, width_here)
    slot = lax.axis_index("calib")
    col_dst = lax.axis_index("peak") * width_here + jnp.arange(width_here, dtype=jnp.int32)
    ypos = slot // SLOT_C * mrows + jnp.arange(mrows, dtype=jnp.int32)
    xpos = slot % SLOT_C * COLS + col_dst
    dy_two = 2 * ypos + 1 - slot_rows * mrows
    dx_two = 2 * xpos + 1 - SLOT_C * COLS
    cycle = cycle_index(dy_two[:, None] * dy_two[:, None] + dx_two[None, :] * dx_two[None, :])
    levels = jnp.arange(CYCLES, dtype=jnp.int32)
    hits = (cycle[None] == levels[:, None, None]).astype(jnp.bfloat16)
    hits = hits.reshape(CYCLES, n_calib, row_dev, width_here)
    values = got.astype(jnp.float32)
    square = values * values
    square_top = lax.reduce_precision(square, exponent_bits=8, mantissa_bits=7)
    square_hi = square_top.astype(jnp.bfloat16)
    square_lo = (square - square_top).astype(jnp.bfloat16)

    def cycle_sums(part):
        sums = jnp.einsum("ipfrc,kirc->pfk", part, hits, preferred_element_type=jnp.float32)
        return sums.reshape(frames_all, CYCLES)

    first = cycle_sums(got)
    second = cycle_sums(square_hi) + cycle_sums(square_lo)
    lanes = 128
    packed = jnp.concatenate(
        [
            first,
            second,
            jnp.zeros((frames_all, CYCLES), jnp.float32).at[0].set(present_part),
            jnp.zeros((frames_all, lanes - 3 * CYCLES), jnp.float32),
        ],
        axis=1,
    )
    summed = gather_sum(packed)
    first = summed[:, :CYCLES]
    second = summed[:, CYCLES : 2 * CYCLES]
    present_flag = summed[0, 2 * CYCLES : 3 * CYCLES]
    cycle_average, cycle_rms = cycle_stats(first, second, present_flag)
    edge_cycle = jnp.stack([cycle[:, width_here - 1], cycle[:, 0]], axis=1)
    edge_values = jnp.stack([got[..., width_here - 1], got[..., 0]], axis=-1)
    edge_values = jnp.transpose(edge_values, (1, 2, 0, 3, 4)).reshape(frames_all, mrows, 2)
    edge_hits = (edge_cycle.reshape(1, -1) == levels[:, None]).astype(jnp.float32)
    edge_table = jnp.einsum(
        "fk,kp->fp",
        jnp.concatenate([cycle_average, cycle_rms], axis=0),
        edge_hits,
        precision=precise_variant,
    ).reshape(2 * frames_all, mrows, 2)
    edge_mean = edge_table[:frames_all]
    edge_rms = edge_table[frames_all:]
    edge_score = (edge_values.astype(jnp.float32) - edge_mean) / edge_rms
    fwd = [(i, i + 1) for i in range(n_peak - 1)]
    bwd = [(i + 1, i) for i in range(n_peak - 1)]
    left = lax.ppermute(edge_score[:, :, :1], "peak", fwd)
    right = lax.ppermute(edge_score[:, :, 1:], "peak", bwd)
    snr, bent = score_outputs(got, cycle, cycle_average, cycle_rms, left, right, n_peak)
    return (snr[:, None], bent[:, None])


def solution(mesh):
    in_specs = (
        P("peak", None, "calib", None),
        P(None, None, "calib", None),
        P(None, None, "calib", None),
        P(None, "calib", None),
        P(),
        P(),
    )
    out_specs = (P(None, "calib", None, "peak"), P(None, "calib", None, "peak"))
    return jax.shard_map(body, mesh=mesh, in_specs=in_specs, out_specs=out_specs, check_vma=False)
```

```python
import jax
import jax.numpy as jnp
from jax import lax
from jax.sharding import PartitionSpec as P
from jax.experimental import pallas as pl
from jax.experimental.pallas import tpu as pltpu

COLS = 1024
BANDS = 8
SLOT_C = 4
CYCLES = 32
CYCLE_W = 64


precise_variant = lax.Precision.HIGHEST


def padded_2(block, sides, width):
    for axis, dim in sides:
        count = lax.axis_size(axis)
        forward = [(i, i + 1) for i in range(count - 1)]
        backward = [(target, source) for source, target in forward]
        low = lax.ppermute(
            lax.slice_in_dim(block, block.shape[dim] - width, None, axis=dim), axis, forward
        )
        high = lax.ppermute(lax.slice_in_dim(block, 0, width, axis=dim), axis, backward)
        block = jnp.concatenate([low, block, high], axis=dim)
    return block


def cycle_index(dist):
    levels = jnp.arange(1, CYCLES, dtype=jnp.int32)
    lows = (2 * CYCLE_W * levels) ** 2
    return jnp.sum((dist[..., None] >= lows).astype(jnp.int32), axis=-1)


def cycle_onehot(slot, row_pos, col_pos, mrows, slot_rows):
    ypos = slot // SLOT_C * mrows + row_pos
    xpos = slot % SLOT_C * COLS + col_pos
    dy_two = 2 * ypos + 1 - slot_rows * mrows
    dx_two = 2 * xpos + 1 - SLOT_C * COLS
    dist = dy_two[:, None] * dy_two[:, None] + dx_two[None, :] * dx_two[None, :]
    levels = jnp.arange(CYCLES, dtype=jnp.int32)
    lows = (2 * CYCLE_W * levels) ** 2
    cycle = jnp.sum((dist[None] >= lows[:, None, None]).astype(jnp.int32), axis=0) - 1
    hits = (cycle[None] == levels[:, None, None]).astype(jnp.float32)
    return hits.reshape(CYCLES, -1)


def calibrate(raw, pedestal, gain, good, bounds):
    code = raw // 2048
    counts_adc = (raw % 2048).astype(jnp.float32)
    base = jnp.where(code == 0, pedestal[0], jnp.where(code == 1, pedestal[1], pedestal[2]))
    gain_factor = gain.astype(jnp.float32)
    scale = jnp.where(
        code == 0, gain_factor[0], jnp.where(code == 1, gain_factor[1], gain_factor[2])
    )
    weight_factor = good.astype(jnp.float32)
    energy = weight_factor * (counts_adc - base) / scale
    columns = jnp.arange(raw.shape[-1], dtype=jnp.int32)
    band = jnp.sum((columns[None, :, None] >= bounds[:, None, :]).astype(jnp.int32), axis=2)
    member_entry = (band[:, :, None] == jnp.arange(BANDS, dtype=jnp.int32)[None, None, :]).astype(
        jnp.float32
    )
    totals = jnp.einsum("fmrc,mcb->fmrb", energy, member_entry, precision=precise_variant)
    present_flag = jnp.einsum(
        "tlg,tgd->tld", weight_factor, member_entry, precision=precise_variant
    )
    level = totals / jnp.maximum(present_flag, 1.0)
    spread = jnp.einsum("fmrb,mcb->fmrc", level, member_entry, precision=precise_variant)
    return (weight_factor * (energy - spread)).astype(jnp.bfloat16)


def calibrate_kernel(group, table_ref, bounds_ref, raw_ref, ped_ref, gain_ref, good_ref, out_ref):
    step = pl.program_id(0)
    cols = raw_ref.shape[-1]
    columns = lax.broadcasted_iota(jnp.int32, (1, cols), 1)
    quarters = out_ref.shape[1]
    width = cols // quarters
    for inner in range(group):
        module = step * group + inner
        raw = raw_ref[:, inner]
        code = raw // 2048
        counts_adc = (raw % 2048).astype(jnp.float32)
        base = jnp.where(
            code == 0, ped_ref[0, inner], jnp.where(code == 1, ped_ref[1, inner], ped_ref[2, inner])
        )
        scale = jnp.where(
            code == 0,
            gain_ref[0, inner].astype(jnp.float32),
            jnp.where(
                code == 1,
                gain_ref[1, inner].astype(jnp.float32),
                gain_ref[2, inner].astype(jnp.float32),
            ),
        )
        weight_factor = good_ref[inner].astype(jnp.float32)
        energy = weight_factor * (counts_adc - base) / scale
        band = jnp.zeros((1, cols), jnp.int32)
        for j in range(BANDS - 1):
            band = band + (columns >= bounds_ref[module * (BANDS - 1) + j]).astype(jnp.int32)
        spread = jnp.zeros(energy.shape, jnp.float32)
        for b in range(BANDS):
            member = band == b
            totals = jnp.sum(jnp.where(member, energy, 0.0), axis=-1, keepdims=True)
            present = jnp.sum(jnp.where(member, weight_factor, 0.0), axis=-1, keepdims=True)
            spread = jnp.where(member, totals / jnp.maximum(present, 1.0), spread)
        corrected = (weight_factor * (energy - spread)).astype(jnp.bfloat16)
        slot = table_ref[module]
        for q in range(quarters):
            out_ref[slot, q] = corrected[:, :, q * width : (q + 1) * width]


def calibrate_send(raw, pedestal, gain, good, bounds, table, n_peak):
    frame_dev, mods, row_dev, cols = raw.shape
    width = cols // n_peak
    group = 8
    grid_spec = pltpu.PrefetchScalarGridSpec(
        num_scalar_prefetch=2,
        grid=(mods // group,),
        in_specs=[
            pl.BlockSpec((frame_dev, group, row_dev, cols), lambda m, t, b: (0, m, 0, 0)),
            pl.BlockSpec((3, group, row_dev, cols), lambda m, t, b: (0, m, 0, 0)),
            pl.BlockSpec((3, group, row_dev, cols), lambda m, t, b: (0, m, 0, 0)),
            pl.BlockSpec((group, row_dev, cols), lambda m, t, b: (m, 0, 0)),
        ],
        out_specs=pl.BlockSpec(
            (mods, n_peak, frame_dev, row_dev, width), lambda m, t, b: (0, 0, 0, 0, 0)
        ),
    )
    return pl.pallas_call(
        lambda *refs: calibrate_kernel(group, *refs),
        grid_spec=grid_spec,
        out_shape=jax.ShapeDtypeStruct((mods, n_peak, frame_dev, row_dev, width), jnp.bfloat16),
    )(table, bounds.reshape(-1), raw, pedestal, gain, good)


def score_kernel(
    n_peak, levels, low_ref, mean_ref, rms_ref, frame_ref, cycle_ref, left_ref, right_ref,
    left_cycle_ref, right_cycle_ref, snr_ref, bent_ref
):
    frame_pos = pl.program_id(0)
    cycle = cycle_ref[...]
    values = frame_ref[...].astype(jnp.float32)
    rows, cols = values.shape
    tops = mean_ref.shape[1] - 1
    pixel_mean = jnp.zeros((rows, cols), jnp.float32)
    pixel_rms = jnp.ones((rows, cols), jnp.float32)
    for j in range(levels):
        level = jnp.minimum(low_ref[0] + j, tops)
        hit = cycle == level
        pixel_mean = jnp.where(hit, mean_ref[frame_pos, level], pixel_mean)
        pixel_rms = jnp.where(hit, rms_ref[frame_pos, level], pixel_rms)
    score = (values - pixel_mean) / pixel_rms
    peak_pos = lax.axis_index("peak")
    row_ids = lax.broadcasted_iota(jnp.int32, (rows, cols), 0)
    col_ids = lax.broadcasted_iota(jnp.int32, (rows, cols), 1)
    def edge_score(edge_ref, edge_cycle_ref):
        edge_values = edge_ref[...].astype(jnp.float32)
        edge_cycle = edge_cycle_ref[...]
        edge_mean = jnp.zeros(edge_values.shape, jnp.float32)
        edge_rms = jnp.ones(edge_values.shape, jnp.float32)
        for j in range(levels):
            level = jnp.minimum(low_ref[0] + j, tops)
            hit = edge_cycle == level
            edge_mean = jnp.where(hit, mean_ref[frame_pos, level], edge_mean)
            edge_rms = jnp.where(hit, rms_ref[frame_pos, level], edge_rms)
        return (edge_values - edge_mean) / edge_rms

    left_col = jnp.where(peak_pos == 0, 0.0, edge_score(left_ref, left_cycle_ref))
    right_col = jnp.where(peak_pos == n_peak - 1, 0.0, edge_score(right_ref, right_cycle_ref))
    total = 4.0 * score
    for shift in (1, rows - 1):
        moved = pltpu.roll(score, shift, 0)
        source = pltpu.roll(row_ids, shift, 0)
        total = total - jnp.where(jnp.abs(source - row_ids) == 1, moved, 0.0)
    for shift in (1, cols - 1):
        moved = pltpu.roll(score, shift, 1)
        source = pltpu.roll(col_ids, shift, 1)
        near = jnp.where(source == cols - 1, left_col, right_col)
        total = total - jnp.where(jnp.abs(source - col_ids) == 1, moved, near)
    snr_ref[...] = score.astype(snr_ref.dtype)
    bent_ref[...] = total.astype(bent_ref.dtype)


def score_outputs(frame, cycle, low, cycle_average, cycle_rms, left, right, left_cycle, right_cycle, n_peak):
    frames, rows, cols = frame.shape
    span = (rows * rows + (cols + 2) * (cols + 2)) ** 0.5
    levels = min(CYCLES, int(span // CYCLE_W) + 3)
    block = pl.BlockSpec((None, rows, cols), lambda f, *_: (f, 0, 0))
    edge = pl.BlockSpec((None, rows, 1), lambda f, *_: (f, 0, 0))
    fixed = pl.BlockSpec((rows, cols), lambda f, *_: (0, 0))
    fixed_edge = pl.BlockSpec((rows, 1), lambda f, *_: (0, 0))
    grid_spec = pltpu.PrefetchScalarGridSpec(
        num_scalar_prefetch=3,
        grid=(frames,),
        in_specs=[block, fixed, edge, edge, fixed_edge, fixed_edge],
        out_specs=[block, block],
    )
    return pl.pallas_call(
        lambda *refs: score_kernel(n_peak, levels, *refs),
        grid_spec=grid_spec,
        out_shape=[jax.ShapeDtypeStruct(frame.shape, jnp.bfloat16)] * 2,
    )(low, cycle_average, cycle_rms, frame, cycle, left, right, left_cycle, right_cycle)


def laplace(padded):
    center = padded[..., 1:-1, 1:-1]
    return (
        4.0 * center
        - padded[..., :-2, 1:-1]
        - padded[..., 2:, 1:-1]
        - padded[..., 1:-1, :-2]
        - padded[..., 1:-1, 2:]
    )


def local_present(good, table, row_src, mrows, slot_rows):
    n_peak = lax.axis_size("peak")
    width = good.shape[2] // n_peak
    start = lax.axis_index("peak") * width
    part = lax.dynamic_slice_in_dim(good, start, width, axis=2)
    col = start + jnp.arange(width, dtype=jnp.int32)
    ypos = (table // SLOT_C)[:, None] * mrows + row_src[None, :]
    xpos = (table % SLOT_C)[:, None] * COLS + col[None, :]
    dy_two = 2 * ypos + 1 - slot_rows * mrows
    dx_two = 2 * xpos + 1 - SLOT_C * COLS
    dist = dy_two[:, :, None] * dy_two[:, :, None] + dx_two[:, None, :] * dx_two[:, None, :]
    cycle = cycle_index(dist)
    levels = jnp.arange(CYCLES, dtype=jnp.int32)
    hit = jnp.where(cycle[..., None] == levels, part[..., None], 0)
    return jnp.sum(hit, axis=(0, 1, 2)).astype(jnp.float32)


def gather_sum_kernel(
    n_calib, n_peak, x_ref, o_ref, near, far, partial, near_send, near_recv, far_send, far_recv
):
    my_calib = lax.axis_index("calib")
    my_peak = lax.axis_index("peak")
    near[n_peak - 1] = x_ref[...]
    barrier = pltpu.get_barrier_semaphore()

    def peak_peer(step):
        return (my_calib, lax.rem(my_peak + step, n_peak))

    def calib_peer(step):
        return (lax.rem(my_calib + step, n_calib), my_peak)

    def greet_peak(step, carry):
        pl.semaphore_signal(
            barrier, inc=1, device_id=peak_peer(step), device_id_type=pl.DeviceIdType.MESH
        )
        return carry

    def greet_calib(step, carry):
        pl.semaphore_signal(
            barrier, inc=1, device_id=calib_peer(step), device_id_type=pl.DeviceIdType.MESH
        )
        return carry

    lax.fori_loop(1, n_peak, greet_peak, 0)
    lax.fori_loop(1, n_calib, greet_calib, 0)
    pl.semaphore_wait(barrier, n_peak - 1 + n_calib - 1)

    def send_near(step, carry):
        pltpu.make_async_remote_copy(
            src_ref=x_ref,
            dst_ref=near.at[n_peak - 1 - step],
            send_sem=near_send,
            recv_sem=near_recv,
            device_id=peak_peer(step),
            device_id_type=pl.DeviceIdType.MESH,
        ).start()
        return carry

    lax.fori_loop(1, n_peak, send_near, 0)
    every_near = pltpu.make_async_remote_copy(
        src_ref=near.at[pl.ds(0, n_peak - 1)],
        dst_ref=near.at[pl.ds(0, n_peak - 1)],
        send_sem=near_send,
        recv_sem=near_recv,
        device_id=peak_peer(1),
        device_id_type=pl.DeviceIdType.MESH,
    )
    every_near.wait_send()
    every_near.wait_recv()

    def add_near(source, acc):
        return acc + near[lax.rem(source - my_peak - 1 + 2 * n_peak, n_peak)]

    partial[...] = lax.fori_loop(0, n_peak, add_near, jnp.zeros(x_ref.shape, x_ref.dtype))
    far[n_calib - 1] = partial[...]

    def send_far(step, carry):
        pltpu.make_async_remote_copy(
            src_ref=partial,
            dst_ref=far.at[n_calib - 1 - step],
            send_sem=far_send,
            recv_sem=far_recv,
            device_id=calib_peer(step),
            device_id_type=pl.DeviceIdType.MESH,
        ).start()
        return carry

    lax.fori_loop(1, n_calib, send_far, 0)
    every_far = pltpu.make_async_remote_copy(
        src_ref=far.at[pl.ds(0, n_calib - 1)],
        dst_ref=far.at[pl.ds(0, n_calib - 1)],
        send_sem=far_send,
        recv_sem=far_recv,
        device_id=calib_peer(1),
        device_id_type=pl.DeviceIdType.MESH,
    )
    every_far.wait_send()
    every_far.wait_recv()

    def add_far(source, acc):
        return acc + far[lax.rem(source - my_calib - 1 + 2 * n_calib, n_calib)]

    o_ref[...] = lax.fori_loop(0, n_calib, add_far, jnp.zeros(x_ref.shape, x_ref.dtype))


def gather_sum(x, *after):
    n_calib = lax.axis_size("calib")
    n_peak = lax.axis_size("peak")
    held = len(after)
    return pl.pallas_call(
        lambda x_ref, *refs: gather_sum_kernel(n_calib, n_peak, x_ref, *refs[held:]),
        out_shape=jax.ShapeDtypeStruct(x.shape, x.dtype),
        in_specs=[pl.BlockSpec(memory_space=pltpu.VMEM)]
        + [pl.BlockSpec(memory_space=pl.ANY)] * held,
        out_specs=pl.BlockSpec(memory_space=pltpu.VMEM),
        scratch_shapes=[
            pltpu.VMEM((n_peak,) + x.shape, x.dtype),
            pltpu.VMEM((n_calib,) + x.shape, x.dtype),
            pltpu.VMEM(x.shape, x.dtype),
            pltpu.SemaphoreType.DMA,
            pltpu.SemaphoreType.DMA,
            pltpu.SemaphoreType.DMA,
            pltpu.SemaphoreType.DMA,
        ],
        compiler_params=pltpu.CompilerParams(collective_id=0, has_side_effects=True),
    )(x, *after)


def cycle_stats(first, second, present_flag):
    cycle_average = first / present_flag[None, :]
    cycle_rms = jnp.sqrt(second / present_flag[None, :] + 1e-06)
    return (cycle_average, cycle_rms)


def body(raw, pedestal, gain, good, bounds, table):
    frame_dev, mods, row_dev, cols = raw.shape
    n_calib = lax.axis_size("calib")
    n_peak = lax.axis_size("peak")
    mrows = row_dev * n_calib
    slot_rows = mods // SLOT_C
    width_here = cols // n_peak
    frames_all = frame_dev * n_peak
    row_src = lax.axis_index("calib") * row_dev + jnp.arange(row_dev, dtype=jnp.int32)
    send = calibrate_send(raw, pedestal, gain, good, bounds, table, n_peak)
    send = send.reshape(mods * n_peak, frame_dev, row_dev, width_here)
    present_part = local_present(good, table, row_src, mrows, slot_rows)
    got = lax.all_to_all(send, ("calib", "peak"), 0, 0, tiled=True)
    got = got.reshape(n_calib, n_peak, frame_dev, row_dev, width_here)
    frame = jnp.transpose(got, (1, 2, 0, 3, 4)).reshape(frames_all, mrows, width_here)
    slot = lax.axis_index("calib")
    col_dst = lax.axis_index("peak") * width_here + jnp.arange(width_here, dtype=jnp.int32)
    ypos = slot // SLOT_C * mrows + jnp.arange(mrows, dtype=jnp.int32)
    xpos = slot % SLOT_C * COLS + col_dst
    dy_two = 2 * ypos + 1 - slot_rows * mrows
    dx_two = 2 * xpos + 1 - SLOT_C * COLS
    cycle = cycle_index(dy_two[:, None] * dy_two[:, None] + dx_two[None, :] * dx_two[None, :])
    side_x = jnp.stack([dx_two[0] - 2, dx_two[width_here - 1] + 2])
    side_cycle = cycle_index(dy_two[:, None] * dy_two[:, None] + side_x[None, :] * side_x[None, :])
    left_cycle = side_cycle[:, :1]
    right_cycle = side_cycle[:, 1:]
    low = jnp.minimum(jnp.min(cycle), jnp.min(side_cycle)).reshape(1)
    fwd = [(i, i + 1) for i in range(n_peak - 1)]
    bwd = [(i + 1, i) for i in range(n_peak - 1)]
    left = lax.ppermute(frame[:, :, width_here - 1 :], "peak", fwd)
    right = lax.ppermute(frame[:, :, :1], "peak", bwd)
    levels = jnp.arange(CYCLES, dtype=jnp.int32)
    hits = (cycle.reshape(1, -1) == levels[:, None]).astype(jnp.bfloat16)
    pixels = frame.reshape(frames_all, -1)
    values = pixels.astype(jnp.float32)
    square = values * values
    square_top = lax.reduce_precision(square, exponent_bits=8, mantissa_bits=7)
    square_hi = square_top.astype(jnp.bfloat16)
    square_lo = (square - square_top).astype(jnp.bfloat16)
    stacked = jnp.concatenate([pixels, square_hi, square_lo], axis=0)
    sums = jnp.einsum("fp,kp->fk", stacked, hits, preferred_element_type=jnp.float32)
    first = sums[:frames_all]
    second = sums[frames_all : 2 * frames_all] + sums[2 * frames_all :]
    lanes = 128
    packed = jnp.concatenate(
        [
            first,
            second,
            jnp.zeros((frames_all, CYCLES), jnp.float32).at[0].set(present_part),
            jnp.zeros((frames_all, lanes - 3 * CYCLES), jnp.float32),
        ],
        axis=1,
    )
    summed = gather_sum(packed, left, right)
    first = summed[:, :CYCLES]
    second = summed[:, CYCLES : 2 * CYCLES]
    present_flag = summed[0, 2 * CYCLES : 3 * CYCLES]
    cycle_average, cycle_rms = cycle_stats(first, second, present_flag)
    snr, bent = score_outputs(
        frame, cycle, low, cycle_average, cycle_rms, left, right, left_cycle, right_cycle, n_peak
    )
    return (snr[:, None], bent[:, None])


def solution(mesh):
    in_specs = (
        P("peak", None, "calib", None),
        P(None, None, "calib", None),
        P(None, None, "calib", None),
        P(None, "calib", None),
        P(),
        P(),
    )
    out_specs = (P(None, "calib", None, "peak"), P(None, "calib", None, "peak"))
    return jax.shard_map(body, mesh=mesh, in_specs=in_specs, out_specs=out_specs, check_vma=False)
```

```python
import jax
import jax.numpy as jnp
from jax import lax
from jax.sharding import PartitionSpec as P
from jax.experimental import pallas as pl
from jax.experimental.pallas import tpu as pltpu

COLS = 1024
BANDS = 8
SLOT_C = 4
CYCLES = 32
CYCLE_W = 64


precise_variant = lax.Precision.HIGHEST


def padded_2(block, sides, width):
    for axis, dim in sides:
        count = lax.axis_size(axis)
        forward = [(i, i + 1) for i in range(count - 1)]
        backward = [(target, source) for source, target in forward]
        low = lax.ppermute(
            lax.slice_in_dim(block, block.shape[dim] - width, None, axis=dim), axis, forward
        )
        high = lax.ppermute(lax.slice_in_dim(block, 0, width, axis=dim), axis, backward)
        block = jnp.concatenate([low, block, high], axis=dim)
    return block


def cycle_index(dist):
    levels = jnp.arange(1, CYCLES, dtype=jnp.int32)
    lows = (2 * CYCLE_W * levels) ** 2
    return jnp.sum((dist[..., None] >= lows).astype(jnp.int32), axis=-1)


def cycle_onehot(slot, row_pos, col_pos, mrows, slot_rows):
    ypos = slot // SLOT_C * mrows + row_pos
    xpos = slot % SLOT_C * COLS + col_pos
    dy_two = 2 * ypos + 1 - slot_rows * mrows
    dx_two = 2 * xpos + 1 - SLOT_C * COLS
    dist = dy_two[:, None] * dy_two[:, None] + dx_two[None, :] * dx_two[None, :]
    levels = jnp.arange(CYCLES, dtype=jnp.int32)
    lows = (2 * CYCLE_W * levels) ** 2
    cycle = jnp.sum((dist[None] >= lows[:, None, None]).astype(jnp.int32), axis=0) - 1
    hits = (cycle[None] == levels[:, None, None]).astype(jnp.float32)
    return hits.reshape(CYCLES, -1)


def calibrate(raw, pedestal, gain, good, bounds):
    code = raw // 2048
    counts_adc = (raw % 2048).astype(jnp.float32)
    base = jnp.where(code == 0, pedestal[0], jnp.where(code == 1, pedestal[1], pedestal[2]))
    gain_factor = gain.astype(jnp.float32)
    scale = jnp.where(
        code == 0, gain_factor[0], jnp.where(code == 1, gain_factor[1], gain_factor[2])
    )
    weight_factor = good.astype(jnp.float32)
    energy = weight_factor * (counts_adc - base) / scale
    columns = jnp.arange(raw.shape[-1], dtype=jnp.int32)
    band = jnp.sum((columns[None, :, None] >= bounds[:, None, :]).astype(jnp.int32), axis=2)
    member_entry = (band[:, :, None] == jnp.arange(BANDS, dtype=jnp.int32)[None, None, :]).astype(
        jnp.float32
    )
    totals = jnp.einsum("fmrc,mcb->fmrb", energy, member_entry, precision=precise_variant)
    present_flag = jnp.einsum(
        "tlg,tgd->tld", weight_factor, member_entry, precision=precise_variant
    )
    level = totals / jnp.maximum(present_flag, 1.0)
    spread = jnp.einsum("fmrb,mcb->fmrc", level, member_entry, precision=precise_variant)
    return (weight_factor * (energy - spread)).astype(jnp.bfloat16)


def calibrate_kernel(group, table_ref, bounds_ref, raw_ref, ped_ref, gain_ref, good_ref, out_ref):
    step = pl.program_id(0)
    cols = raw_ref.shape[-1]
    columns = lax.broadcasted_iota(jnp.int32, (1, cols), 1)
    quarters = out_ref.shape[1]
    width = cols // quarters
    for inner in range(group):
        module = step * group + inner
        raw = raw_ref[:, inner]
        code = raw // 2048
        counts_adc = (raw % 2048).astype(jnp.float32)
        base = jnp.where(
            code == 0, ped_ref[0, inner], jnp.where(code == 1, ped_ref[1, inner], ped_ref[2, inner])
        )
        scale = jnp.where(
            code == 0,
            gain_ref[0, inner].astype(jnp.float32),
            jnp.where(
                code == 1,
                gain_ref[1, inner].astype(jnp.float32),
                gain_ref[2, inner].astype(jnp.float32),
            ),
        )
        weight_factor = good_ref[inner].astype(jnp.float32)
        energy = weight_factor * (counts_adc - base) / scale
        band = jnp.zeros((1, cols), jnp.int32)
        for j in range(BANDS - 1):
            band = band + (columns >= bounds_ref[module * (BANDS - 1) + j]).astype(jnp.int32)
        spread = jnp.zeros(energy.shape, jnp.float32)
        for b in range(BANDS):
            member = band == b
            totals = jnp.sum(jnp.where(member, energy, 0.0), axis=-1, keepdims=True)
            present = jnp.sum(jnp.where(member, weight_factor, 0.0), axis=-1, keepdims=True)
            spread = jnp.where(member, totals / jnp.maximum(present, 1.0), spread)
        corrected = (weight_factor * (energy - spread)).astype(jnp.bfloat16)
        slot = table_ref[module]
        for q in range(quarters):
            out_ref[slot, q] = corrected[:, :, q * width : (q + 1) * width]


def calibrate_send(raw, pedestal, gain, good, bounds, table, n_peak):
    frame_dev, mods, row_dev, cols = raw.shape
    width = cols // n_peak
    group = 8
    grid_spec = pltpu.PrefetchScalarGridSpec(
        num_scalar_prefetch=2,
        grid=(mods // group,),
        in_specs=[
            pl.BlockSpec((frame_dev, group, row_dev, cols), lambda m, t, b: (0, m, 0, 0)),
            pl.BlockSpec((3, group, row_dev, cols), lambda m, t, b: (0, m, 0, 0)),
            pl.BlockSpec((3, group, row_dev, cols), lambda m, t, b: (0, m, 0, 0)),
            pl.BlockSpec((group, row_dev, cols), lambda m, t, b: (m, 0, 0)),
        ],
        out_specs=pl.BlockSpec(
            (mods, n_peak, frame_dev, row_dev, width), lambda m, t, b: (0, 0, 0, 0, 0)
        ),
    )
    return pl.pallas_call(
        lambda *refs: calibrate_kernel(group, *refs),
        grid_spec=grid_spec,
        out_shape=jax.ShapeDtypeStruct((mods, n_peak, frame_dev, row_dev, width), jnp.bfloat16),
    )(table, bounds.reshape(-1), raw, pedestal, gain, good)


def score_kernel(n_peak, levels, low_ref, mean_ref, rms_ref, frame_ref, cycle_ref, left_ref, right_ref, snr_ref, bent_ref):
    frame_pos = pl.program_id(0)
    cycle = cycle_ref[...]
    values = frame_ref[...].astype(jnp.float32)
    rows, cols = values.shape
    tops = mean_ref.shape[1] - 1
    pixel_mean = jnp.zeros((rows, cols), jnp.float32)
    pixel_rms = jnp.ones((rows, cols), jnp.float32)
    for j in range(levels):
        level = jnp.minimum(low_ref[0] + j, tops)
        hit = cycle == level
        pixel_mean = jnp.where(hit, mean_ref[frame_pos, level], pixel_mean)
        pixel_rms = jnp.where(hit, rms_ref[frame_pos, level], pixel_rms)
    score = (values - pixel_mean) / pixel_rms
    peak_pos = lax.axis_index("peak")
    row_ids = lax.broadcasted_iota(jnp.int32, (rows, cols), 0)
    col_ids = lax.broadcasted_iota(jnp.int32, (rows, cols), 1)
    left_col = jnp.where(peak_pos == 0, 0.0, left_ref[...])
    right_col = jnp.where(peak_pos == n_peak - 1, 0.0, right_ref[...])
    total = 4.0 * score
    for shift in (1, rows - 1):
        moved = pltpu.roll(score, shift, 0)
        source = pltpu.roll(row_ids, shift, 0)
        total = total - jnp.where(jnp.abs(source - row_ids) == 1, moved, 0.0)
    for shift in (1, cols - 1):
        moved = pltpu.roll(score, shift, 1)
        source = pltpu.roll(col_ids, shift, 1)
        near = jnp.where(source == cols - 1, left_col, right_col)
        total = total - jnp.where(jnp.abs(source - col_ids) == 1, moved, near)
    snr_ref[...] = score.astype(snr_ref.dtype)
    bent_ref[...] = total.astype(bent_ref.dtype)


def score_outputs(frame, cycle, cycle_average, cycle_rms, left, right, n_peak):
    frames, rows, cols = frame.shape
    span = (rows * rows + cols * cols) ** 0.5
    levels = min(CYCLES, int(span // CYCLE_W) + 3)
    low = jnp.min(cycle).reshape(1)
    block = pl.BlockSpec((None, rows, cols), lambda f, *_: (f, 0, 0))
    edge = pl.BlockSpec((None, rows, 1), lambda f, *_: (f, 0, 0))
    grid_spec = pltpu.PrefetchScalarGridSpec(
        num_scalar_prefetch=3,
        grid=(frames,),
        in_specs=[block, pl.BlockSpec((rows, cols), lambda f, *_: (0, 0)), edge, edge],
        out_specs=[block, block],
    )
    return pl.pallas_call(
        lambda *refs: score_kernel(n_peak, levels, *refs),
        grid_spec=grid_spec,
        out_shape=[jax.ShapeDtypeStruct(frame.shape, jnp.bfloat16)] * 2,
    )(low, cycle_average, cycle_rms, frame, cycle, left, right)


def laplace(padded):
    center = padded[..., 1:-1, 1:-1]
    return (
        4.0 * center
        - padded[..., :-2, 1:-1]
        - padded[..., 2:, 1:-1]
        - padded[..., 1:-1, :-2]
        - padded[..., 1:-1, 2:]
    )


def local_present(good, table, row_src, mrows, slot_rows):
    n_peak = lax.axis_size("peak")
    width = good.shape[2] // n_peak
    start = lax.axis_index("peak") * width
    part = lax.dynamic_slice_in_dim(good, start, width, axis=2)
    col = start + jnp.arange(width, dtype=jnp.int32)
    ypos = (table // SLOT_C)[:, None] * mrows + row_src[None, :]
    xpos = (table % SLOT_C)[:, None] * COLS + col[None, :]
    dy_two = 2 * ypos + 1 - slot_rows * mrows
    dx_two = 2 * xpos + 1 - SLOT_C * COLS
    dist = dy_two[:, :, None] * dy_two[:, :, None] + dx_two[:, None, :] * dx_two[:, None, :]
    cycle = cycle_index(dist)
    levels = jnp.arange(CYCLES, dtype=jnp.int32)
    hit = jnp.where(cycle[..., None] == levels, part[..., None], 0)
    return jnp.sum(hit, axis=(0, 1, 2)).astype(jnp.float32)


def gather_sum_kernel(stages, x_ref, o_ref, *scratch):
    count = len(stages)
    bufs = scratch[:count]
    partials = scratch[count : 2 * count]
    sems = scratch[2 * count :]
    me = (lax.axis_index("calib"), lax.axis_index("peak"))

    def peer(stage, step):
        axis, size, stride = stages[stage]
        pos = (me[axis] // stride) % size
        target = me[axis] + (lax.rem(pos + step, size) - pos) * stride
        return (target, me[1]) if axis == 0 else (me[0], target)

    def position(stage):
        axis, size, stride = stages[stage]
        return (me[axis] // stride) % size

    barrier = pltpu.get_barrier_semaphore()
    peers = 0
    for stage, (axis, size, stride) in enumerate(stages):
        peers += size - 1

        def greet(step, carry, stage=stage):
            pl.semaphore_signal(
                barrier, inc=1, device_id=peer(stage, step), device_id_type=pl.DeviceIdType.MESH
            )
            return carry

        lax.fori_loop(1, size, greet, 0)
    pl.semaphore_wait(barrier, peers)

    source = x_ref
    for stage, (axis, size, stride) in enumerate(stages):
        buf = bufs[stage]
        send_sem = sems[2 * stage]
        recv_sem = sems[2 * stage + 1]
        buf[size - 1] = source[...]

        def send(step, carry, stage=stage, buf=buf, send_sem=send_sem, recv_sem=recv_sem, source=source, size=size):
            pltpu.make_async_remote_copy(
                src_ref=source,
                dst_ref=buf.at[size - 1 - step],
                send_sem=send_sem,
                recv_sem=recv_sem,
                device_id=peer(stage, step),
                device_id_type=pl.DeviceIdType.MESH,
            ).start()
            return carry

        lax.fori_loop(1, size, send, 0)
        every = pltpu.make_async_remote_copy(
            src_ref=buf.at[pl.ds(0, size - 1)],
            dst_ref=buf.at[pl.ds(0, size - 1)],
            send_sem=send_sem,
            recv_sem=recv_sem,
            device_id=peer(stage, 1),
            device_id_type=pl.DeviceIdType.MESH,
        )
        every.wait_send()
        every.wait_recv()
        pos = position(stage)

        def add(origin, acc, buf=buf, pos=pos, size=size):
            return acc + buf[lax.rem(origin - pos - 1 + 2 * size, size)]

        total = lax.fori_loop(0, size, add, jnp.zeros(x_ref.shape, x_ref.dtype))
        if stage == count - 1:
            o_ref[...] = total
        else:
            partials[stage][...] = total
            source = partials[stage]


def gather_sum(x):
    n_calib = lax.axis_size("calib")
    n_peak = lax.axis_size("peak")
    stages = [(1, n_peak, 1)]
    stride = 1
    for size in (4, 4, 2):
        if n_calib % (stride * size) == 0 and stride * size <= n_calib:
            stages.append((0, size, stride))
            stride *= size
    if stride < n_calib:
        stages.append((0, n_calib // stride, stride))
    count = len(stages)
    scratch = [pltpu.VMEM((size,) + x.shape, x.dtype) for _, size, _ in stages]
    scratch += [pltpu.VMEM(x.shape, x.dtype) for _ in range(count)]
    scratch += [pltpu.SemaphoreType.DMA] * (2 * count)
    return pl.pallas_call(
        lambda *refs: gather_sum_kernel(stages, *refs),
        out_shape=jax.ShapeDtypeStruct(x.shape, x.dtype),
        in_specs=[pl.BlockSpec(memory_space=pltpu.VMEM)],
        out_specs=pl.BlockSpec(memory_space=pltpu.VMEM),
        scratch_shapes=scratch,
        compiler_params=pltpu.CompilerParams(collective_id=0, has_side_effects=True),
    )(x)


def cycle_stats(first, second, present_flag):
    cycle_average = first / present_flag[None, :]
    cycle_rms = jnp.sqrt(second / present_flag[None, :] + 1e-06)
    return (cycle_average, cycle_rms)


def body(raw, pedestal, gain, good, bounds, table):
    frame_dev, mods, row_dev, cols = raw.shape
    n_calib = lax.axis_size("calib")
    n_peak = lax.axis_size("peak")
    mrows = row_dev * n_calib
    slot_rows = mods // SLOT_C
    width_here = cols // n_peak
    frames_all = frame_dev * n_peak
    row_src = lax.axis_index("calib") * row_dev + jnp.arange(row_dev, dtype=jnp.int32)
    send = calibrate_send(raw, pedestal, gain, good, bounds, table, n_peak)
    send = send.reshape(mods * n_peak, frame_dev, row_dev, width_here)
    present_part = local_present(good, table, row_src, mrows, slot_rows)
    got = lax.all_to_all(send, ("calib", "peak"), 0, 0, tiled=True)
    got = got.reshape(n_calib, n_peak, frame_dev, row_dev, width_here)
    frame = jnp.transpose(got, (1, 2, 0, 3, 4)).reshape(frames_all, mrows, width_here)
    slot = lax.axis_index("calib")
    col_dst = lax.axis_index("peak") * width_here + jnp.arange(width_here, dtype=jnp.int32)
    ypos = slot // SLOT_C * mrows + jnp.arange(mrows, dtype=jnp.int32)
    xpos = slot % SLOT_C * COLS + col_dst
    dy_two = 2 * ypos + 1 - slot_rows * mrows
    dx_two = 2 * xpos + 1 - SLOT_C * COLS
    cycle = cycle_index(dy_two[:, None] * dy_two[:, None] + dx_two[None, :] * dx_two[None, :])
    levels = jnp.arange(CYCLES, dtype=jnp.int32)
    hits = (cycle.reshape(1, -1) == levels[:, None]).astype(jnp.bfloat16)
    pixels = frame.reshape(frames_all, -1)
    values = pixels.astype(jnp.float32)
    square = values * values
    square_top = lax.reduce_precision(square, exponent_bits=8, mantissa_bits=7)
    square_hi = square_top.astype(jnp.bfloat16)
    square_lo = (square - square_top).astype(jnp.bfloat16)
    stacked = jnp.concatenate([pixels, square_hi, square_lo], axis=0)
    sums = jnp.einsum("fp,kp->fk", stacked, hits, preferred_element_type=jnp.float32)
    first = sums[:frames_all]
    second = sums[frames_all : 2 * frames_all] + sums[2 * frames_all :]
    lanes = 128
    packed = jnp.concatenate(
        [
            first,
            second,
            jnp.zeros((frames_all, CYCLES), jnp.float32).at[0].set(present_part),
            jnp.zeros((frames_all, lanes - 3 * CYCLES), jnp.float32),
        ],
        axis=1,
    )
    summed = gather_sum(packed)
    first = summed[:, :CYCLES]
    second = summed[:, CYCLES : 2 * CYCLES]
    present_flag = summed[0, 2 * CYCLES : 3 * CYCLES]
    cycle_average, cycle_rms = cycle_stats(first, second, present_flag)
    edge_cycle = jnp.stack([cycle[:, width_here - 1], cycle[:, 0]], axis=1)
    edge_values = jnp.stack([frame[:, :, width_here - 1], frame[:, :, 0]], axis=2)
    edge_hits = (edge_cycle.reshape(1, -1) == levels[:, None]).astype(jnp.float32)
    edge_table = jnp.einsum(
        "fk,kp->fp",
        jnp.concatenate([cycle_average, cycle_rms], axis=0),
        edge_hits,
        precision=precise_variant,
    ).reshape(2 * frames_all, mrows, 2)
    edge_mean = edge_table[:frames_all]
    edge_rms = edge_table[frames_all:]
    edge_score = (edge_values.astype(jnp.float32) - edge_mean) / edge_rms
    fwd = [(i, i + 1) for i in range(n_peak - 1)]
    bwd = [(i + 1, i) for i in range(n_peak - 1)]
    left = lax.ppermute(edge_score[:, :, :1], "peak", fwd)
    right = lax.ppermute(edge_score[:, :, 1:], "peak", bwd)
    snr, bent = score_outputs(frame, cycle, cycle_average, cycle_rms, left, right, n_peak)
    return (snr[:, None], bent[:, None])


def solution(mesh):
    in_specs = (
        P("peak", None, "calib", None),
        P(None, None, "calib", None),
        P(None, None, "calib", None),
        P(None, "calib", None),
        P(),
        P(),
    )
    out_specs = (P(None, "calib", None, "peak"), P(None, "calib", None, "peak"))
    return jax.shard_map(body, mesh=mesh, in_specs=in_specs, out_specs=out_specs, check_vma=False)
```

```python
import jax
import jax.numpy as jnp
from jax import lax
from jax.sharding import PartitionSpec as P
from jax.experimental import pallas as pl
from jax.experimental.pallas import tpu as pltpu

COLS = 1024
BANDS = 8
SLOT_C = 4
CYCLES = 32
CYCLE_W = 64


precise_variant = lax.Precision.HIGHEST


def padded_2(block, sides, width):
    for axis, dim in sides:
        count = lax.axis_size(axis)
        forward = [(i, i + 1) for i in range(count - 1)]
        backward = [(target, source) for source, target in forward]
        low = lax.ppermute(
            lax.slice_in_dim(block, block.shape[dim] - width, None, axis=dim), axis, forward
        )
        high = lax.ppermute(lax.slice_in_dim(block, 0, width, axis=dim), axis, backward)
        block = jnp.concatenate([low, block, high], axis=dim)
    return block


def cycle_index(dist):
    levels = jnp.arange(1, CYCLES, dtype=jnp.int32)
    lows = (2 * CYCLE_W * levels) ** 2
    return jnp.sum((dist[..., None] >= lows).astype(jnp.int32), axis=-1)


def cycle_onehot(slot, row_pos, col_pos, mrows, slot_rows):
    ypos = slot // SLOT_C * mrows + row_pos
    xpos = slot % SLOT_C * COLS + col_pos
    dy_two = 2 * ypos + 1 - slot_rows * mrows
    dx_two = 2 * xpos + 1 - SLOT_C * COLS
    dist = dy_two[:, None] * dy_two[:, None] + dx_two[None, :] * dx_two[None, :]
    levels = jnp.arange(CYCLES, dtype=jnp.int32)
    lows = (2 * CYCLE_W * levels) ** 2
    cycle = jnp.sum((dist[None] >= lows[:, None, None]).astype(jnp.int32), axis=0) - 1
    hits = (cycle[None] == levels[:, None, None]).astype(jnp.float32)
    return hits.reshape(CYCLES, -1)


def calibrate(raw, pedestal, gain, good, bounds):
    code = raw // 2048
    counts_adc = (raw % 2048).astype(jnp.float32)
    base = jnp.where(code == 0, pedestal[0], jnp.where(code == 1, pedestal[1], pedestal[2]))
    gain_factor = gain.astype(jnp.float32)
    scale = jnp.where(
        code == 0, gain_factor[0], jnp.where(code == 1, gain_factor[1], gain_factor[2])
    )
    weight_factor = good.astype(jnp.float32)
    energy = weight_factor * (counts_adc - base) / scale
    columns = jnp.arange(raw.shape[-1], dtype=jnp.int32)
    band = jnp.sum((columns[None, :, None] >= bounds[:, None, :]).astype(jnp.int32), axis=2)
    member_entry = (band[:, :, None] == jnp.arange(BANDS, dtype=jnp.int32)[None, None, :]).astype(
        jnp.float32
    )
    totals = jnp.einsum("fmrc,mcb->fmrb", energy, member_entry, precision=precise_variant)
    present_flag = jnp.einsum(
        "tlg,tgd->tld", weight_factor, member_entry, precision=precise_variant
    )
    level = totals / jnp.maximum(present_flag, 1.0)
    spread = jnp.einsum("fmrb,mcb->fmrc", level, member_entry, precision=precise_variant)
    return (weight_factor * (energy - spread)).astype(jnp.bfloat16)


def calibrate_kernel(group, table_ref, bounds_ref, raw_ref, ped_ref, gain_ref, good_ref, out_ref):
    step = pl.program_id(0)
    cols = raw_ref.shape[-1]
    columns = lax.broadcasted_iota(jnp.int32, (1, cols), 1)
    quarters = out_ref.shape[1]
    width = cols // quarters
    for inner in range(group):
        module = step * group + inner
        raw = raw_ref[:, inner]
        code = raw // 2048
        counts_adc = (raw % 2048).astype(jnp.float32)
        base = jnp.where(
            code == 0, ped_ref[0, inner], jnp.where(code == 1, ped_ref[1, inner], ped_ref[2, inner])
        )
        scale = jnp.where(
            code == 0,
            gain_ref[0, inner].astype(jnp.float32),
            jnp.where(
                code == 1,
                gain_ref[1, inner].astype(jnp.float32),
                gain_ref[2, inner].astype(jnp.float32),
            ),
        )
        weight_factor = good_ref[inner].astype(jnp.float32)
        energy = weight_factor * (counts_adc - base) / scale
        band = jnp.zeros((1, cols), jnp.int32)
        for j in range(BANDS - 1):
            band = band + (columns >= bounds_ref[module * (BANDS - 1) + j]).astype(jnp.int32)
        spread = jnp.zeros(energy.shape, jnp.float32)
        for b in range(BANDS):
            member = band == b
            totals = jnp.sum(jnp.where(member, energy, 0.0), axis=-1, keepdims=True)
            present = jnp.sum(jnp.where(member, weight_factor, 0.0), axis=-1, keepdims=True)
            spread = jnp.where(member, totals / jnp.maximum(present, 1.0), spread)
        corrected = (weight_factor * (energy - spread)).astype(jnp.bfloat16)
        slot = table_ref[module]
        for q in range(quarters):
            out_ref[slot, q] = corrected[:, :, q * width : (q + 1) * width]


def calibrate_send(raw, pedestal, gain, good, bounds, table, n_peak):
    frame_dev, mods, row_dev, cols = raw.shape
    width = cols // n_peak
    group = 8
    grid_spec = pltpu.PrefetchScalarGridSpec(
        num_scalar_prefetch=2,
        grid=(mods // group,),
        in_specs=[
            pl.BlockSpec((frame_dev, group, row_dev, cols), lambda m, t, b: (0, m, 0, 0)),
            pl.BlockSpec((3, group, row_dev, cols), lambda m, t, b: (0, m, 0, 0)),
            pl.BlockSpec((3, group, row_dev, cols), lambda m, t, b: (0, m, 0, 0)),
            pl.BlockSpec((group, row_dev, cols), lambda m, t, b: (m, 0, 0)),
        ],
        out_specs=pl.BlockSpec(
            (mods, n_peak, frame_dev, row_dev, width), lambda m, t, b: (0, 0, 0, 0, 0)
        ),
    )
    return pl.pallas_call(
        lambda *refs: calibrate_kernel(group, *refs),
        grid_spec=grid_spec,
        out_shape=jax.ShapeDtypeStruct((mods, n_peak, frame_dev, row_dev, width), jnp.bfloat16),
    )(table, bounds.reshape(-1), raw, pedestal, gain, good)


def score_kernel(n_peak, levels, per, low_ref, mean_ref, rms_ref, frame_ref, cycle_ref, left_ref, right_ref, snr_ref, bent_ref):
    cycle = cycle_ref[...]
    rows, cols = cycle.shape
    tops = mean_ref.shape[1] - 1
    peak_pos = lax.axis_index("peak")
    row_ids = lax.broadcasted_iota(jnp.int32, (rows, cols), 0)
    col_ids = lax.broadcasted_iota(jnp.int32, (rows, cols), 1)
    row_shifts = []
    for shift in (1, rows - 1):
        source = pltpu.roll(row_ids, shift, 0)
        row_shifts.append((shift, jnp.abs(source - row_ids) == 1))
    col_shifts = []
    for shift in (1, cols - 1):
        source = pltpu.roll(col_ids, shift, 1)
        col_shifts.append((shift, jnp.abs(source - col_ids) == 1, source == cols - 1))
    hits = []
    for j in range(levels):
        level = jnp.minimum(low_ref[0] + j, tops)
        hits.append((level, cycle == level))
    for inner in range(per):
        frame_pos = pl.program_id(0) * per + inner
        values = frame_ref[inner].astype(jnp.float32)
        pixel_mean = jnp.zeros((rows, cols), jnp.float32)
        pixel_rms = jnp.ones((rows, cols), jnp.float32)
        for level, hit in hits:
            pixel_mean = jnp.where(hit, mean_ref[frame_pos, level], pixel_mean)
            pixel_rms = jnp.where(hit, rms_ref[frame_pos, level], pixel_rms)
        score = (values - pixel_mean) / pixel_rms
        left_col = jnp.where(peak_pos == 0, 0.0, left_ref[inner])
        right_col = jnp.where(peak_pos == n_peak - 1, 0.0, right_ref[inner])
        total = 4.0 * score
        for shift, inside in row_shifts:
            total = total - jnp.where(inside, pltpu.roll(score, shift, 0), 0.0)
        for shift, inside, wrapped_left in col_shifts:
            near = jnp.where(wrapped_left, left_col, right_col)
            total = total - jnp.where(inside, pltpu.roll(score, shift, 1), near)
        snr_ref[inner] = score.astype(snr_ref.dtype)
        bent_ref[inner] = total.astype(bent_ref.dtype)


def score_outputs(frame, cycle, cycle_average, cycle_rms, left, right, n_peak):
    frames, rows, cols = frame.shape
    span = (rows * rows + cols * cols) ** 0.5
    levels = min(CYCLES, int(span // CYCLE_W) + 2)
    per = 2 if frames % 2 == 0 else 1
    low = jnp.min(cycle).reshape(1)
    block = pl.BlockSpec((per, rows, cols), lambda f, *_: (f, 0, 0))
    edge = pl.BlockSpec((per, rows, 1), lambda f, *_: (f, 0, 0))
    grid_spec = pltpu.PrefetchScalarGridSpec(
        num_scalar_prefetch=3,
        grid=(frames // per,),
        in_specs=[block, pl.BlockSpec((rows, cols), lambda f, *_: (0, 0)), edge, edge],
        out_specs=[block, block],
    )
    return pl.pallas_call(
        lambda *refs: score_kernel(n_peak, levels, per, *refs),
        grid_spec=grid_spec,
        out_shape=[jax.ShapeDtypeStruct(frame.shape, jnp.bfloat16)] * 2,
    )(low, cycle_average, cycle_rms, frame, cycle, left, right)


def laplace(padded):
    center = padded[..., 1:-1, 1:-1]
    return (
        4.0 * center
        - padded[..., :-2, 1:-1]
        - padded[..., 2:, 1:-1]
        - padded[..., 1:-1, :-2]
        - padded[..., 1:-1, 2:]
    )


def local_present(good, table, row_src, mrows, slot_rows):
    n_peak = lax.axis_size("peak")
    width = good.shape[2] // n_peak
    start = lax.axis_index("peak") * width
    part = lax.dynamic_slice_in_dim(good, start, width, axis=2)
    col = start + jnp.arange(width, dtype=jnp.int32)
    ypos = (table // SLOT_C)[:, None] * mrows + row_src[None, :]
    xpos = (table % SLOT_C)[:, None] * COLS + col[None, :]
    dy_two = 2 * ypos + 1 - slot_rows * mrows
    dx_two = 2 * xpos + 1 - SLOT_C * COLS
    dist = dy_two[:, :, None] * dy_two[:, :, None] + dx_two[:, None, :] * dx_two[:, None, :]
    cycle = cycle_index(dist)
    levels = jnp.arange(CYCLES, dtype=jnp.int32)
    hit = jnp.where(cycle[..., None] == levels, part[..., None], 0)
    return jnp.sum(hit, axis=(0, 1, 2)).astype(jnp.float32)


def gather_sum_kernel(
    n_calib, n_peak, x_ref, o_ref, near, far, partial, near_send, near_recv, far_send, far_recv
):
    my_calib = lax.axis_index("calib")
    my_peak = lax.axis_index("peak")
    near[n_peak - 1] = x_ref[...]
    barrier = pltpu.get_barrier_semaphore()

    def peak_peer(step):
        return (my_calib, lax.rem(my_peak + step, n_peak))

    def calib_peer(step):
        return (lax.rem(my_calib + step, n_calib), my_peak)

    def greet_peak(step, carry):
        pl.semaphore_signal(
            barrier, inc=1, device_id=peak_peer(step), device_id_type=pl.DeviceIdType.MESH
        )
        return carry

    def greet_calib(step, carry):
        pl.semaphore_signal(
            barrier, inc=1, device_id=calib_peer(step), device_id_type=pl.DeviceIdType.MESH
        )
        return carry

    lax.fori_loop(1, n_peak, greet_peak, 0)
    lax.fori_loop(1, n_calib, greet_calib, 0)
    pl.semaphore_wait(barrier, n_peak - 1 + n_calib - 1)

    def send_near(step, carry):
        pltpu.make_async_remote_copy(
            src_ref=x_ref,
            dst_ref=near.at[n_peak - 1 - step],
            send_sem=near_send,
            recv_sem=near_recv,
            device_id=peak_peer(step),
            device_id_type=pl.DeviceIdType.MESH,
        ).start()
        return carry

    lax.fori_loop(1, n_peak, send_near, 0)
    every_near = pltpu.make_async_remote_copy(
        src_ref=near.at[pl.ds(0, n_peak - 1)],
        dst_ref=near.at[pl.ds(0, n_peak - 1)],
        send_sem=near_send,
        recv_sem=near_recv,
        device_id=peak_peer(1),
        device_id_type=pl.DeviceIdType.MESH,
    )
    every_near.wait_send()
    every_near.wait_recv()

    def add_near(source, acc):
        return acc + near[lax.rem(source - my_peak - 1 + 2 * n_peak, n_peak)]

    partial[...] = lax.fori_loop(0, n_peak, add_near, jnp.zeros(x_ref.shape, x_ref.dtype))
    far[n_calib - 1] = partial[...]

    def send_far(step, carry):
        pltpu.make_async_remote_copy(
            src_ref=partial,
            dst_ref=far.at[n_calib - 1 - step],
            send_sem=far_send,
            recv_sem=far_recv,
            device_id=calib_peer(step),
            device_id_type=pl.DeviceIdType.MESH,
        ).start()
        return carry

    lax.fori_loop(1, n_calib, send_far, 0)
    every_far = pltpu.make_async_remote_copy(
        src_ref=far.at[pl.ds(0, n_calib - 1)],
        dst_ref=far.at[pl.ds(0, n_calib - 1)],
        send_sem=far_send,
        recv_sem=far_recv,
        device_id=calib_peer(1),
        device_id_type=pl.DeviceIdType.MESH,
    )
    every_far.wait_send()
    every_far.wait_recv()

    def add_far(source, acc):
        return acc + far[lax.rem(source - my_calib - 1 + 2 * n_calib, n_calib)]

    o_ref[...] = lax.fori_loop(0, n_calib, add_far, jnp.zeros(x_ref.shape, x_ref.dtype))


def gather_sum(x):
    n_calib = lax.axis_size("calib")
    n_peak = lax.axis_size("peak")
    return pl.pallas_call(
        lambda *refs: gather_sum_kernel(n_calib, n_peak, *refs),
        out_shape=jax.ShapeDtypeStruct(x.shape, x.dtype),
        in_specs=[pl.BlockSpec(memory_space=pltpu.VMEM)],
        out_specs=pl.BlockSpec(memory_space=pltpu.VMEM),
        scratch_shapes=[
            pltpu.VMEM((n_peak,) + x.shape, x.dtype),
            pltpu.VMEM((n_calib,) + x.shape, x.dtype),
            pltpu.VMEM(x.shape, x.dtype),
            pltpu.SemaphoreType.DMA,
            pltpu.SemaphoreType.DMA,
            pltpu.SemaphoreType.DMA,
            pltpu.SemaphoreType.DMA,
        ],
        compiler_params=pltpu.CompilerParams(collective_id=0, has_side_effects=True),
    )(x)


def cycle_stats(first, second, present_flag):
    cycle_average = first / present_flag[None, :]
    cycle_rms = jnp.sqrt(second / present_flag[None, :] + 1e-06)
    return (cycle_average, cycle_rms)


def body(raw, pedestal, gain, good, bounds, table):
    frame_dev, mods, row_dev, cols = raw.shape
    n_calib = lax.axis_size("calib")
    n_peak = lax.axis_size("peak")
    mrows = row_dev * n_calib
    slot_rows = mods // SLOT_C
    width_here = cols // n_peak
    frames_all = frame_dev * n_peak
    row_src = lax.axis_index("calib") * row_dev + jnp.arange(row_dev, dtype=jnp.int32)
    send = calibrate_send(raw, pedestal, gain, good, bounds, table, n_peak)
    send = send.reshape(mods * n_peak, frame_dev, row_dev, width_here)
    present_part = local_present(good, table, row_src, mrows, slot_rows)
    got = lax.all_to_all(send, ("calib", "peak"), 0, 0, tiled=True)
    got = got.reshape(n_calib, n_peak, frame_dev, row_dev, width_here)
    frame = jnp.transpose(got, (1, 2, 0, 3, 4)).reshape(frames_all, mrows, width_here)
    slot = lax.axis_index("calib")
    col_dst = lax.axis_index("peak") * width_here + jnp.arange(width_here, dtype=jnp.int32)
    ypos = slot // SLOT_C * mrows + jnp.arange(mrows, dtype=jnp.int32)
    xpos = slot % SLOT_C * COLS + col_dst
    dy_two = 2 * ypos + 1 - slot_rows * mrows
    dx_two = 2 * xpos + 1 - SLOT_C * COLS
    cycle = cycle_index(dy_two[:, None] * dy_two[:, None] + dx_two[None, :] * dx_two[None, :])
    levels = jnp.arange(CYCLES, dtype=jnp.int32)
    hits = (cycle.reshape(1, -1) == levels[:, None]).astype(jnp.bfloat16)
    pixels = frame.reshape(frames_all, -1)
    values = pixels.astype(jnp.float32)
    square = values * values
    square_top = lax.reduce_precision(square, exponent_bits=8, mantissa_bits=7)
    square_hi = square_top.astype(jnp.bfloat16)
    square_lo = (square - square_top).astype(jnp.bfloat16)
    stacked = jnp.concatenate([pixels, square_hi, square_lo], axis=0)
    sums = jnp.einsum("fp,kp->fk", stacked, hits, preferred_element_type=jnp.float32)
    first = sums[:frames_all]
    second = sums[frames_all : 2 * frames_all] + sums[2 * frames_all :]
    lanes = 128
    packed = jnp.concatenate(
        [
            first,
            second,
            jnp.zeros((frames_all, CYCLES), jnp.float32).at[0].set(present_part),
            jnp.zeros((frames_all, lanes - 3 * CYCLES), jnp.float32),
        ],
        axis=1,
    )
    summed = gather_sum(packed)
    first = summed[:, :CYCLES]
    second = summed[:, CYCLES : 2 * CYCLES]
    present_flag = summed[0, 2 * CYCLES : 3 * CYCLES]
    cycle_average, cycle_rms = cycle_stats(first, second, present_flag)
    edge_cycle = jnp.stack([cycle[:, width_here - 1], cycle[:, 0]], axis=1)
    edge_values = jnp.stack([frame[:, :, width_here - 1], frame[:, :, 0]], axis=2)
    edge_hits = (edge_cycle.reshape(1, -1) == levels[:, None]).astype(jnp.float32)
    edge_table = jnp.einsum(
        "fk,kp->fp",
        jnp.concatenate([cycle_average, cycle_rms], axis=0),
        edge_hits,
        precision=precise_variant,
    ).reshape(2 * frames_all, mrows, 2)
    edge_mean = edge_table[:frames_all]
    edge_rms = edge_table[frames_all:]
    edge_score = (edge_values.astype(jnp.float32) - edge_mean) / edge_rms
    fwd = [(i, i + 1) for i in range(n_peak - 1)]
    bwd = [(i + 1, i) for i in range(n_peak - 1)]
    left = lax.ppermute(edge_score[:, :, :1], "peak", fwd)
    right = lax.ppermute(edge_score[:, :, 1:], "peak", bwd)
    snr, bent = score_outputs(frame, cycle, cycle_average, cycle_rms, left, right, n_peak)
    return (snr[:, None], bent[:, None])


def solution(mesh):
    in_specs = (
        P("peak", None, "calib", None),
        P(None, None, "calib", None),
        P(None, None, "calib", None),
        P(None, "calib", None),
        P(),
        P(),
    )
    out_specs = (P(None, "calib", None, "peak"), P(None, "calib", None, "peak"))
    return jax.shard_map(body, mesh=mesh, in_specs=in_specs, out_specs=out_specs, check_vma=False)
```

```python
import jax
import jax.numpy as jnp
from jax import lax
from jax.sharding import PartitionSpec as P
from jax.experimental import pallas as pl
from jax.experimental.pallas import tpu as pltpu

COLS = 1024
BANDS = 8
SLOT_C = 4
CYCLES = 32
CYCLE_W = 64


precise_variant = lax.Precision.HIGHEST


def padded_2(block, sides, width):
    for axis, dim in sides:
        count = lax.axis_size(axis)
        forward = [(i, i + 1) for i in range(count - 1)]
        backward = [(target, source) for source, target in forward]
        low = lax.ppermute(
            lax.slice_in_dim(block, block.shape[dim] - width, None, axis=dim), axis, forward
        )
        high = lax.ppermute(lax.slice_in_dim(block, 0, width, axis=dim), axis, backward)
        block = jnp.concatenate([low, block, high], axis=dim)
    return block


def cycle_index(dist):
    levels = jnp.arange(1, CYCLES, dtype=jnp.int32)
    lows = (2 * CYCLE_W * levels) ** 2
    return jnp.sum((dist[..., None] >= lows).astype(jnp.int32), axis=-1)


def cycle_onehot(slot, row_pos, col_pos, mrows, slot_rows):
    ypos = slot // SLOT_C * mrows + row_pos
    xpos = slot % SLOT_C * COLS + col_pos
    dy_two = 2 * ypos + 1 - slot_rows * mrows
    dx_two = 2 * xpos + 1 - SLOT_C * COLS
    dist = dy_two[:, None] * dy_two[:, None] + dx_two[None, :] * dx_two[None, :]
    levels = jnp.arange(CYCLES, dtype=jnp.int32)
    lows = (2 * CYCLE_W * levels) ** 2
    cycle = jnp.sum((dist[None] >= lows[:, None, None]).astype(jnp.int32), axis=0) - 1
    hits = (cycle[None] == levels[:, None, None]).astype(jnp.float32)
    return hits.reshape(CYCLES, -1)


def calibrate(raw, pedestal, gain, good, bounds):
    code = raw // 2048
    counts_adc = (raw % 2048).astype(jnp.float32)
    base = jnp.where(code == 0, pedestal[0], jnp.where(code == 1, pedestal[1], pedestal[2]))
    gain_factor = gain.astype(jnp.float32)
    scale = jnp.where(
        code == 0, gain_factor[0], jnp.where(code == 1, gain_factor[1], gain_factor[2])
    )
    weight_factor = good.astype(jnp.float32)
    energy = weight_factor * (counts_adc - base) / scale
    columns = jnp.arange(raw.shape[-1], dtype=jnp.int32)
    band = jnp.sum((columns[None, :, None] >= bounds[:, None, :]).astype(jnp.int32), axis=2)
    member_entry = (band[:, :, None] == jnp.arange(BANDS, dtype=jnp.int32)[None, None, :]).astype(
        jnp.float32
    )
    totals = jnp.einsum("fmrc,mcb->fmrb", energy, member_entry, precision=precise_variant)
    present_flag = jnp.einsum(
        "tlg,tgd->tld", weight_factor, member_entry, precision=precise_variant
    )
    level = totals / jnp.maximum(present_flag, 1.0)
    spread = jnp.einsum("fmrb,mcb->fmrc", level, member_entry, precision=precise_variant)
    return (weight_factor * (energy - spread)).astype(jnp.bfloat16)


def calibrate_kernel(group, table_ref, bounds_ref, raw_ref, ped_ref, gain_ref, good_ref, out_ref):
    step = pl.program_id(0)
    cols = raw_ref.shape[-1]
    columns = lax.broadcasted_iota(jnp.int32, (1, cols), 1)
    quarters = out_ref.shape[1]
    width = cols // quarters
    for inner in range(group):
        module = step * group + inner
        raw = raw_ref[:, inner]
        code = lax.shift_right_logical(raw, 11)
        counts_adc = (raw & 2047).astype(jnp.float32)
        base = jnp.where(
            code == 0, ped_ref[0, inner], jnp.where(code == 1, ped_ref[1, inner], ped_ref[2, inner])
        )
        scale = jnp.where(
            code == 0,
            gain_ref[0, inner].astype(jnp.float32),
            jnp.where(
                code == 1,
                gain_ref[1, inner].astype(jnp.float32),
                gain_ref[2, inner].astype(jnp.float32),
            ),
        )
        weight_factor = good_ref[inner].astype(jnp.float32)
        energy = weight_factor * (counts_adc - base) / scale
        band = jnp.zeros((1, cols), jnp.int32)
        for j in range(BANDS - 1):
            band = band + (columns >= bounds_ref[module * (BANDS - 1) + j]).astype(jnp.int32)
        spread = jnp.zeros(energy.shape, jnp.float32)
        for b in range(BANDS):
            member = band == b
            totals = jnp.sum(jnp.where(member, energy, 0.0), axis=-1, keepdims=True)
            present = jnp.sum(jnp.where(member, weight_factor, 0.0), axis=-1, keepdims=True)
            spread = jnp.where(member, totals / jnp.maximum(present, 1.0), spread)
        corrected = (weight_factor * (energy - spread)).astype(jnp.bfloat16)
        slot = table_ref[module]
        for q in range(quarters):
            out_ref[slot, q] = corrected[:, :, q * width : (q + 1) * width]


def calibrate_send(raw, pedestal, gain, good, bounds, table, n_peak):
    frame_dev, mods, row_dev, cols = raw.shape
    width = cols // n_peak
    group = 8
    grid_spec = pltpu.PrefetchScalarGridSpec(
        num_scalar_prefetch=2,
        grid=(mods // group,),
        in_specs=[
            pl.BlockSpec((frame_dev, group, row_dev, cols), lambda m, t, b: (0, m, 0, 0)),
            pl.BlockSpec((3, group, row_dev, cols), lambda m, t, b: (0, m, 0, 0)),
            pl.BlockSpec((3, group, row_dev, cols), lambda m, t, b: (0, m, 0, 0)),
            pl.BlockSpec((group, row_dev, cols), lambda m, t, b: (m, 0, 0)),
        ],
        out_specs=pl.BlockSpec(
            (mods, n_peak, frame_dev, row_dev, width), lambda m, t, b: (0, 0, 0, 0, 0)
        ),
    )
    return pl.pallas_call(
        lambda *refs: calibrate_kernel(group, *refs),
        grid_spec=grid_spec,
        out_shape=jax.ShapeDtypeStruct((mods, n_peak, frame_dev, row_dev, width), jnp.bfloat16),
    )(table, bounds.reshape(-1), raw, pedestal, gain, good)


def score_kernel(n_peak, levels, per, low_ref, mean_ref, rms_ref, frame_ref, cycle_ref, left_ref, right_ref, snr_ref, bent_ref):
    cycle = cycle_ref[...]
    rows, cols = cycle.shape
    tops = mean_ref.shape[1] - 1
    peak_pos = lax.axis_index("peak")
    row_ids = lax.broadcasted_iota(jnp.int32, (rows, cols), 0)
    col_ids = lax.broadcasted_iota(jnp.int32, (rows, cols), 1)
    row_shifts = []
    for shift in (1, rows - 1):
        source = pltpu.roll(row_ids, shift, 0)
        row_shifts.append((shift, jnp.abs(source - row_ids) == 1))
    col_shifts = []
    for shift in (1, cols - 1):
        source = pltpu.roll(col_ids, shift, 1)
        col_shifts.append((shift, jnp.abs(source - col_ids) == 1, source == cols - 1))
    hits = []
    for j in range(levels):
        level = jnp.minimum(low_ref[0] + j, tops)
        hits.append((level, cycle == level))
    for inner in range(per):
        frame_pos = pl.program_id(0) * per + inner
        values = frame_ref[inner].astype(jnp.float32)
        pixel_mean = jnp.zeros((rows, cols), jnp.float32)
        pixel_rms = jnp.ones((rows, cols), jnp.float32)
        for level, hit in hits:
            pixel_mean = jnp.where(hit, mean_ref[frame_pos, level], pixel_mean)
            pixel_rms = jnp.where(hit, rms_ref[frame_pos, level], pixel_rms)
        score = (values - pixel_mean) / pixel_rms
        left_col = jnp.where(peak_pos == 0, 0.0, left_ref[inner])
        right_col = jnp.where(peak_pos == n_peak - 1, 0.0, right_ref[inner])
        total = 4.0 * score
        for shift, inside in row_shifts:
            total = total - jnp.where(inside, pltpu.roll(score, shift, 0), 0.0)
        for shift, inside, wrapped_left in col_shifts:
            near = jnp.where(wrapped_left, left_col, right_col)
            total = total - jnp.where(inside, pltpu.roll(score, shift, 1), near)
        snr_ref[inner] = score.astype(snr_ref.dtype)
        bent_ref[inner] = total.astype(bent_ref.dtype)


def score_outputs(frame, cycle, cycle_average, cycle_rms, left, right, n_peak):
    frames, rows, cols = frame.shape
    span = (rows * rows + cols * cols) ** 0.5
    levels = min(CYCLES, int(span // CYCLE_W) + 2)
    per = 2 if frames % 2 == 0 else 1
    low = jnp.min(cycle).reshape(1)
    block = pl.BlockSpec((per, rows, cols), lambda f, *_: (f, 0, 0))
    edge = pl.BlockSpec((per, rows, 1), lambda f, *_: (f, 0, 0))
    grid_spec = pltpu.PrefetchScalarGridSpec(
        num_scalar_prefetch=3,
        grid=(frames // per,),
        in_specs=[block, pl.BlockSpec((rows, cols), lambda f, *_: (0, 0)), edge, edge],
        out_specs=[block, block],
    )
    return pl.pallas_call(
        lambda *refs: score_kernel(n_peak, levels, per, *refs),
        grid_spec=grid_spec,
        out_shape=[jax.ShapeDtypeStruct(frame.shape, jnp.bfloat16)] * 2,
    )(low, cycle_average, cycle_rms, frame, cycle, left, right)


def laplace(padded):
    center = padded[..., 1:-1, 1:-1]
    return (
        4.0 * center
        - padded[..., :-2, 1:-1]
        - padded[..., 2:, 1:-1]
        - padded[..., 1:-1, :-2]
        - padded[..., 1:-1, 2:]
    )


def local_present(good, table, row_src, mrows, slot_rows):
    n_peak = lax.axis_size("peak")
    width = good.shape[2] // n_peak
    start = lax.axis_index("peak") * width
    part = lax.dynamic_slice_in_dim(good, start, width, axis=2)
    col = start + jnp.arange(width, dtype=jnp.int32)
    ypos = (table // SLOT_C)[:, None] * mrows + row_src[None, :]
    xpos = (table % SLOT_C)[:, None] * COLS + col[None, :]
    dy_two = 2 * ypos + 1 - slot_rows * mrows
    dx_two = 2 * xpos + 1 - SLOT_C * COLS
    dist = dy_two[:, :, None] * dy_two[:, :, None] + dx_two[:, None, :] * dx_two[:, None, :]
    cycle = cycle_index(dist)
    levels = jnp.arange(CYCLES, dtype=jnp.int32)
    hit = jnp.where(cycle[..., None] == levels, part[..., None], 0)
    return jnp.sum(hit, axis=(0, 1, 2)).astype(jnp.float32)


def gather_sum_kernel(
    n_calib, n_peak, x_ref, o_ref, near, far, partial, near_send, near_recv, far_send, far_recv
):
    my_calib = lax.axis_index("calib")
    my_peak = lax.axis_index("peak")
    near[n_peak - 1] = x_ref[...]
    barrier = pltpu.get_barrier_semaphore()

    def peak_peer(step):
        return (my_calib, lax.rem(my_peak + step, n_peak))

    def calib_peer(step):
        return (lax.rem(my_calib + step, n_calib), my_peak)

    def greet_peak(step, carry):
        pl.semaphore_signal(
            barrier, inc=1, device_id=peak_peer(step), device_id_type=pl.DeviceIdType.MESH
        )
        return carry

    def greet_calib(step, carry):
        pl.semaphore_signal(
            barrier, inc=1, device_id=calib_peer(step), device_id_type=pl.DeviceIdType.MESH
        )
        return carry

    lax.fori_loop(1, n_peak, greet_peak, 0)
    lax.fori_loop(1, n_calib, greet_calib, 0)
    pl.semaphore_wait(barrier, n_peak - 1 + n_calib - 1)

    def send_near(step, carry):
        pltpu.make_async_remote_copy(
            src_ref=x_ref,
            dst_ref=near.at[n_peak - 1 - step],
            send_sem=near_send,
            recv_sem=near_recv,
            device_id=peak_peer(step),
            device_id_type=pl.DeviceIdType.MESH,
        ).start()
        return carry

    lax.fori_loop(1, n_peak, send_near, 0)
    every_near = pltpu.make_async_remote_copy(
        src_ref=near.at[pl.ds(0, n_peak - 1)],
        dst_ref=near.at[pl.ds(0, n_peak - 1)],
        send_sem=near_send,
        recv_sem=near_recv,
        device_id=peak_peer(1),
        device_id_type=pl.DeviceIdType.MESH,
    )
    every_near.wait_send()
    every_near.wait_recv()

    def add_near(source, acc):
        return acc + near[lax.rem(source - my_peak - 1 + 2 * n_peak, n_peak)]

    partial[...] = lax.fori_loop(0, n_peak, add_near, jnp.zeros(x_ref.shape, x_ref.dtype))
    far[n_calib - 1] = partial[...]

    def send_far(step, carry):
        pltpu.make_async_remote_copy(
            src_ref=partial,
            dst_ref=far.at[n_calib - 1 - step],
            send_sem=far_send,
            recv_sem=far_recv,
            device_id=calib_peer(step),
            device_id_type=pl.DeviceIdType.MESH,
        ).start()
        return carry

    lax.fori_loop(1, n_calib, send_far, 0)
    every_far = pltpu.make_async_remote_copy(
        src_ref=far.at[pl.ds(0, n_calib - 1)],
        dst_ref=far.at[pl.ds(0, n_calib - 1)],
        send_sem=far_send,
        recv_sem=far_recv,
        device_id=calib_peer(1),
        device_id_type=pl.DeviceIdType.MESH,
    )
    every_far.wait_send()
    every_far.wait_recv()

    def add_far(source, acc):
        return acc + far[lax.rem(source - my_calib - 1 + 2 * n_calib, n_calib)]

    o_ref[...] = lax.fori_loop(0, n_calib, add_far, jnp.zeros(x_ref.shape, x_ref.dtype))


def gather_sum(x):
    n_calib = lax.axis_size("calib")
    n_peak = lax.axis_size("peak")
    return pl.pallas_call(
        lambda *refs: gather_sum_kernel(n_calib, n_peak, *refs),
        out_shape=jax.ShapeDtypeStruct(x.shape, x.dtype),
        in_specs=[pl.BlockSpec(memory_space=pltpu.VMEM)],
        out_specs=pl.BlockSpec(memory_space=pltpu.VMEM),
        scratch_shapes=[
            pltpu.VMEM((n_peak,) + x.shape, x.dtype),
            pltpu.VMEM((n_calib,) + x.shape, x.dtype),
            pltpu.VMEM(x.shape, x.dtype),
            pltpu.SemaphoreType.DMA,
            pltpu.SemaphoreType.DMA,
            pltpu.SemaphoreType.DMA,
            pltpu.SemaphoreType.DMA,
        ],
        compiler_params=pltpu.CompilerParams(collective_id=0, has_side_effects=True),
    )(x)


def cycle_stats(first, second, present_flag):
    cycle_average = first / present_flag[None, :]
    cycle_rms = jnp.sqrt(second / present_flag[None, :] + 1e-06)
    return (cycle_average, cycle_rms)


def body(raw, pedestal, gain, good, bounds, table):
    frame_dev, mods, row_dev, cols = raw.shape
    n_calib = lax.axis_size("calib")
    n_peak = lax.axis_size("peak")
    mrows = row_dev * n_calib
    slot_rows = mods // SLOT_C
    width_here = cols // n_peak
    frames_all = frame_dev * n_peak
    row_src = lax.axis_index("calib") * row_dev + jnp.arange(row_dev, dtype=jnp.int32)
    send = calibrate_send(raw, pedestal, gain, good, bounds, table, n_peak)
    send = send.reshape(mods * n_peak, frame_dev, row_dev, width_here)
    present_part = local_present(good, table, row_src, mrows, slot_rows)
    got = lax.all_to_all(send, ("calib", "peak"), 0, 0, tiled=True)
    got = got.reshape(n_calib, n_peak, frame_dev, row_dev, width_here)
    frame = jnp.transpose(got, (1, 2, 0, 3, 4)).reshape(frames_all, mrows, width_here)
    slot = lax.axis_index("calib")
    col_dst = lax.axis_index("peak") * width_here + jnp.arange(width_here, dtype=jnp.int32)
    ypos = slot // SLOT_C * mrows + jnp.arange(mrows, dtype=jnp.int32)
    xpos = slot % SLOT_C * COLS + col_dst
    dy_two = 2 * ypos + 1 - slot_rows * mrows
    dx_two = 2 * xpos + 1 - SLOT_C * COLS
    cycle = cycle_index(dy_two[:, None] * dy_two[:, None] + dx_two[None, :] * dx_two[None, :])
    levels = jnp.arange(CYCLES, dtype=jnp.int32)
    hits = (cycle.reshape(1, -1) == levels[:, None]).astype(jnp.bfloat16)
    pixels = frame.reshape(frames_all, -1)
    values = pixels.astype(jnp.float32)
    square = values * values
    square_top = lax.reduce_precision(square, exponent_bits=8, mantissa_bits=7)
    square_hi = square_top.astype(jnp.bfloat16)
    square_lo = (square - square_top).astype(jnp.bfloat16)
    stacked = jnp.concatenate([pixels, square_hi, square_lo], axis=0)
    sums = jnp.einsum("fp,kp->fk", stacked, hits, preferred_element_type=jnp.float32)
    first = sums[:frames_all]
    second = sums[frames_all : 2 * frames_all] + sums[2 * frames_all :]
    lanes = 128
    packed = jnp.concatenate(
        [
            first,
            second,
            jnp.zeros((frames_all, CYCLES), jnp.float32).at[0].set(present_part),
            jnp.zeros((frames_all, lanes - 3 * CYCLES), jnp.float32),
        ],
        axis=1,
    )
    summed = gather_sum(packed)
    first = summed[:, :CYCLES]
    second = summed[:, CYCLES : 2 * CYCLES]
    present_flag = summed[0, 2 * CYCLES : 3 * CYCLES]
    cycle_average, cycle_rms = cycle_stats(first, second, present_flag)
    edge_cycle = jnp.stack([cycle[:, width_here - 1], cycle[:, 0]], axis=1)
    edge_values = jnp.stack([frame[:, :, width_here - 1], frame[:, :, 0]], axis=2)
    edge_hits = (edge_cycle.reshape(1, -1) == levels[:, None]).astype(jnp.float32)
    edge_table = jnp.einsum(
        "fk,kp->fp",
        jnp.concatenate([cycle_average, cycle_rms], axis=0),
        edge_hits,
        precision=precise_variant,
    ).reshape(2 * frames_all, mrows, 2)
    edge_mean = edge_table[:frames_all]
    edge_rms = edge_table[frames_all:]
    edge_score = (edge_values.astype(jnp.float32) - edge_mean) / edge_rms
    fwd = [(i, i + 1) for i in range(n_peak - 1)]
    bwd = [(i + 1, i) for i in range(n_peak - 1)]
    left = lax.ppermute(edge_score[:, :, :1], "peak", fwd)
    right = lax.ppermute(edge_score[:, :, 1:], "peak", bwd)
    snr, bent = score_outputs(frame, cycle, cycle_average, cycle_rms, left, right, n_peak)
    return (snr[:, None], bent[:, None])


def solution(mesh):
    in_specs = (
        P("peak", None, "calib", None),
        P(None, None, "calib", None),
        P(None, None, "calib", None),
        P(None, "calib", None),
        P(),
        P(),
    )
    out_specs = (P(None, "calib", None, "peak"), P(None, "calib", None, "peak"))
    return jax.shard_map(body, mesh=mesh, in_specs=in_specs, out_specs=out_specs, check_vma=False)
```

```python
import jax
import jax.numpy as jnp
from jax import lax
from jax.sharding import PartitionSpec as P
from jax.experimental import pallas as pl
from jax.experimental.pallas import tpu as pltpu

COLS = 1024
BANDS = 8
SLOT_C = 4
CYCLES = 32
CYCLE_W = 64


precise_variant = lax.Precision.HIGHEST


def padded_2(block, sides, width):
    for axis, dim in sides:
        count = lax.axis_size(axis)
        forward = [(i, i + 1) for i in range(count - 1)]
        backward = [(target, source) for source, target in forward]
        low = lax.ppermute(
            lax.slice_in_dim(block, block.shape[dim] - width, None, axis=dim), axis, forward
        )
        high = lax.ppermute(lax.slice_in_dim(block, 0, width, axis=dim), axis, backward)
        block = jnp.concatenate([low, block, high], axis=dim)
    return block


def cycle_index(dist):
    levels = jnp.arange(1, CYCLES, dtype=jnp.int32)
    lows = (2 * CYCLE_W * levels) ** 2
    return jnp.sum((dist[..., None] >= lows).astype(jnp.int32), axis=-1)


def cycle_onehot(slot, row_pos, col_pos, mrows, slot_rows):
    ypos = slot // SLOT_C * mrows + row_pos
    xpos = slot % SLOT_C * COLS + col_pos
    dy_two = 2 * ypos + 1 - slot_rows * mrows
    dx_two = 2 * xpos + 1 - SLOT_C * COLS
    dist = dy_two[:, None] * dy_two[:, None] + dx_two[None, :] * dx_two[None, :]
    levels = jnp.arange(CYCLES, dtype=jnp.int32)
    lows = (2 * CYCLE_W * levels) ** 2
    cycle = jnp.sum((dist[None] >= lows[:, None, None]).astype(jnp.int32), axis=0) - 1
    hits = (cycle[None] == levels[:, None, None]).astype(jnp.float32)
    return hits.reshape(CYCLES, -1)


def calibrate(raw, pedestal, gain, good, bounds):
    code = raw // 2048
    counts_adc = (raw % 2048).astype(jnp.float32)
    base = jnp.where(code == 0, pedestal[0], jnp.where(code == 1, pedestal[1], pedestal[2]))
    gain_factor = gain.astype(jnp.float32)
    scale = jnp.where(
        code == 0, gain_factor[0], jnp.where(code == 1, gain_factor[1], gain_factor[2])
    )
    weight_factor = good.astype(jnp.float32)
    energy = weight_factor * (counts_adc - base) / scale
    columns = jnp.arange(raw.shape[-1], dtype=jnp.int32)
    band = jnp.sum((columns[None, :, None] >= bounds[:, None, :]).astype(jnp.int32), axis=2)
    member_entry = (band[:, :, None] == jnp.arange(BANDS, dtype=jnp.int32)[None, None, :]).astype(
        jnp.float32
    )
    totals = jnp.einsum("fmrc,mcb->fmrb", energy, member_entry, precision=precise_variant)
    present_flag = jnp.einsum(
        "tlg,tgd->tld", weight_factor, member_entry, precision=precise_variant
    )
    level = totals / jnp.maximum(present_flag, 1.0)
    spread = jnp.einsum("fmrb,mcb->fmrc", level, member_entry, precision=precise_variant)
    return (weight_factor * (energy - spread)).astype(jnp.bfloat16)


def calibrate_kernel(group, table_ref, bounds_ref, raw_ref, ped_ref, gain_ref, good_ref, out_ref):
    step = pl.program_id(0)
    cols = raw_ref.shape[-1]
    columns = lax.broadcasted_iota(jnp.int32, (1, cols), 1)
    quarters = out_ref.shape[1]
    width = cols // quarters
    for inner in range(group):
        module = step * group + inner
        raw = raw_ref[:, inner]
        code = lax.shift_right_logical(raw, 11)
        counts_adc = (raw & 2047).astype(jnp.float32)
        base = jnp.where(
            code == 0, ped_ref[0, inner], jnp.where(code == 1, ped_ref[1, inner], ped_ref[2, inner])
        )
        scale = jnp.where(
            code == 0,
            gain_ref[0, inner].astype(jnp.float32),
            jnp.where(
                code == 1,
                gain_ref[1, inner].astype(jnp.float32),
                gain_ref[2, inner].astype(jnp.float32),
            ),
        )
        weight_factor = good_ref[inner].astype(jnp.float32)
        energy = weight_factor * (counts_adc - base) / scale
        band = jnp.zeros((1, cols), jnp.int32)
        for j in range(BANDS - 1):
            band = band + (columns >= bounds_ref[module * (BANDS - 1) + j]).astype(jnp.int32)
        spread = jnp.zeros(energy.shape, jnp.float32)
        for b in range(BANDS):
            member = band == b
            totals = jnp.sum(jnp.where(member, energy, 0.0), axis=-1, keepdims=True)
            present = jnp.sum(jnp.where(member, weight_factor, 0.0), axis=-1, keepdims=True)
            spread = jnp.where(member, totals / jnp.maximum(present, 1.0), spread)
        corrected = (weight_factor * (energy - spread)).astype(jnp.bfloat16)
        slot = table_ref[module]
        for q in range(quarters):
            out_ref[slot, q] = corrected[:, :, q * width : (q + 1) * width]


def calibrate_send(raw, pedestal, gain, good, bounds, table, n_peak):
    frame_dev, mods, row_dev, cols = raw.shape
    width = cols // n_peak
    group = 8
    grid_spec = pltpu.PrefetchScalarGridSpec(
        num_scalar_prefetch=2,
        grid=(mods // group,),
        in_specs=[
            pl.BlockSpec((frame_dev, group, row_dev, cols), lambda m, t, b: (0, m, 0, 0)),
            pl.BlockSpec((3, group, row_dev, cols), lambda m, t, b: (0, m, 0, 0)),
            pl.BlockSpec((3, group, row_dev, cols), lambda m, t, b: (0, m, 0, 0)),
            pl.BlockSpec((group, row_dev, cols), lambda m, t, b: (m, 0, 0)),
        ],
        out_specs=pl.BlockSpec(
            (mods, n_peak, frame_dev, row_dev, width), lambda m, t, b: (0, 0, 0, 0, 0)
        ),
    )
    return pl.pallas_call(
        lambda *refs: calibrate_kernel(group, *refs),
        grid_spec=grid_spec,
        out_shape=jax.ShapeDtypeStruct((mods, n_peak, frame_dev, row_dev, width), jnp.bfloat16),
    )(table, bounds.reshape(-1), raw, pedestal, gain, good)


def score_kernel(n_peak, levels, per, low_ref, mean_ref, rms_ref, frame_ref, cycle_ref, left_ref, right_ref, snr_ref, bent_ref):
    cycle = cycle_ref[...]
    rows, cols = cycle.shape
    tops = mean_ref.shape[1] - 1
    peak_pos = lax.axis_index("peak")
    row_ids = lax.broadcasted_iota(jnp.int32, (rows, cols), 0)
    col_ids = lax.broadcasted_iota(jnp.int32, (rows, cols), 1)
    row_shifts = []
    for shift in (1, rows - 1):
        source = pltpu.roll(row_ids, shift, 0)
        row_shifts.append((shift, jnp.abs(source - row_ids) == 1))
    col_shifts = []
    for shift in (1, cols - 1):
        source = pltpu.roll(col_ids, shift, 1)
        col_shifts.append((shift, jnp.abs(source - col_ids) == 1, source == cols - 1))
    hits = []
    for j in range(levels):
        level = jnp.minimum(low_ref[0] + j, tops)
        hits.append((level, cycle == level))
    for inner in range(per):
        frame_pos = pl.program_id(0) * per + inner
        values = frame_ref[inner].astype(jnp.float32)
        pixel_mean = jnp.zeros((rows, cols), jnp.float32)
        pixel_rms = jnp.ones((rows, cols), jnp.float32)
        for level, hit in hits:
            pixel_mean = jnp.where(hit, mean_ref[frame_pos, level], pixel_mean)
            pixel_rms = jnp.where(hit, rms_ref[frame_pos, level], pixel_rms)
        score = (values - pixel_mean) / pixel_rms
        pick = lax.broadcasted_iota(jnp.int32, (rows, left_ref.shape[0]), 1) == frame_pos
        left_all = jnp.transpose(left_ref[...])
        right_all = jnp.transpose(right_ref[...])
        left_col = jnp.sum(jnp.where(pick, left_all, 0.0), axis=1, keepdims=True)
        right_col = jnp.sum(jnp.where(pick, right_all, 0.0), axis=1, keepdims=True)
        left_col = jnp.where(peak_pos == 0, 0.0, left_col)
        right_col = jnp.where(peak_pos == n_peak - 1, 0.0, right_col)
        total = 4.0 * score
        for shift, inside in row_shifts:
            total = total - jnp.where(inside, pltpu.roll(score, shift, 0), 0.0)
        for shift, inside, wrapped_left in col_shifts:
            near = jnp.where(wrapped_left, left_col, right_col)
            total = total - jnp.where(inside, pltpu.roll(score, shift, 1), near)
        snr_ref[inner] = score.astype(snr_ref.dtype)
        bent_ref[inner] = total.astype(bent_ref.dtype)


def score_outputs(frame, cycle, cycle_average, cycle_rms, left, right, n_peak):
    frames, rows, cols = frame.shape
    span = (rows * rows + cols * cols) ** 0.5
    levels = min(CYCLES, int(span // CYCLE_W) + 2)
    per = 2 if frames % 2 == 0 else 1
    low = jnp.min(cycle).reshape(1)
    block = pl.BlockSpec((per, rows, cols), lambda f, *_: (f, 0, 0))
    edge = pl.BlockSpec((frames, rows), lambda f, *_: (0, 0))
    grid_spec = pltpu.PrefetchScalarGridSpec(
        num_scalar_prefetch=3,
        grid=(frames // per,),
        in_specs=[block, pl.BlockSpec((rows, cols), lambda f, *_: (0, 0)), edge, edge],
        out_specs=[block, block],
    )
    return pl.pallas_call(
        lambda *refs: score_kernel(n_peak, levels, per, *refs),
        grid_spec=grid_spec,
        out_shape=[jax.ShapeDtypeStruct(frame.shape, jnp.bfloat16)] * 2,
    )(low, cycle_average, cycle_rms, frame, cycle, left, right)


def laplace(padded):
    center = padded[..., 1:-1, 1:-1]
    return (
        4.0 * center
        - padded[..., :-2, 1:-1]
        - padded[..., 2:, 1:-1]
        - padded[..., 1:-1, :-2]
        - padded[..., 1:-1, 2:]
    )


def local_present(good, table, row_src, mrows, slot_rows):
    n_peak = lax.axis_size("peak")
    width = good.shape[2] // n_peak
    start = lax.axis_index("peak") * width
    part = lax.dynamic_slice_in_dim(good, start, width, axis=2)
    col = start + jnp.arange(width, dtype=jnp.int32)
    ypos = (table // SLOT_C)[:, None] * mrows + row_src[None, :]
    xpos = (table % SLOT_C)[:, None] * COLS + col[None, :]
    dy_two = 2 * ypos + 1 - slot_rows * mrows
    dx_two = 2 * xpos + 1 - SLOT_C * COLS
    dist = dy_two[:, :, None] * dy_two[:, :, None] + dx_two[:, None, :] * dx_two[:, None, :]
    cycle = cycle_index(dist)
    levels = jnp.arange(CYCLES, dtype=jnp.int32)
    hit = jnp.where(cycle[..., None] == levels, part[..., None], 0)
    return jnp.sum(hit, axis=(0, 1, 2)).astype(jnp.float32)


def gather_sum_kernel(
    n_calib, n_peak, x_ref, o_ref, near, far, partial, near_send, near_recv, far_send, far_recv
):
    my_calib = lax.axis_index("calib")
    my_peak = lax.axis_index("peak")
    near[n_peak - 1] = x_ref[...]
    barrier = pltpu.get_barrier_semaphore()

    def peak_peer(step):
        return (my_calib, lax.rem(my_peak + step, n_peak))

    def calib_peer(step):
        return (lax.rem(my_calib + step, n_calib), my_peak)

    def greet_peak(step, carry):
        pl.semaphore_signal(
            barrier, inc=1, device_id=peak_peer(step), device_id_type=pl.DeviceIdType.MESH
        )
        return carry

    def greet_calib(step, carry):
        pl.semaphore_signal(
            barrier, inc=1, device_id=calib_peer(step), device_id_type=pl.DeviceIdType.MESH
        )
        return carry

    lax.fori_loop(1, n_peak, greet_peak, 0)
    lax.fori_loop(1, n_calib, greet_calib, 0)
    pl.semaphore_wait(barrier, n_peak - 1 + n_calib - 1)

    def send_near(step, carry):
        pltpu.make_async_remote_copy(
            src_ref=x_ref,
            dst_ref=near.at[n_peak - 1 - step],
            send_sem=near_send,
            recv_sem=near_recv,
            device_id=peak_peer(step),
            device_id_type=pl.DeviceIdType.MESH,
        ).start()
        return carry

    lax.fori_loop(1, n_peak, send_near, 0)
    every_near = pltpu.make_async_remote_copy(
        src_ref=near.at[pl.ds(0, n_peak - 1)],
        dst_ref=near.at[pl.ds(0, n_peak - 1)],
        send_sem=near_send,
        recv_sem=near_recv,
        device_id=peak_peer(1),
        device_id_type=pl.DeviceIdType.MESH,
    )
    every_near.wait_send()
    every_near.wait_recv()

    def add_near(source, acc):
        return acc + near[lax.rem(source - my_peak - 1 + 2 * n_peak, n_peak)]

    partial[...] = lax.fori_loop(0, n_peak, add_near, jnp.zeros(x_ref.shape, x_ref.dtype))
    far[n_calib - 1] = partial[...]

    def send_far(step, carry):
        pltpu.make_async_remote_copy(
            src_ref=partial,
            dst_ref=far.at[n_calib - 1 - step],
            send_sem=far_send,
            recv_sem=far_recv,
            device_id=calib_peer(step),
            device_id_type=pl.DeviceIdType.MESH,
        ).start()
        return carry

    lax.fori_loop(1, n_calib, send_far, 0)
    every_far = pltpu.make_async_remote_copy(
        src_ref=far.at[pl.ds(0, n_calib - 1)],
        dst_ref=far.at[pl.ds(0, n_calib - 1)],
        send_sem=far_send,
        recv_sem=far_recv,
        device_id=calib_peer(1),
        device_id_type=pl.DeviceIdType.MESH,
    )
    every_far.wait_send()
    every_far.wait_recv()

    def add_far(source, acc):
        return acc + far[lax.rem(source - my_calib - 1 + 2 * n_calib, n_calib)]

    o_ref[...] = lax.fori_loop(0, n_calib, add_far, jnp.zeros(x_ref.shape, x_ref.dtype))


def gather_sum(x):
    n_calib = lax.axis_size("calib")
    n_peak = lax.axis_size("peak")
    return pl.pallas_call(
        lambda *refs: gather_sum_kernel(n_calib, n_peak, *refs),
        out_shape=jax.ShapeDtypeStruct(x.shape, x.dtype),
        in_specs=[pl.BlockSpec(memory_space=pltpu.VMEM)],
        out_specs=pl.BlockSpec(memory_space=pltpu.VMEM),
        scratch_shapes=[
            pltpu.VMEM((n_peak,) + x.shape, x.dtype),
            pltpu.VMEM((n_calib,) + x.shape, x.dtype),
            pltpu.VMEM(x.shape, x.dtype),
            pltpu.SemaphoreType.DMA,
            pltpu.SemaphoreType.DMA,
            pltpu.SemaphoreType.DMA,
            pltpu.SemaphoreType.DMA,
        ],
        compiler_params=pltpu.CompilerParams(collective_id=0, has_side_effects=True),
    )(x)


def cycle_stats(first, second, present_flag):
    cycle_average = first / present_flag[None, :]
    cycle_rms = jnp.sqrt(second / present_flag[None, :] + 1e-06)
    return (cycle_average, cycle_rms)


def body(raw, pedestal, gain, good, bounds, table):
    frame_dev, mods, row_dev, cols = raw.shape
    n_calib = lax.axis_size("calib")
    n_peak = lax.axis_size("peak")
    mrows = row_dev * n_calib
    slot_rows = mods // SLOT_C
    width_here = cols // n_peak
    frames_all = frame_dev * n_peak
    row_src = lax.axis_index("calib") * row_dev + jnp.arange(row_dev, dtype=jnp.int32)
    send = calibrate_send(raw, pedestal, gain, good, bounds, table, n_peak)
    send = send.reshape(mods * n_peak, frame_dev, row_dev, width_here)
    present_part = local_present(good, table, row_src, mrows, slot_rows)
    got = lax.all_to_all(send, ("calib", "peak"), 0, 0, tiled=True)
    got = got.reshape(n_calib, n_peak, frame_dev, row_dev, width_here)
    frame = jnp.transpose(got, (1, 2, 0, 3, 4)).reshape(frames_all, mrows, width_here)
    slot = lax.axis_index("calib")
    col_dst = lax.axis_index("peak") * width_here + jnp.arange(width_here, dtype=jnp.int32)
    ypos = slot // SLOT_C * mrows + jnp.arange(mrows, dtype=jnp.int32)
    xpos = slot % SLOT_C * COLS + col_dst
    dy_two = 2 * ypos + 1 - slot_rows * mrows
    dx_two = 2 * xpos + 1 - SLOT_C * COLS
    cycle = cycle_index(dy_two[:, None] * dy_two[:, None] + dx_two[None, :] * dx_two[None, :])
    levels = jnp.arange(CYCLES, dtype=jnp.int32)
    hits = (cycle.reshape(1, -1) == levels[:, None]).astype(jnp.bfloat16)
    pixels = frame.reshape(frames_all, -1)
    values = pixels.astype(jnp.float32)
    square = values * values
    square_top = lax.reduce_precision(square, exponent_bits=8, mantissa_bits=7)
    square_hi = square_top.astype(jnp.bfloat16)
    square_lo = (square - square_top).astype(jnp.bfloat16)
    stacked = jnp.concatenate([pixels, square_hi, square_lo], axis=0)
    sums = jnp.einsum("fp,kp->fk", stacked, hits, preferred_element_type=jnp.float32)
    first = sums[:frames_all]
    second = sums[frames_all : 2 * frames_all] + sums[2 * frames_all :]
    lanes = 128
    packed = jnp.concatenate(
        [
            first,
            second,
            jnp.zeros((frames_all, CYCLES), jnp.float32).at[0].set(present_part),
            jnp.zeros((frames_all, lanes - 3 * CYCLES), jnp.float32),
        ],
        axis=1,
    )
    summed = gather_sum(packed)
    first = summed[:, :CYCLES]
    second = summed[:, CYCLES : 2 * CYCLES]
    present_flag = summed[0, 2 * CYCLES : 3 * CYCLES]
    cycle_average, cycle_rms = cycle_stats(first, second, present_flag)
    edge_cycle = jnp.stack([cycle[:, width_here - 1], cycle[:, 0]], axis=1)
    edge_values = jnp.stack([frame[:, :, width_here - 1], frame[:, :, 0]], axis=2)
    edge_hits = (edge_cycle.reshape(1, -1) == levels[:, None]).astype(jnp.float32)
    edge_table = jnp.einsum(
        "fk,kp->fp",
        jnp.concatenate([cycle_average, cycle_rms], axis=0),
        edge_hits,
        precision=precise_variant,
    ).reshape(2 * frames_all, mrows, 2)
    edge_mean = edge_table[:frames_all]
    edge_rms = edge_table[frames_all:]
    edge_score = (edge_values.astype(jnp.float32) - edge_mean) / edge_rms
    fwd = [(i, i + 1) for i in range(n_peak - 1)]
    bwd = [(i + 1, i) for i in range(n_peak - 1)]
    left = lax.ppermute(edge_score[:, :, 0], "peak", fwd)
    right = lax.ppermute(edge_score[:, :, 1], "peak", bwd)
    snr, bent = score_outputs(frame, cycle, cycle_average, cycle_rms, left, right, n_peak)
    return (snr[:, None], bent[:, None])


def solution(mesh):
    in_specs = (
        P("peak", None, "calib", None),
        P(None, None, "calib", None),
        P(None, None, "calib", None),
        P(None, "calib", None),
        P(),
        P(),
    )
    out_specs = (P(None, "calib", None, "peak"), P(None, "calib", None, "peak"))
    return jax.shard_map(body, mesh=mesh, in_specs=in_specs, out_specs=out_specs, check_vma=False)
```

```python
import jax
import jax.numpy as jnp
from jax import lax
from jax.sharding import PartitionSpec as P
from jax.experimental import pallas as pl
from jax.experimental.pallas import tpu as pltpu

COLS = 1024
BANDS = 8
SLOT_C = 4
CYCLES = 32
CYCLE_W = 64


precise_variant = lax.Precision.HIGHEST


def padded_2(block, sides, width):
    for axis, dim in sides:
        count = lax.axis_size(axis)
        forward = [(i, i + 1) for i in range(count - 1)]
        backward = [(target, source) for source, target in forward]
        low = lax.ppermute(
            lax.slice_in_dim(block, block.shape[dim] - width, None, axis=dim), axis, forward
        )
        high = lax.ppermute(lax.slice_in_dim(block, 0, width, axis=dim), axis, backward)
        block = jnp.concatenate([low, block, high], axis=dim)
    return block


def cycle_index(dist):
    levels = jnp.arange(1, CYCLES, dtype=jnp.int32)
    lows = (2 * CYCLE_W * levels) ** 2
    return jnp.sum((dist[..., None] >= lows).astype(jnp.int32), axis=-1)


def cycle_onehot(slot, row_pos, col_pos, mrows, slot_rows):
    ypos = slot // SLOT_C * mrows + row_pos
    xpos = slot % SLOT_C * COLS + col_pos
    dy_two = 2 * ypos + 1 - slot_rows * mrows
    dx_two = 2 * xpos + 1 - SLOT_C * COLS
    dist = dy_two[:, None] * dy_two[:, None] + dx_two[None, :] * dx_two[None, :]
    levels = jnp.arange(CYCLES, dtype=jnp.int32)
    lows = (2 * CYCLE_W * levels) ** 2
    cycle = jnp.sum((dist[None] >= lows[:, None, None]).astype(jnp.int32), axis=0) - 1
    hits = (cycle[None] == levels[:, None, None]).astype(jnp.float32)
    return hits.reshape(CYCLES, -1)


def calibrate(raw, pedestal, gain, good, bounds):
    code = raw // 2048
    counts_adc = (raw % 2048).astype(jnp.float32)
    base = jnp.where(code == 0, pedestal[0], jnp.where(code == 1, pedestal[1], pedestal[2]))
    gain_factor = gain.astype(jnp.float32)
    scale = jnp.where(
        code == 0, gain_factor[0], jnp.where(code == 1, gain_factor[1], gain_factor[2])
    )
    weight_factor = good.astype(jnp.float32)
    energy = weight_factor * (counts_adc - base) / scale
    columns = jnp.arange(raw.shape[-1], dtype=jnp.int32)
    band = jnp.sum((columns[None, :, None] >= bounds[:, None, :]).astype(jnp.int32), axis=2)
    member_entry = (band[:, :, None] == jnp.arange(BANDS, dtype=jnp.int32)[None, None, :]).astype(
        jnp.float32
    )
    totals = jnp.einsum("fmrc,mcb->fmrb", energy, member_entry, precision=precise_variant)
    present_flag = jnp.einsum(
        "tlg,tgd->tld", weight_factor, member_entry, precision=precise_variant
    )
    level = totals / jnp.maximum(present_flag, 1.0)
    spread = jnp.einsum("fmrb,mcb->fmrc", level, member_entry, precision=precise_variant)
    return (weight_factor * (energy - spread)).astype(jnp.bfloat16)


def calibrate_kernel(group, table_ref, bounds_ref, raw_ref, ped_ref, gain_ref, good_ref, out_ref):
    step = pl.program_id(0)
    cols = raw_ref.shape[-1]
    columns = lax.broadcasted_iota(jnp.int32, (1, cols), 1)
    quarters = out_ref.shape[1]
    width = cols // quarters
    for inner in range(group):
        module = step * group + inner
        raw = raw_ref[:, inner]
        code = lax.shift_right_logical(raw, 11)
        counts_adc = (raw & 2047).astype(jnp.float32)
        base = jnp.where(
            code == 0, ped_ref[0, inner], jnp.where(code == 1, ped_ref[1, inner], ped_ref[2, inner])
        )
        scale = jnp.where(
            code == 0,
            gain_ref[0, inner].astype(jnp.float32),
            jnp.where(
                code == 1,
                gain_ref[1, inner].astype(jnp.float32),
                gain_ref[2, inner].astype(jnp.float32),
            ),
        )
        weight_factor = good_ref[inner].astype(jnp.float32)
        energy = weight_factor * (counts_adc - base) / scale
        band = jnp.zeros((1, cols), jnp.int32)
        for j in range(BANDS - 1):
            band = band + (columns >= bounds_ref[module * (BANDS - 1) + j]).astype(jnp.int32)
        spread = jnp.zeros(energy.shape, jnp.float32)
        for b in range(BANDS):
            member = band == b
            totals = jnp.sum(jnp.where(member, energy, 0.0), axis=-1, keepdims=True)
            present = jnp.sum(jnp.where(member, weight_factor, 0.0), axis=-1, keepdims=True)
            spread = jnp.where(member, totals / jnp.maximum(present, 1.0), spread)
        corrected = (weight_factor * (energy - spread)).astype(jnp.bfloat16)
        slot = table_ref[module]
        for q in range(quarters):
            out_ref[slot, q] = corrected[:, :, q * width : (q + 1) * width]


def calibrate_send(raw, pedestal, gain, good, bounds, table, n_peak):
    frame_dev, mods, row_dev, cols = raw.shape
    width = cols // n_peak
    group = 8
    grid_spec = pltpu.PrefetchScalarGridSpec(
        num_scalar_prefetch=2,
        grid=(mods // group,),
        in_specs=[
            pl.BlockSpec((frame_dev, group, row_dev, cols), lambda m, t, b: (0, m, 0, 0)),
            pl.BlockSpec((3, group, row_dev, cols), lambda m, t, b: (0, m, 0, 0)),
            pl.BlockSpec((3, group, row_dev, cols), lambda m, t, b: (0, m, 0, 0)),
            pl.BlockSpec((group, row_dev, cols), lambda m, t, b: (m, 0, 0)),
        ],
        out_specs=pl.BlockSpec(
            (mods, n_peak, frame_dev, row_dev, width), lambda m, t, b: (0, 0, 0, 0, 0)
        ),
    )
    return pl.pallas_call(
        lambda *refs: calibrate_kernel(group, *refs),
        grid_spec=grid_spec,
        out_shape=jax.ShapeDtypeStruct((mods, n_peak, frame_dev, row_dev, width), jnp.bfloat16),
    )(table, bounds.reshape(-1), raw, pedestal, gain, good)


def score_kernel(n_peak, levels, per, low_ref, mean_ref, rms_ref, frame_ref, cycle_ref, left_ref, right_ref, snr_ref, bent_ref):
    cycle = cycle_ref[...]
    rows, cols = cycle.shape
    tops = mean_ref.shape[1] - 1
    peak_pos = lax.axis_index("peak")
    row_ids = lax.broadcasted_iota(jnp.int32, (rows, cols), 0)
    col_ids = lax.broadcasted_iota(jnp.int32, (rows, cols), 1)
    row_shifts = []
    for shift in (1, rows - 1):
        source = pltpu.roll(row_ids, shift, 0)
        row_shifts.append((shift, jnp.abs(source - row_ids) == 1))
    col_shifts = []
    for shift in (1, cols - 1):
        source = pltpu.roll(col_ids, shift, 1)
        col_shifts.append((shift, jnp.abs(source - col_ids) == 1, source == cols - 1))
    hits = []
    for j in range(levels):
        level = jnp.minimum(low_ref[0] + j, tops)
        hits.append((level, cycle == level))
    for inner in range(per):
        frame_pos = pl.program_id(0) * per + inner
        values = frame_ref[inner].astype(jnp.float32)
        pixel_mean = jnp.zeros((rows, cols), jnp.float32)
        pixel_rms = jnp.ones((rows, cols), jnp.float32)
        for level, hit in hits:
            pixel_mean = jnp.where(hit, mean_ref[frame_pos, level], pixel_mean)
            pixel_rms = jnp.where(hit, rms_ref[frame_pos, level], pixel_rms)
        score = (values - pixel_mean) / pixel_rms
        pick = lax.broadcasted_iota(jnp.int32, (rows, left_ref.shape[0]), 1) == frame_pos
        left_all = jnp.transpose(left_ref[...])
        right_all = jnp.transpose(right_ref[...])
        left_col = jnp.sum(jnp.where(pick, left_all, 0.0), axis=1, keepdims=True)
        right_col = jnp.sum(jnp.where(pick, right_all, 0.0), axis=1, keepdims=True)
        left_col = jnp.where(peak_pos == 0, 0.0, left_col)
        right_col = jnp.where(peak_pos == n_peak - 1, 0.0, right_col)
        total = 4.0 * score
        for shift, inside in row_shifts:
            total = total - jnp.where(inside, pltpu.roll(score, shift, 0), 0.0)
        for shift, inside, wrapped_left in col_shifts:
            near = jnp.where(wrapped_left, left_col, right_col)
            total = total - jnp.where(inside, pltpu.roll(score, shift, 1), near)
        snr_ref[inner] = score.astype(snr_ref.dtype)
        bent_ref[inner] = total.astype(bent_ref.dtype)


def score_outputs(frame, cycle, cycle_average, cycle_rms, left, right, n_peak):
    frames, rows, cols = frame.shape
    span = (rows * rows + cols * cols) ** 0.5
    levels = min(CYCLES, int(span // CYCLE_W) + 2)
    per = 2 if frames % 2 == 0 else 1
    low = jnp.min(cycle).reshape(1)
    block = pl.BlockSpec((per, rows, cols), lambda f, *_: (f, 0, 0))
    edge = pl.BlockSpec((frames, rows), lambda f, *_: (0, 0))
    grid_spec = pltpu.PrefetchScalarGridSpec(
        num_scalar_prefetch=3,
        grid=(frames // per,),
        in_specs=[block, pl.BlockSpec((rows, cols), lambda f, *_: (0, 0)), edge, edge],
        out_specs=[block, block],
    )
    return pl.pallas_call(
        lambda *refs: score_kernel(n_peak, levels, per, *refs),
        grid_spec=grid_spec,
        out_shape=[jax.ShapeDtypeStruct(frame.shape, jnp.bfloat16)] * 2,
    )(low, cycle_average, cycle_rms, frame, cycle, left, right)


def laplace(padded):
    center = padded[..., 1:-1, 1:-1]
    return (
        4.0 * center
        - padded[..., :-2, 1:-1]
        - padded[..., 2:, 1:-1]
        - padded[..., 1:-1, :-2]
        - padded[..., 1:-1, 2:]
    )


def local_present(good, table, row_src, mrows, slot_rows):
    n_peak = lax.axis_size("peak")
    width = good.shape[2] // n_peak
    start = lax.axis_index("peak") * width
    part = lax.dynamic_slice_in_dim(good, start, width, axis=2)
    col = start + jnp.arange(width, dtype=jnp.int32)
    ypos = (table // SLOT_C)[:, None] * mrows + row_src[None, :]
    xpos = (table % SLOT_C)[:, None] * COLS + col[None, :]
    dy_two = 2 * ypos + 1 - slot_rows * mrows
    dx_two = 2 * xpos + 1 - SLOT_C * COLS
    dist = dy_two[:, :, None] * dy_two[:, :, None] + dx_two[:, None, :] * dx_two[:, None, :]
    cycle = cycle_index(dist)
    levels = jnp.arange(CYCLES, dtype=jnp.int32)
    hit = jnp.where(cycle[..., None] == levels, part[..., None], 0)
    return jnp.sum(hit, axis=(0, 1, 2)).astype(jnp.float32)


def gather_sum_kernel(
    n_calib, n_peak, x_ref, o_ref, near, far, partial, near_send, near_recv, far_send, far_recv
):
    my_calib = lax.axis_index("calib")
    my_peak = lax.axis_index("peak")
    near[n_peak - 1] = x_ref[...]
    barrier = pltpu.get_barrier_semaphore()

    def peak_peer(step):
        return (my_calib, lax.rem(my_peak + step, n_peak))

    def calib_peer(step):
        return (lax.rem(my_calib + step, n_calib), my_peak)

    def greet_peak(step, carry):
        pl.semaphore_signal(
            barrier, inc=1, device_id=peak_peer(step), device_id_type=pl.DeviceIdType.MESH
        )
        return carry

    def greet_calib(step, carry):
        pl.semaphore_signal(
            barrier, inc=1, device_id=calib_peer(step), device_id_type=pl.DeviceIdType.MESH
        )
        return carry

    lax.fori_loop(1, n_peak, greet_peak, 0)
    lax.fori_loop(1, n_calib, greet_calib, 0)
    pl.semaphore_wait(barrier, n_peak - 1 + n_calib - 1)

    def send_near(step, carry):
        pltpu.make_async_remote_copy(
            src_ref=x_ref,
            dst_ref=near.at[n_peak - 1 - step],
            send_sem=near_send,
            recv_sem=near_recv,
            device_id=peak_peer(step),
            device_id_type=pl.DeviceIdType.MESH,
        ).start()
        return carry

    lax.fori_loop(1, n_peak, send_near, 0)
    every_near = pltpu.make_async_remote_copy(
        src_ref=near.at[pl.ds(0, n_peak - 1)],
        dst_ref=near.at[pl.ds(0, n_peak - 1)],
        send_sem=near_send,
        recv_sem=near_recv,
        device_id=peak_peer(1),
        device_id_type=pl.DeviceIdType.MESH,
    )
    every_near.wait_send()
    every_near.wait_recv()

    def add_near(source, acc):
        return acc + near[lax.rem(source - my_peak - 1 + 2 * n_peak, n_peak)]

    partial[...] = lax.fori_loop(0, n_peak, add_near, jnp.zeros(x_ref.shape, x_ref.dtype))
    far[n_calib - 1] = partial[...]

    def send_far(step, carry):
        pltpu.make_async_remote_copy(
            src_ref=partial,
            dst_ref=far.at[n_calib - 1 - step],
            send_sem=far_send,
            recv_sem=far_recv,
            device_id=calib_peer(step),
            device_id_type=pl.DeviceIdType.MESH,
        ).start()
        return carry

    lax.fori_loop(1, n_calib, send_far, 0)
    every_far = pltpu.make_async_remote_copy(
        src_ref=far.at[pl.ds(0, n_calib - 1)],
        dst_ref=far.at[pl.ds(0, n_calib - 1)],
        send_sem=far_send,
        recv_sem=far_recv,
        device_id=calib_peer(1),
        device_id_type=pl.DeviceIdType.MESH,
    )
    every_far.wait_send()
    every_far.wait_recv()

    def add_far(source, acc):
        return acc + far[lax.rem(source - my_calib - 1 + 2 * n_calib, n_calib)]

    o_ref[...] = lax.fori_loop(0, n_calib, add_far, jnp.zeros(x_ref.shape, x_ref.dtype))


def gather_sum(x):
    n_calib = lax.axis_size("calib")
    n_peak = lax.axis_size("peak")
    return pl.pallas_call(
        lambda *refs: gather_sum_kernel(n_calib, n_peak, *refs),
        out_shape=jax.ShapeDtypeStruct(x.shape, x.dtype),
        in_specs=[pl.BlockSpec(memory_space=pltpu.VMEM)],
        out_specs=pl.BlockSpec(memory_space=pltpu.VMEM),
        scratch_shapes=[
            pltpu.VMEM((n_peak,) + x.shape, x.dtype),
            pltpu.VMEM((n_calib,) + x.shape, x.dtype),
            pltpu.VMEM(x.shape, x.dtype),
            pltpu.SemaphoreType.DMA,
            pltpu.SemaphoreType.DMA,
            pltpu.SemaphoreType.DMA,
            pltpu.SemaphoreType.DMA,
        ],
        compiler_params=pltpu.CompilerParams(collective_id=0, has_side_effects=True),
    )(x)


def cycle_stats(first, second, present_flag):
    cycle_average = first / present_flag[None, :]
    cycle_rms = jnp.sqrt(second / present_flag[None, :] + 1e-06)
    return (cycle_average, cycle_rms)


def body(raw, pedestal, gain, good, bounds, table):
    frame_dev, mods, row_dev, cols = raw.shape
    n_calib = lax.axis_size("calib")
    n_peak = lax.axis_size("peak")
    mrows = row_dev * n_calib
    slot_rows = mods // SLOT_C
    width_here = cols // n_peak
    frames_all = frame_dev * n_peak
    row_src = lax.axis_index("calib") * row_dev + jnp.arange(row_dev, dtype=jnp.int32)
    send = calibrate_send(raw, pedestal, gain, good, bounds, table, n_peak)
    send = send.reshape(mods * n_peak, frame_dev, row_dev, width_here)
    present_part = local_present(good, table, row_src, mrows, slot_rows)
    got = lax.all_to_all(send, ("calib", "peak"), 0, 0, tiled=True)
    got = got.reshape(n_calib, n_peak, frame_dev, row_dev, width_here)
    frame = jnp.transpose(got, (1, 2, 0, 3, 4)).reshape(frames_all, mrows, width_here)
    slot = lax.axis_index("calib")
    col_dst = lax.axis_index("peak") * width_here + jnp.arange(width_here, dtype=jnp.int32)
    ypos = slot // SLOT_C * mrows + jnp.arange(mrows, dtype=jnp.int32)
    xpos = slot % SLOT_C * COLS + col_dst
    dy_two = 2 * ypos + 1 - slot_rows * mrows
    dx_two = 2 * xpos + 1 - SLOT_C * COLS
    cycle = cycle_index(dy_two[:, None] * dy_two[:, None] + dx_two[None, :] * dx_two[None, :])
    levels = jnp.arange(CYCLES, dtype=jnp.int32)
    hits = (cycle.reshape(1, -1) == levels[:, None]).astype(jnp.bfloat16)
    pixels = frame.reshape(frames_all, -1)
    values = pixels.astype(jnp.float32)
    square = values * values
    square_top = lax.reduce_precision(square, exponent_bits=8, mantissa_bits=7)
    square_hi = square_top.astype(jnp.bfloat16)
    square_lo = (square - square_top).astype(jnp.bfloat16)
    stacked = jnp.concatenate([pixels, square_hi, square_lo], axis=0)
    sums = jnp.einsum("fp,kp->fk", stacked, hits, preferred_element_type=jnp.float32)
    first = sums[:frames_all]
    second = sums[frames_all : 2 * frames_all] + sums[2 * frames_all :]
    lanes = 128
    packed = jnp.concatenate(
        [
            first,
            second,
            jnp.zeros((frames_all, CYCLES), jnp.float32).at[0].set(present_part),
            jnp.zeros((frames_all, lanes - 3 * CYCLES), jnp.float32),
        ],
        axis=1,
    )
    summed = gather_sum(packed)
    first = summed[:, :CYCLES]
    second = summed[:, CYCLES : 2 * CYCLES]
    present_flag = summed[0, 2 * CYCLES : 3 * CYCLES]
    cycle_average, cycle_rms = cycle_stats(first, second, present_flag)
    edge_cycle = jnp.concatenate([cycle[:, width_here - 1], cycle[:, 0]])
    edge_values = jnp.concatenate([frame[:, :, width_here - 1], frame[:, :, 0]], axis=1)
    edge_hits = (edge_cycle[None, :] == levels[:, None]).astype(jnp.float32)
    edge_table = jnp.einsum(
        "fk,kp->fp",
        jnp.concatenate([cycle_average, cycle_rms], axis=0),
        edge_hits,
        precision=precise_variant,
    )
    edge_score = (edge_values.astype(jnp.float32) - edge_table[:frames_all]) / edge_table[frames_all:]
    fwd = [(i, i + 1) for i in range(n_peak - 1)]
    bwd = [(i + 1, i) for i in range(n_peak - 1)]
    left = lax.ppermute(edge_score[:, :mrows], "peak", fwd)
    right = lax.ppermute(edge_score[:, mrows:], "peak", bwd)
    snr, bent = score_outputs(frame, cycle, cycle_average, cycle_rms, left, right, n_peak)
    return (snr[:, None], bent[:, None])


def solution(mesh):
    in_specs = (
        P("peak", None, "calib", None),
        P(None, None, "calib", None),
        P(None, None, "calib", None),
        P(None, "calib", None),
        P(),
        P(),
    )
    out_specs = (P(None, "calib", None, "peak"), P(None, "calib", None, "peak"))
    return jax.shard_map(body, mesh=mesh, in_specs=in_specs, out_specs=out_specs, check_vma=False)
```

```python
import jax
import jax.numpy as jnp
from jax import lax
from jax.sharding import PartitionSpec as P
from jax.experimental import pallas as pl
from jax.experimental.pallas import tpu as pltpu

COLS = 1024
BANDS = 8
SLOT_C = 4
CYCLES = 32
CYCLE_W = 64


precise_variant = lax.Precision.HIGHEST


def padded_2(block, sides, width):
    for axis, dim in sides:
        count = lax.axis_size(axis)
        forward = [(i, i + 1) for i in range(count - 1)]
        backward = [(target, source) for source, target in forward]
        low = lax.ppermute(
            lax.slice_in_dim(block, block.shape[dim] - width, None, axis=dim), axis, forward
        )
        high = lax.ppermute(lax.slice_in_dim(block, 0, width, axis=dim), axis, backward)
        block = jnp.concatenate([low, block, high], axis=dim)
    return block


def cycle_index(dist):
    levels = jnp.arange(1, CYCLES, dtype=jnp.int32)
    lows = (2 * CYCLE_W * levels) ** 2
    return jnp.sum((dist[..., None] >= lows).astype(jnp.int32), axis=-1)


def cycle_onehot(slot, row_pos, col_pos, mrows, slot_rows):
    ypos = slot // SLOT_C * mrows + row_pos
    xpos = slot % SLOT_C * COLS + col_pos
    dy_two = 2 * ypos + 1 - slot_rows * mrows
    dx_two = 2 * xpos + 1 - SLOT_C * COLS
    dist = dy_two[:, None] * dy_two[:, None] + dx_two[None, :] * dx_two[None, :]
    levels = jnp.arange(CYCLES, dtype=jnp.int32)
    lows = (2 * CYCLE_W * levels) ** 2
    cycle = jnp.sum((dist[None] >= lows[:, None, None]).astype(jnp.int32), axis=0) - 1
    hits = (cycle[None] == levels[:, None, None]).astype(jnp.float32)
    return hits.reshape(CYCLES, -1)


def calibrate(raw, pedestal, gain, good, bounds):
    code = raw // 2048
    counts_adc = (raw % 2048).astype(jnp.float32)
    base = jnp.where(code == 0, pedestal[0], jnp.where(code == 1, pedestal[1], pedestal[2]))
    gain_factor = gain.astype(jnp.float32)
    scale = jnp.where(
        code == 0, gain_factor[0], jnp.where(code == 1, gain_factor[1], gain_factor[2])
    )
    weight_factor = good.astype(jnp.float32)
    energy = weight_factor * (counts_adc - base) / scale
    columns = jnp.arange(raw.shape[-1], dtype=jnp.int32)
    band = jnp.sum((columns[None, :, None] >= bounds[:, None, :]).astype(jnp.int32), axis=2)
    member_entry = (band[:, :, None] == jnp.arange(BANDS, dtype=jnp.int32)[None, None, :]).astype(
        jnp.float32
    )
    totals = jnp.einsum("fmrc,mcb->fmrb", energy, member_entry, precision=precise_variant)
    present_flag = jnp.einsum(
        "tlg,tgd->tld", weight_factor, member_entry, precision=precise_variant
    )
    level = totals / jnp.maximum(present_flag, 1.0)
    spread = jnp.einsum("fmrb,mcb->fmrc", level, member_entry, precision=precise_variant)
    return (weight_factor * (energy - spread)).astype(jnp.bfloat16)


def calibrate_kernel(group, table_ref, bounds_ref, raw_ref, ped_ref, gain_ref, good_ref, out_ref):
    step = pl.program_id(0)
    cols = raw_ref.shape[-1]
    columns = lax.broadcasted_iota(jnp.int32, (1, cols), 1)
    quarters = out_ref.shape[1]
    width = cols // quarters
    for inner in range(group):
        module = step * group + inner
        raw = raw_ref[:, inner]
        code = lax.shift_right_logical(raw, 11)
        counts_adc = (raw & 2047).astype(jnp.float32)
        base = jnp.where(
            code == 0, ped_ref[0, inner], jnp.where(code == 1, ped_ref[1, inner], ped_ref[2, inner])
        )
        scale = jnp.where(
            code == 0,
            gain_ref[0, inner].astype(jnp.float32),
            jnp.where(
                code == 1,
                gain_ref[1, inner].astype(jnp.float32),
                gain_ref[2, inner].astype(jnp.float32),
            ),
        )
        weight_factor = good_ref[inner].astype(jnp.float32)
        energy = weight_factor * (counts_adc - base) / scale
        band = jnp.zeros((1, cols), jnp.int32)
        for j in range(BANDS - 1):
            band = band + (columns >= bounds_ref[module * (BANDS - 1) + j]).astype(jnp.int32)
        spread = jnp.zeros(energy.shape, jnp.float32)
        for b in range(BANDS):
            member = band == b
            totals = jnp.sum(jnp.where(member, energy, 0.0), axis=-1, keepdims=True)
            present = jnp.sum(jnp.where(member, weight_factor, 0.0), axis=-1, keepdims=True)
            spread = jnp.where(member, totals / jnp.maximum(present, 1.0), spread)
        corrected = (weight_factor * (energy - spread)).astype(jnp.bfloat16)
        slot = table_ref[module]
        for q in range(quarters):
            out_ref[slot, q] = corrected[:, :, q * width : (q + 1) * width]


def calibrate_send(raw, pedestal, gain, good, bounds, table, n_peak):
    frame_dev, mods, row_dev, cols = raw.shape
    width = cols // n_peak
    group = 8
    grid_spec = pltpu.PrefetchScalarGridSpec(
        num_scalar_prefetch=2,
        grid=(mods // group,),
        in_specs=[
            pl.BlockSpec((frame_dev, group, row_dev, cols), lambda m, t, b: (0, m, 0, 0)),
            pl.BlockSpec((3, group, row_dev, cols), lambda m, t, b: (0, m, 0, 0)),
            pl.BlockSpec((3, group, row_dev, cols), lambda m, t, b: (0, m, 0, 0)),
            pl.BlockSpec((group, row_dev, cols), lambda m, t, b: (m, 0, 0)),
        ],
        out_specs=pl.BlockSpec(
            (mods, n_peak, frame_dev, row_dev, width), lambda m, t, b: (0, 0, 0, 0, 0)
        ),
    )
    return pl.pallas_call(
        lambda *refs: calibrate_kernel(group, *refs),
        grid_spec=grid_spec,
        out_shape=jax.ShapeDtypeStruct((mods, n_peak, frame_dev, row_dev, width), jnp.bfloat16),
    )(table, bounds.reshape(-1), raw, pedestal, gain, good)


def score_kernel(n_peak, levels, per, low_ref, mean_ref, rms_ref, frame_ref, cycle_ref, left_ref, right_ref, snr_ref, bent_ref):
    cycle = cycle_ref[...]
    rows, cols = cycle.shape
    tops = mean_ref.shape[1] - 1
    peak_pos = lax.axis_index("peak")
    row_ids = lax.broadcasted_iota(jnp.int32, (rows, cols), 0)
    col_ids = lax.broadcasted_iota(jnp.int32, (rows, cols), 1)
    row_shifts = []
    for shift in (1, rows - 1):
        source = pltpu.roll(row_ids, shift, 0)
        row_shifts.append((shift, jnp.abs(source - row_ids) == 1))
    col_shifts = []
    for shift in (1, cols - 1):
        source = pltpu.roll(col_ids, shift, 1)
        col_shifts.append((shift, jnp.abs(source - col_ids) == 1, source == cols - 1))
    hits = []
    for j in range(levels):
        level = jnp.minimum(low_ref[0] + j, tops)
        hits.append((level, cycle == level))
    for inner in range(per):
        frame_pos = pl.program_id(0) * per + inner
        values = frame_ref[inner].astype(jnp.float32)
        pixel_mean = jnp.zeros((rows, cols), jnp.float32)
        pixel_rms = jnp.ones((rows, cols), jnp.float32)
        for level, hit in hits:
            pixel_mean = jnp.where(hit, mean_ref[frame_pos, level], pixel_mean)
            pixel_rms = jnp.where(hit, rms_ref[frame_pos, level], pixel_rms)
        score = (values - pixel_mean) / pixel_rms
        pick = lax.broadcasted_iota(jnp.int32, (rows, left_ref.shape[0]), 1) == frame_pos
        left_all = jnp.transpose(left_ref[...])
        right_all = jnp.transpose(right_ref[...])
        left_col = jnp.sum(jnp.where(pick, left_all, 0.0), axis=1, keepdims=True)
        right_col = jnp.sum(jnp.where(pick, right_all, 0.0), axis=1, keepdims=True)
        left_col = jnp.where(peak_pos == 0, 0.0, left_col)
        right_col = jnp.where(peak_pos == n_peak - 1, 0.0, right_col)
        total = 4.0 * score
        for shift, inside in row_shifts:
            total = total - jnp.where(inside, pltpu.roll(score, shift, 0), 0.0)
        for shift, inside, wrapped_left in col_shifts:
            near = jnp.where(wrapped_left, left_col, right_col)
            total = total - jnp.where(inside, pltpu.roll(score, shift, 1), near)
        snr_ref[inner] = score.astype(snr_ref.dtype)
        bent_ref[inner] = total.astype(bent_ref.dtype)


def score_outputs(frame, cycle, cycle_average, cycle_rms, left, right, n_peak):
    frames, rows, cols = frame.shape
    span = (rows * rows + cols * cols) ** 0.5
    levels = min(CYCLES, int(span // CYCLE_W) + 2)
    per = 2 if frames % 2 == 0 else 1
    low = jnp.min(cycle).reshape(1)
    block = pl.BlockSpec((per, rows, cols), lambda f, *_: (f, 0, 0))
    edge = pl.BlockSpec((frames, rows), lambda f, *_: (0, 0))
    grid_spec = pltpu.PrefetchScalarGridSpec(
        num_scalar_prefetch=3,
        grid=(frames // per,),
        in_specs=[block, pl.BlockSpec((rows, cols), lambda f, *_: (0, 0)), edge, edge],
        out_specs=[block, block],
    )
    return pl.pallas_call(
        lambda *refs: score_kernel(n_peak, levels, per, *refs),
        grid_spec=grid_spec,
        out_shape=[jax.ShapeDtypeStruct(frame.shape, jnp.bfloat16)] * 2,
    )(low, cycle_average, cycle_rms, frame, cycle, left, right)


def laplace(padded):
    center = padded[..., 1:-1, 1:-1]
    return (
        4.0 * center
        - padded[..., :-2, 1:-1]
        - padded[..., 2:, 1:-1]
        - padded[..., 1:-1, :-2]
        - padded[..., 1:-1, 2:]
    )


def local_present(good, table, row_src, mrows, slot_rows):
    n_peak = lax.axis_size("peak")
    width = good.shape[2] // n_peak
    start = lax.axis_index("peak") * width
    part = lax.dynamic_slice_in_dim(good, start, width, axis=2)
    col = start + jnp.arange(width, dtype=jnp.int32)
    ypos = (table // SLOT_C)[:, None] * mrows + row_src[None, :]
    xpos = (table % SLOT_C)[:, None] * COLS + col[None, :]
    dy_two = 2 * ypos + 1 - slot_rows * mrows
    dx_two = 2 * xpos + 1 - SLOT_C * COLS
    dist = dy_two[:, :, None] * dy_two[:, :, None] + dx_two[:, None, :] * dx_two[:, None, :]
    cycle = cycle_index(dist)
    levels = jnp.arange(CYCLES, dtype=jnp.int32)
    hit = jnp.where(cycle[..., None] == levels, part[..., None], 0)
    return jnp.sum(hit, axis=(0, 1, 2)).astype(jnp.float32)


def gather_sum_kernel(
    n_calib, n_peak, x_ref, o_ref, near, far, partial, near_send, near_recv, far_send, far_recv
):
    my_calib = lax.axis_index("calib")
    my_peak = lax.axis_index("peak")
    near[n_peak - 1] = x_ref[...]
    barrier = pltpu.get_barrier_semaphore()

    def peak_peer(step):
        return (my_calib, lax.rem(my_peak + step, n_peak))

    def calib_peer(step):
        return (lax.rem(my_calib + step, n_calib), my_peak)

    def greet_peak(step, carry):
        pl.semaphore_signal(
            barrier, inc=1, device_id=peak_peer(step), device_id_type=pl.DeviceIdType.MESH
        )
        return carry

    def greet_calib(step, carry):
        pl.semaphore_signal(
            barrier, inc=1, device_id=calib_peer(step), device_id_type=pl.DeviceIdType.MESH
        )
        return carry

    lax.fori_loop(1, n_peak, greet_peak, 0)
    lax.fori_loop(1, n_calib, greet_calib, 0)
    pl.semaphore_wait(barrier, n_peak - 1 + n_calib - 1)

    def send_near(step, carry):
        pltpu.make_async_remote_copy(
            src_ref=x_ref,
            dst_ref=near.at[n_peak - 1 - step],
            send_sem=near_send,
            recv_sem=near_recv,
            device_id=peak_peer(step),
            device_id_type=pl.DeviceIdType.MESH,
        ).start()
        return carry

    lax.fori_loop(1, n_peak, send_near, 0)
    every_near = pltpu.make_async_remote_copy(
        src_ref=near.at[pl.ds(0, n_peak - 1)],
        dst_ref=near.at[pl.ds(0, n_peak - 1)],
        send_sem=near_send,
        recv_sem=near_recv,
        device_id=peak_peer(1),
        device_id_type=pl.DeviceIdType.MESH,
    )
    every_near.wait_send()
    every_near.wait_recv()

    def add_near(source, acc):
        return acc + near[lax.rem(source - my_peak - 1 + 2 * n_peak, n_peak)]

    partial[...] = lax.fori_loop(0, n_peak, add_near, jnp.zeros(x_ref.shape, x_ref.dtype))
    far[n_calib - 1] = partial[...]

    def send_far(step, carry):
        pltpu.make_async_remote_copy(
            src_ref=partial,
            dst_ref=far.at[n_calib - 1 - step],
            send_sem=far_send,
            recv_sem=far_recv,
            device_id=calib_peer(step),
            device_id_type=pl.DeviceIdType.MESH,
        ).start()
        return carry

    lax.fori_loop(1, n_calib, send_far, 0)
    every_far = pltpu.make_async_remote_copy(
        src_ref=far.at[pl.ds(0, n_calib - 1)],
        dst_ref=far.at[pl.ds(0, n_calib - 1)],
        send_sem=far_send,
        recv_sem=far_recv,
        device_id=calib_peer(1),
        device_id_type=pl.DeviceIdType.MESH,
    )
    every_far.wait_send()
    every_far.wait_recv()

    def add_far(source, acc):
        return acc + far[lax.rem(source - my_calib - 1 + 2 * n_calib, n_calib)]

    o_ref[...] = lax.fori_loop(0, n_calib, add_far, jnp.zeros(x_ref.shape, x_ref.dtype))


def gather_sum(x):
    n_calib = lax.axis_size("calib")
    n_peak = lax.axis_size("peak")
    return pl.pallas_call(
        lambda *refs: gather_sum_kernel(n_calib, n_peak, *refs),
        out_shape=jax.ShapeDtypeStruct(x.shape, x.dtype),
        in_specs=[pl.BlockSpec(memory_space=pltpu.VMEM)],
        out_specs=pl.BlockSpec(memory_space=pltpu.VMEM),
        scratch_shapes=[
            pltpu.VMEM((n_peak,) + x.shape, x.dtype),
            pltpu.VMEM((n_calib,) + x.shape, x.dtype),
            pltpu.VMEM(x.shape, x.dtype),
            pltpu.SemaphoreType.DMA,
            pltpu.SemaphoreType.DMA,
            pltpu.SemaphoreType.DMA,
            pltpu.SemaphoreType.DMA,
        ],
        compiler_params=pltpu.CompilerParams(collective_id=0, has_side_effects=True),
    )(x)


def cycle_stats(first, second, present_flag):
    cycle_average = first / present_flag[None, :]
    cycle_rms = jnp.sqrt(second / present_flag[None, :] + 1e-06)
    return (cycle_average, cycle_rms)


def body(raw, pedestal, gain, good, bounds, table):
    frame_dev, mods, row_dev, cols = raw.shape
    n_calib = lax.axis_size("calib")
    n_peak = lax.axis_size("peak")
    mrows = row_dev * n_calib
    slot_rows = mods // SLOT_C
    width_here = cols // n_peak
    frames_all = frame_dev * n_peak
    row_src = lax.axis_index("calib") * row_dev + jnp.arange(row_dev, dtype=jnp.int32)
    send = calibrate_send(raw, pedestal, gain, good, bounds, table, n_peak)
    send = send.reshape(mods * n_peak, frame_dev, row_dev, width_here)
    present_part = local_present(good, table, row_src, mrows, slot_rows)
    got = lax.all_to_all(send, ("calib", "peak"), 0, 0, tiled=True)
    got = got.reshape(n_calib, n_peak, frame_dev, row_dev, width_here)
    frame = jnp.transpose(got, (1, 2, 0, 3, 4)).reshape(frames_all, mrows, width_here)
    slot = lax.axis_index("calib")
    col_dst = lax.axis_index("peak") * width_here + jnp.arange(width_here, dtype=jnp.int32)
    ypos = slot // SLOT_C * mrows + jnp.arange(mrows, dtype=jnp.int32)
    xpos = slot % SLOT_C * COLS + col_dst
    dy_two = 2 * ypos + 1 - slot_rows * mrows
    dx_two = 2 * xpos + 1 - SLOT_C * COLS
    cycle = cycle_index(dy_two[:, None] * dy_two[:, None] + dx_two[None, :] * dx_two[None, :])
    levels = jnp.arange(CYCLES, dtype=jnp.int32)
    hits = (cycle[None] == levels[:, None, None]).astype(jnp.bfloat16)
    pixels = frame
    values = pixels.astype(jnp.float32)
    square = values * values
    square_top = lax.reduce_precision(square, exponent_bits=8, mantissa_bits=7)
    square_hi = square_top.astype(jnp.bfloat16)
    square_lo = (square - square_top).astype(jnp.bfloat16)
    stacked = jnp.concatenate([pixels, square_hi, square_lo], axis=0)
    sums = jnp.einsum("frc,krc->fk", stacked, hits, preferred_element_type=jnp.float32)
    first = sums[:frames_all]
    second = sums[frames_all : 2 * frames_all] + sums[2 * frames_all :]
    lanes = 128
    packed = jnp.concatenate(
        [
            first,
            second,
            jnp.zeros((frames_all, CYCLES), jnp.float32).at[0].set(present_part),
            jnp.zeros((frames_all, lanes - 3 * CYCLES), jnp.float32),
        ],
        axis=1,
    )
    summed = gather_sum(packed)
    first = summed[:, :CYCLES]
    second = summed[:, CYCLES : 2 * CYCLES]
    present_flag = summed[0, 2 * CYCLES : 3 * CYCLES]
    cycle_average, cycle_rms = cycle_stats(first, second, present_flag)
    edge_cycle = jnp.concatenate([cycle[:, width_here - 1], cycle[:, 0]])
    edge_values = jnp.concatenate([frame[:, :, width_here - 1], frame[:, :, 0]], axis=1)
    edge_hits = (edge_cycle[None, :] == levels[:, None]).astype(jnp.float32)
    edge_table = jnp.einsum(
        "fk,kp->fp",
        jnp.concatenate([cycle_average, cycle_rms], axis=0),
        edge_hits,
        precision=precise_variant,
    )
    edge_score = (edge_values.astype(jnp.float32) - edge_table[:frames_all]) / edge_table[frames_all:]
    fwd = [(i, i + 1) for i in range(n_peak - 1)]
    bwd = [(i + 1, i) for i in range(n_peak - 1)]
    left = lax.ppermute(edge_score[:, :mrows], "peak", fwd)
    right = lax.ppermute(edge_score[:, mrows:], "peak", bwd)
    snr, bent = score_outputs(frame, cycle, cycle_average, cycle_rms, left, right, n_peak)
    return (snr[:, None], bent[:, None])


def solution(mesh):
    in_specs = (
        P("peak", None, "calib", None),
        P(None, None, "calib", None),
        P(None, None, "calib", None),
        P(None, "calib", None),
        P(),
        P(),
    )
    out_specs = (P(None, "calib", None, "peak"), P(None, "calib", None, "peak"))
    return jax.shard_map(body, mesh=mesh, in_specs=in_specs, out_specs=out_specs, check_vma=False)
```

```python
import jax
import jax.numpy as jnp
from jax import lax
from jax.sharding import PartitionSpec as P
from jax.experimental import pallas as pl
from jax.experimental.pallas import tpu as pltpu

COLS = 1024
BANDS = 8
SLOT_C = 4
CYCLES = 32
CYCLE_W = 64


precise_variant = lax.Precision.HIGHEST


def padded_2(block, sides, width):
    for axis, dim in sides:
        count = lax.axis_size(axis)
        forward = [(i, i + 1) for i in range(count - 1)]
        backward = [(target, source) for source, target in forward]
        low = lax.ppermute(
            lax.slice_in_dim(block, block.shape[dim] - width, None, axis=dim), axis, forward
        )
        high = lax.ppermute(lax.slice_in_dim(block, 0, width, axis=dim), axis, backward)
        block = jnp.concatenate([low, block, high], axis=dim)
    return block


def cycle_index(dist):
    levels = jnp.arange(1, CYCLES, dtype=jnp.int32)
    lows = (2 * CYCLE_W * levels) ** 2
    return jnp.sum((dist[..., None] >= lows).astype(jnp.int32), axis=-1)


def cycle_onehot(slot, row_pos, col_pos, mrows, slot_rows):
    ypos = slot // SLOT_C * mrows + row_pos
    xpos = slot % SLOT_C * COLS + col_pos
    dy_two = 2 * ypos + 1 - slot_rows * mrows
    dx_two = 2 * xpos + 1 - SLOT_C * COLS
    dist = dy_two[:, None] * dy_two[:, None] + dx_two[None, :] * dx_two[None, :]
    levels = jnp.arange(CYCLES, dtype=jnp.int32)
    lows = (2 * CYCLE_W * levels) ** 2
    cycle = jnp.sum((dist[None] >= lows[:, None, None]).astype(jnp.int32), axis=0) - 1
    hits = (cycle[None] == levels[:, None, None]).astype(jnp.float32)
    return hits.reshape(CYCLES, -1)


def calibrate(raw, pedestal, gain, good, bounds):
    code = raw // 2048
    counts_adc = (raw % 2048).astype(jnp.float32)
    base = jnp.where(code == 0, pedestal[0], jnp.where(code == 1, pedestal[1], pedestal[2]))
    gain_factor = gain.astype(jnp.float32)
    scale = jnp.where(
        code == 0, gain_factor[0], jnp.where(code == 1, gain_factor[1], gain_factor[2])
    )
    weight_factor = good.astype(jnp.float32)
    energy = weight_factor * (counts_adc - base) / scale
    columns = jnp.arange(raw.shape[-1], dtype=jnp.int32)
    band = jnp.sum((columns[None, :, None] >= bounds[:, None, :]).astype(jnp.int32), axis=2)
    member_entry = (band[:, :, None] == jnp.arange(BANDS, dtype=jnp.int32)[None, None, :]).astype(
        jnp.float32
    )
    totals = jnp.einsum("fmrc,mcb->fmrb", energy, member_entry, precision=precise_variant)
    present_flag = jnp.einsum(
        "tlg,tgd->tld", weight_factor, member_entry, precision=precise_variant
    )
    level = totals / jnp.maximum(present_flag, 1.0)
    spread = jnp.einsum("fmrb,mcb->fmrc", level, member_entry, precision=precise_variant)
    return (weight_factor * (energy - spread)).astype(jnp.bfloat16)


def calibrate_kernel(group, table_ref, bounds_ref, raw_ref, ped_ref, gain_ref, good_ref, out_ref):
    step = pl.program_id(0)
    cols = raw_ref.shape[-1]
    columns = lax.broadcasted_iota(jnp.int32, (1, cols), 1)
    quarters = out_ref.shape[1]
    width = cols // quarters
    for inner in range(group):
        module = step * group + inner
        raw = raw_ref[:, inner]
        code = lax.shift_right_logical(raw, 11)
        counts_adc = (raw & 2047).astype(jnp.float32)
        base = jnp.where(
            code == 0, ped_ref[0, inner], jnp.where(code == 1, ped_ref[1, inner], ped_ref[2, inner])
        )
        scale = jnp.where(
            code == 0,
            gain_ref[0, inner].astype(jnp.float32),
            jnp.where(
                code == 1,
                gain_ref[1, inner].astype(jnp.float32),
                gain_ref[2, inner].astype(jnp.float32),
            ),
        )
        weight_factor = good_ref[inner].astype(jnp.float32)
        energy = weight_factor * (counts_adc - base) / scale
        band = jnp.zeros((1, cols), jnp.int32)
        for j in range(BANDS - 1):
            band = band + (columns >= bounds_ref[module * (BANDS - 1) + j]).astype(jnp.int32)
        spread = jnp.zeros(energy.shape, jnp.float32)
        for b in range(BANDS):
            member = band == b
            totals = jnp.sum(jnp.where(member, energy, 0.0), axis=-1, keepdims=True)
            present = jnp.sum(jnp.where(member, weight_factor, 0.0), axis=-1, keepdims=True)
            spread = jnp.where(member, totals / jnp.maximum(present, 1.0), spread)
        corrected = (weight_factor * (energy - spread)).astype(jnp.bfloat16)
        slot = table_ref[module]
        for q in range(quarters):
            out_ref[slot, q] = corrected[:, :, q * width : (q + 1) * width]


def calibrate_send(raw, pedestal, gain, good, bounds, table, n_peak):
    frame_dev, mods, row_dev, cols = raw.shape
    width = cols // n_peak
    group = 8
    grid_spec = pltpu.PrefetchScalarGridSpec(
        num_scalar_prefetch=2,
        grid=(mods // group,),
        in_specs=[
            pl.BlockSpec((frame_dev, group, row_dev, cols), lambda m, t, b: (0, m, 0, 0)),
            pl.BlockSpec((3, group, row_dev, cols), lambda m, t, b: (0, m, 0, 0)),
            pl.BlockSpec((3, group, row_dev, cols), lambda m, t, b: (0, m, 0, 0)),
            pl.BlockSpec((group, row_dev, cols), lambda m, t, b: (m, 0, 0)),
        ],
        out_specs=pl.BlockSpec(
            (mods, n_peak, frame_dev, row_dev, width), lambda m, t, b: (0, 0, 0, 0, 0)
        ),
    )
    return pl.pallas_call(
        lambda *refs: calibrate_kernel(group, *refs),
        grid_spec=grid_spec,
        out_shape=jax.ShapeDtypeStruct((mods, n_peak, frame_dev, row_dev, width), jnp.bfloat16),
    )(table, bounds.reshape(-1), raw, pedestal, gain, good)


def score_kernel(n_peak, levels, per, low_ref, mean_ref, rms_ref, frame_ref, cycle_ref, left_ref, right_ref, snr_ref, bent_ref):
    cycle = cycle_ref[...]
    rows, cols = cycle.shape
    tops = mean_ref.shape[1] - 1
    peak_pos = lax.axis_index("peak")
    row_ids = lax.broadcasted_iota(jnp.int32, (rows, cols), 0)
    col_ids = lax.broadcasted_iota(jnp.int32, (rows, cols), 1)
    row_shifts = []
    for shift in (1, rows - 1):
        source = pltpu.roll(row_ids, shift, 0)
        row_shifts.append((shift, jnp.abs(source - row_ids) == 1))
    col_shifts = []
    for shift in (1, cols - 1):
        source = pltpu.roll(col_ids, shift, 1)
        col_shifts.append((shift, jnp.abs(source - col_ids) == 1, source == cols - 1))
    hits = []
    for j in range(levels):
        level = jnp.minimum(low_ref[0] + j, tops)
        hits.append((level, cycle == level))
    for inner in range(per):
        frame_pos = pl.program_id(0) * per + inner
        values = frame_ref[inner].astype(jnp.float32)
        pixel_mean = jnp.zeros((rows, cols), jnp.float32)
        pixel_rms = jnp.ones((rows, cols), jnp.float32)
        for level, hit in hits:
            pixel_mean = jnp.where(hit, mean_ref[frame_pos, level], pixel_mean)
            pixel_rms = jnp.where(hit, rms_ref[frame_pos, level], pixel_rms)
        score = (values - pixel_mean) / pixel_rms
        pick = lax.broadcasted_iota(jnp.int32, (rows, left_ref.shape[0]), 1) == frame_pos
        left_all = jnp.transpose(left_ref[...])
        right_all = jnp.transpose(right_ref[...])
        left_col = jnp.sum(jnp.where(pick, left_all, 0.0), axis=1, keepdims=True)
        right_col = jnp.sum(jnp.where(pick, right_all, 0.0), axis=1, keepdims=True)
        left_col = jnp.where(peak_pos == 0, 0.0, left_col)
        right_col = jnp.where(peak_pos == n_peak - 1, 0.0, right_col)
        total = 4.0 * score
        for shift, inside in row_shifts:
            total = total - jnp.where(inside, pltpu.roll(score, shift, 0), 0.0)
        for shift, inside, wrapped_left in col_shifts:
            near = jnp.where(wrapped_left, left_col, right_col)
            total = total - jnp.where(inside, pltpu.roll(score, shift, 1), near)
        snr_ref[inner] = score.astype(snr_ref.dtype)
        bent_ref[inner] = total.astype(bent_ref.dtype)


def score_outputs(frame, cycle, low, cycle_average, cycle_rms, left, right, n_peak):
    frames, rows, cols = frame.shape
    span = (rows * rows + cols * cols) ** 0.5
    levels = min(CYCLES, int(span // CYCLE_W) + 2)
    per = 2 if frames % 2 == 0 else 1
    block = pl.BlockSpec((per, rows, cols), lambda f, *_: (f, 0, 0))
    edge = pl.BlockSpec((frames, rows), lambda f, *_: (0, 0))
    grid_spec = pltpu.PrefetchScalarGridSpec(
        num_scalar_prefetch=3,
        grid=(frames // per,),
        in_specs=[block, pl.BlockSpec((rows, cols), lambda f, *_: (0, 0)), edge, edge],
        out_specs=[block, block],
    )
    return pl.pallas_call(
        lambda *refs: score_kernel(n_peak, levels, per, *refs),
        grid_spec=grid_spec,
        out_shape=[jax.ShapeDtypeStruct(frame.shape, jnp.bfloat16)] * 2,
    )(low, cycle_average, cycle_rms, frame, cycle, left, right)


def laplace(padded):
    center = padded[..., 1:-1, 1:-1]
    return (
        4.0 * center
        - padded[..., :-2, 1:-1]
        - padded[..., 2:, 1:-1]
        - padded[..., 1:-1, :-2]
        - padded[..., 1:-1, 2:]
    )


def local_present(good, table, row_src, mrows, slot_rows):
    n_peak = lax.axis_size("peak")
    width = good.shape[2] // n_peak
    start = lax.axis_index("peak") * width
    part = lax.dynamic_slice_in_dim(good, start, width, axis=2)
    col = start + jnp.arange(width, dtype=jnp.int32)
    ypos = (table // SLOT_C)[:, None] * mrows + row_src[None, :]
    xpos = (table % SLOT_C)[:, None] * COLS + col[None, :]
    dy_two = 2 * ypos + 1 - slot_rows * mrows
    dx_two = 2 * xpos + 1 - SLOT_C * COLS
    dist = dy_two[:, :, None] * dy_two[:, :, None] + dx_two[:, None, :] * dx_two[:, None, :]
    cycle = cycle_index(dist)
    levels = jnp.arange(CYCLES, dtype=jnp.int32)
    hit = jnp.where(cycle[..., None] == levels, part[..., None], 0)
    return jnp.sum(hit, axis=(0, 1, 2)).astype(jnp.float32)


def gather_sum_kernel(
    n_calib, n_peak, x_ref, o_ref, near, far, partial, near_send, near_recv, far_send, far_recv
):
    my_calib = lax.axis_index("calib")
    my_peak = lax.axis_index("peak")
    near[n_peak - 1] = x_ref[...]
    barrier = pltpu.get_barrier_semaphore()

    def peak_peer(step):
        return (my_calib, lax.rem(my_peak + step, n_peak))

    def calib_peer(step):
        return (lax.rem(my_calib + step, n_calib), my_peak)

    def greet_peak(step, carry):
        pl.semaphore_signal(
            barrier, inc=1, device_id=peak_peer(step), device_id_type=pl.DeviceIdType.MESH
        )
        return carry

    def greet_calib(step, carry):
        pl.semaphore_signal(
            barrier, inc=1, device_id=calib_peer(step), device_id_type=pl.DeviceIdType.MESH
        )
        return carry

    lax.fori_loop(1, n_peak, greet_peak, 0)
    lax.fori_loop(1, n_calib, greet_calib, 0)
    pl.semaphore_wait(barrier, n_peak - 1 + n_calib - 1)

    def send_near(step, carry):
        pltpu.make_async_remote_copy(
            src_ref=x_ref,
            dst_ref=near.at[n_peak - 1 - step],
            send_sem=near_send,
            recv_sem=near_recv,
            device_id=peak_peer(step),
            device_id_type=pl.DeviceIdType.MESH,
        ).start()
        return carry

    lax.fori_loop(1, n_peak, send_near, 0)
    every_near = pltpu.make_async_remote_copy(
        src_ref=near.at[pl.ds(0, n_peak - 1)],
        dst_ref=near.at[pl.ds(0, n_peak - 1)],
        send_sem=near_send,
        recv_sem=near_recv,
        device_id=peak_peer(1),
        device_id_type=pl.DeviceIdType.MESH,
    )
    every_near.wait_send()
    every_near.wait_recv()

    def add_near(source, acc):
        return acc + near[lax.rem(source - my_peak - 1 + 2 * n_peak, n_peak)]

    partial[...] = lax.fori_loop(0, n_peak, add_near, jnp.zeros(x_ref.shape, x_ref.dtype))
    far[n_calib - 1] = partial[...]

    def send_far(step, carry):
        pltpu.make_async_remote_copy(
            src_ref=partial,
            dst_ref=far.at[n_calib - 1 - step],
            send_sem=far_send,
            recv_sem=far_recv,
            device_id=calib_peer(step),
            device_id_type=pl.DeviceIdType.MESH,
        ).start()
        return carry

    lax.fori_loop(1, n_calib, send_far, 0)
    every_far = pltpu.make_async_remote_copy(
        src_ref=far.at[pl.ds(0, n_calib - 1)],
        dst_ref=far.at[pl.ds(0, n_calib - 1)],
        send_sem=far_send,
        recv_sem=far_recv,
        device_id=calib_peer(1),
        device_id_type=pl.DeviceIdType.MESH,
    )
    every_far.wait_send()
    every_far.wait_recv()

    def add_far(source, acc):
        return acc + far[lax.rem(source - my_calib - 1 + 2 * n_calib, n_calib)]

    o_ref[...] = lax.fori_loop(0, n_calib, add_far, jnp.zeros(x_ref.shape, x_ref.dtype))


def gather_sum(x, *after):
    n_calib = lax.axis_size("calib")
    n_peak = lax.axis_size("peak")
    held = len(after)
    return pl.pallas_call(
        lambda x_ref, *refs: gather_sum_kernel(n_calib, n_peak, x_ref, *refs[held:]),
        out_shape=jax.ShapeDtypeStruct(x.shape, x.dtype),
        in_specs=[pl.BlockSpec(memory_space=pltpu.VMEM)]
        + [pl.BlockSpec(memory_space=pl.ANY)] * held,
        out_specs=pl.BlockSpec(memory_space=pltpu.VMEM),
        scratch_shapes=[
            pltpu.VMEM((n_peak,) + x.shape, x.dtype),
            pltpu.VMEM((n_calib,) + x.shape, x.dtype),
            pltpu.VMEM(x.shape, x.dtype),
            pltpu.SemaphoreType.DMA,
            pltpu.SemaphoreType.DMA,
            pltpu.SemaphoreType.DMA,
            pltpu.SemaphoreType.DMA,
        ],
        compiler_params=pltpu.CompilerParams(collective_id=0, has_side_effects=True),
    )(x, *after)


def cycle_stats(first, second, present_flag):
    cycle_average = first / present_flag[None, :]
    cycle_rms = jnp.sqrt(second / present_flag[None, :] + 1e-06)
    return (cycle_average, cycle_rms)


def body(raw, pedestal, gain, good, bounds, table):
    frame_dev, mods, row_dev, cols = raw.shape
    n_calib = lax.axis_size("calib")
    n_peak = lax.axis_size("peak")
    mrows = row_dev * n_calib
    slot_rows = mods // SLOT_C
    width_here = cols // n_peak
    frames_all = frame_dev * n_peak
    row_src = lax.axis_index("calib") * row_dev + jnp.arange(row_dev, dtype=jnp.int32)
    send = calibrate_send(raw, pedestal, gain, good, bounds, table, n_peak)
    send = send.reshape(mods * n_peak, frame_dev, row_dev, width_here)
    present_part = local_present(good, table, row_src, mrows, slot_rows)
    got = lax.all_to_all(send, ("calib", "peak"), 0, 0, tiled=True)
    got = got.reshape(n_calib, n_peak, frame_dev, row_dev, width_here)
    frame = jnp.transpose(got, (1, 2, 0, 3, 4)).reshape(frames_all, mrows, width_here)
    slot = lax.axis_index("calib")
    col_dst = lax.axis_index("peak") * width_here + jnp.arange(width_here, dtype=jnp.int32)
    ypos = slot // SLOT_C * mrows + jnp.arange(mrows, dtype=jnp.int32)
    xpos = slot % SLOT_C * COLS + col_dst
    dy_two = 2 * ypos + 1 - slot_rows * mrows
    dx_two = 2 * xpos + 1 - SLOT_C * COLS
    cycle = cycle_index(dy_two[:, None] * dy_two[:, None] + dx_two[None, :] * dx_two[None, :])
    levels = jnp.arange(CYCLES, dtype=jnp.int32)
    hits = (cycle[None] == levels[:, None, None]).astype(jnp.bfloat16)
    pixels = frame
    values = pixels.astype(jnp.float32)
    square = values * values
    square_top = lax.reduce_precision(square, exponent_bits=8, mantissa_bits=7)
    square_hi = square_top.astype(jnp.bfloat16)
    square_lo = (square - square_top).astype(jnp.bfloat16)
    stacked = jnp.concatenate([pixels, square_hi, square_lo], axis=0)
    sums = jnp.einsum("frc,krc->fk", stacked, hits, preferred_element_type=jnp.float32)
    first = sums[:frames_all]
    second = sums[frames_all : 2 * frames_all] + sums[2 * frames_all :]
    lanes = 128
    packed = jnp.concatenate(
        [
            first,
            second,
            jnp.zeros((frames_all, CYCLES), jnp.float32).at[0].set(present_part),
            jnp.zeros((frames_all, lanes - 3 * CYCLES), jnp.float32),
        ],
        axis=1,
    )
    low = jnp.min(cycle).reshape(1)
    summed = gather_sum(packed, low)
    first = summed[:, :CYCLES]
    second = summed[:, CYCLES : 2 * CYCLES]
    present_flag = summed[0, 2 * CYCLES : 3 * CYCLES]
    cycle_average, cycle_rms = cycle_stats(first, second, present_flag)
    edge_cycle = jnp.concatenate([cycle[:, width_here - 1], cycle[:, 0]])
    edge_values = jnp.concatenate([frame[:, :, width_here - 1], frame[:, :, 0]], axis=1)
    edge_hits = (edge_cycle[None, :] == levels[:, None]).astype(jnp.float32)
    edge_table = jnp.einsum(
        "fk,kp->fp",
        jnp.concatenate([cycle_average, cycle_rms], axis=0),
        edge_hits,
        precision=precise_variant,
    )
    edge_score = (edge_values.astype(jnp.float32) - edge_table[:frames_all]) / edge_table[frames_all:]
    fwd = [(i, i + 1) for i in range(n_peak - 1)]
    bwd = [(i + 1, i) for i in range(n_peak - 1)]
    left = lax.ppermute(edge_score[:, :mrows], "peak", fwd)
    right = lax.ppermute(edge_score[:, mrows:], "peak", bwd)
    snr, bent = score_outputs(frame, cycle, low, cycle_average, cycle_rms, left, right, n_peak)
    return (snr[:, None], bent[:, None])


def solution(mesh):
    in_specs = (
        P("peak", None, "calib", None),
        P(None, None, "calib", None),
        P(None, None, "calib", None),
        P(None, "calib", None),
        P(),
        P(),
    )
    out_specs = (P(None, "calib", None, "peak"), P(None, "calib", None, "peak"))
    return jax.shard_map(body, mesh=mesh, in_specs=in_specs, out_specs=out_specs, check_vma=False)
```

```python
import jax
import jax.numpy as jnp
from jax import lax
from jax.sharding import PartitionSpec as P
from jax.experimental import pallas as pl
from jax.experimental.pallas import tpu as pltpu

COLS = 1024
BANDS = 8
SLOT_C = 4
CYCLES = 32
CYCLE_W = 64


precise_variant = lax.Precision.HIGHEST


def padded_2(block, sides, width):
    for axis, dim in sides:
        count = lax.axis_size(axis)
        forward = [(i, i + 1) for i in range(count - 1)]
        backward = [(target, source) for source, target in forward]
        low = lax.ppermute(
            lax.slice_in_dim(block, block.shape[dim] - width, None, axis=dim), axis, forward
        )
        high = lax.ppermute(lax.slice_in_dim(block, 0, width, axis=dim), axis, backward)
        block = jnp.concatenate([low, block, high], axis=dim)
    return block


def cycle_index(dist):
    levels = jnp.arange(1, CYCLES, dtype=jnp.int32)
    lows = (2 * CYCLE_W * levels) ** 2
    return jnp.sum((dist[..., None] >= lows).astype(jnp.int32), axis=-1)


def cycle_onehot(slot, row_pos, col_pos, mrows, slot_rows):
    ypos = slot // SLOT_C * mrows + row_pos
    xpos = slot % SLOT_C * COLS + col_pos
    dy_two = 2 * ypos + 1 - slot_rows * mrows
    dx_two = 2 * xpos + 1 - SLOT_C * COLS
    dist = dy_two[:, None] * dy_two[:, None] + dx_two[None, :] * dx_two[None, :]
    levels = jnp.arange(CYCLES, dtype=jnp.int32)
    lows = (2 * CYCLE_W * levels) ** 2
    cycle = jnp.sum((dist[None] >= lows[:, None, None]).astype(jnp.int32), axis=0) - 1
    hits = (cycle[None] == levels[:, None, None]).astype(jnp.float32)
    return hits.reshape(CYCLES, -1)


def calibrate(raw, pedestal, gain, good, bounds):
    code = raw // 2048
    counts_adc = (raw % 2048).astype(jnp.float32)
    base = jnp.where(code == 0, pedestal[0], jnp.where(code == 1, pedestal[1], pedestal[2]))
    gain_factor = gain.astype(jnp.float32)
    scale = jnp.where(
        code == 0, gain_factor[0], jnp.where(code == 1, gain_factor[1], gain_factor[2])
    )
    weight_factor = good.astype(jnp.float32)
    energy = weight_factor * (counts_adc - base) / scale
    columns = jnp.arange(raw.shape[-1], dtype=jnp.int32)
    band = jnp.sum((columns[None, :, None] >= bounds[:, None, :]).astype(jnp.int32), axis=2)
    member_entry = (band[:, :, None] == jnp.arange(BANDS, dtype=jnp.int32)[None, None, :]).astype(
        jnp.float32
    )
    totals = jnp.einsum("fmrc,mcb->fmrb", energy, member_entry, precision=precise_variant)
    present_flag = jnp.einsum(
        "tlg,tgd->tld", weight_factor, member_entry, precision=precise_variant
    )
    level = totals / jnp.maximum(present_flag, 1.0)
    spread = jnp.einsum("fmrb,mcb->fmrc", level, member_entry, precision=precise_variant)
    return (weight_factor * (energy - spread)).astype(jnp.bfloat16)


def calibrate_kernel(group, table_ref, bounds_ref, raw_ref, ped_ref, gain_ref, good_ref, out_ref):
    step = pl.program_id(0)
    cols = raw_ref.shape[-1]
    columns = lax.broadcasted_iota(jnp.int32, (1, cols), 1)
    quarters = out_ref.shape[1]
    width = cols // quarters
    for inner in range(group):
        module = step * group + inner
        raw = raw_ref[:, inner]
        code = lax.shift_right_logical(raw, 11)
        counts_adc = (raw & 2047).astype(jnp.float32)
        base = jnp.where(
            code == 0, ped_ref[0, inner], jnp.where(code == 1, ped_ref[1, inner], ped_ref[2, inner])
        )
        scale = jnp.where(
            code == 0,
            gain_ref[0, inner].astype(jnp.float32),
            jnp.where(
                code == 1,
                gain_ref[1, inner].astype(jnp.float32),
                gain_ref[2, inner].astype(jnp.float32),
            ),
        )
        weight_factor = good_ref[inner].astype(jnp.float32)
        energy = weight_factor * (counts_adc - base) / scale
        band = jnp.zeros((1, cols), jnp.int32)
        for j in range(BANDS - 1):
            band = band + (columns >= bounds_ref[module * (BANDS - 1) + j]).astype(jnp.int32)
        spread = jnp.zeros(energy.shape, jnp.float32)
        for b in range(BANDS):
            member = band == b
            totals = jnp.sum(jnp.where(member, energy, 0.0), axis=-1, keepdims=True)
            present = jnp.sum(jnp.where(member, weight_factor, 0.0), axis=-1, keepdims=True)
            spread = jnp.where(member, totals / jnp.maximum(present, 1.0), spread)
        corrected = (weight_factor * (energy - spread)).astype(jnp.bfloat16)
        slot = table_ref[module]
        for q in range(quarters):
            out_ref[slot, q] = corrected[:, :, q * width : (q + 1) * width]


def calibrate_send(raw, pedestal, gain, good, bounds, table, n_peak):
    frame_dev, mods, row_dev, cols = raw.shape
    width = cols // n_peak
    group = 8
    grid_spec = pltpu.PrefetchScalarGridSpec(
        num_scalar_prefetch=2,
        grid=(mods // group,),
        in_specs=[
            pl.BlockSpec((frame_dev, group, row_dev, cols), lambda m, t, b: (0, m, 0, 0)),
            pl.BlockSpec((3, group, row_dev, cols), lambda m, t, b: (0, m, 0, 0)),
            pl.BlockSpec((3, group, row_dev, cols), lambda m, t, b: (0, m, 0, 0)),
            pl.BlockSpec((group, row_dev, cols), lambda m, t, b: (m, 0, 0)),
        ],
        out_specs=pl.BlockSpec(
            (mods, n_peak, frame_dev, row_dev, width), lambda m, t, b: (0, 0, 0, 0, 0)
        ),
    )
    return pl.pallas_call(
        lambda *refs: calibrate_kernel(group, *refs),
        grid_spec=grid_spec,
        out_shape=jax.ShapeDtypeStruct((mods, n_peak, frame_dev, row_dev, width), jnp.bfloat16),
    )(table, bounds.reshape(-1), raw, pedestal, gain, good)


def score_kernel(n_peak, levels, per, low_ref, mean_ref, rms_ref, frame_ref, cycle_ref, left_ref, right_ref, snr_ref, bent_ref):
    cycle = cycle_ref[...]
    rows, cols = cycle.shape
    tops = mean_ref.shape[1] - 1
    peak_pos = lax.axis_index("peak")
    row_ids = lax.broadcasted_iota(jnp.int32, (rows, cols), 0)
    col_ids = lax.broadcasted_iota(jnp.int32, (rows, cols), 1)
    row_shifts = []
    for shift in (1, rows - 1):
        source = pltpu.roll(row_ids, shift, 0)
        row_shifts.append((shift, jnp.abs(source - row_ids) == 1))
    col_shifts = []
    for shift in (1, cols - 1):
        source = pltpu.roll(col_ids, shift, 1)
        col_shifts.append((shift, jnp.abs(source - col_ids) == 1, source == cols - 1))
    hits = []
    for j in range(levels):
        level = jnp.minimum(low_ref[0] + j, tops)
        hits.append((level, cycle == level))
    left_all = jnp.transpose(left_ref[...])
    right_all = jnp.transpose(right_ref[...])
    for inner in range(per):
        frame_pos = pl.program_id(0) * per + inner
        values = frame_ref[inner].astype(jnp.float32)
        pixel_mean = jnp.zeros((rows, cols), jnp.float32)
        pixel_rms = jnp.ones((rows, cols), jnp.float32)
        for level, hit in hits:
            pixel_mean = jnp.where(hit, mean_ref[frame_pos, level], pixel_mean)
            pixel_rms = jnp.where(hit, rms_ref[frame_pos, level], pixel_rms)
        score = (values - pixel_mean) / pixel_rms
        pick = lax.broadcasted_iota(jnp.int32, (rows, left_ref.shape[0]), 1) == frame_pos
        left_col = jnp.sum(jnp.where(pick, left_all, 0.0), axis=1, keepdims=True)
        right_col = jnp.sum(jnp.where(pick, right_all, 0.0), axis=1, keepdims=True)
        left_col = jnp.where(peak_pos == 0, 0.0, left_col)
        right_col = jnp.where(peak_pos == n_peak - 1, 0.0, right_col)
        total = 4.0 * score
        for shift, inside in row_shifts:
            total = total - jnp.where(inside, pltpu.roll(score, shift, 0), 0.0)
        for shift, inside, wrapped_left in col_shifts:
            near = jnp.where(wrapped_left, left_col, right_col)
            total = total - jnp.where(inside, pltpu.roll(score, shift, 1), near)
        snr_ref[inner] = score.astype(snr_ref.dtype)
        bent_ref[inner] = total.astype(bent_ref.dtype)


def score_outputs(frame, cycle, cycle_average, cycle_rms, left, right, n_peak):
    frames, rows, cols = frame.shape
    span = (rows * rows + cols * cols) ** 0.5
    levels = min(CYCLES, int(span // CYCLE_W) + 2)
    per = 2 if frames % 2 == 0 else 1
    low = jnp.min(cycle).reshape(1)
    block = pl.BlockSpec((per, rows, cols), lambda f, *_: (f, 0, 0))
    edge = pl.BlockSpec((frames, rows), lambda f, *_: (0, 0))
    grid_spec = pltpu.PrefetchScalarGridSpec(
        num_scalar_prefetch=3,
        grid=(frames // per,),
        in_specs=[block, pl.BlockSpec((rows, cols), lambda f, *_: (0, 0)), edge, edge],
        out_specs=[block, block],
    )
    return pl.pallas_call(
        lambda *refs: score_kernel(n_peak, levels, per, *refs),
        grid_spec=grid_spec,
        out_shape=[jax.ShapeDtypeStruct(frame.shape, jnp.bfloat16)] * 2,
    )(low, cycle_average, cycle_rms, frame, cycle, left, right)


def laplace(padded):
    center = padded[..., 1:-1, 1:-1]
    return (
        4.0 * center
        - padded[..., :-2, 1:-1]
        - padded[..., 2:, 1:-1]
        - padded[..., 1:-1, :-2]
        - padded[..., 1:-1, 2:]
    )


def local_present(good, table, row_src, mrows, slot_rows):
    n_peak = lax.axis_size("peak")
    width = good.shape[2] // n_peak
    start = lax.axis_index("peak") * width
    part = lax.dynamic_slice_in_dim(good, start, width, axis=2)
    col = start + jnp.arange(width, dtype=jnp.int32)
    ypos = (table // SLOT_C)[:, None] * mrows + row_src[None, :]
    xpos = (table % SLOT_C)[:, None] * COLS + col[None, :]
    dy_two = 2 * ypos + 1 - slot_rows * mrows
    dx_two = 2 * xpos + 1 - SLOT_C * COLS
    dist = dy_two[:, :, None] * dy_two[:, :, None] + dx_two[:, None, :] * dx_two[:, None, :]
    cycle = cycle_index(dist)
    levels = jnp.arange(CYCLES, dtype=jnp.int32)
    hit = jnp.where(cycle[..., None] == levels, part[..., None], 0)
    return jnp.sum(hit, axis=(0, 1, 2)).astype(jnp.float32)


def gather_sum_kernel(
    n_calib, n_peak, x_ref, o_ref, near, far, partial, near_send, near_recv, far_send, far_recv
):
    my_calib = lax.axis_index("calib")
    my_peak = lax.axis_index("peak")
    near[n_peak - 1] = x_ref[...]
    barrier = pltpu.get_barrier_semaphore()

    def peak_peer(step):
        return (my_calib, lax.rem(my_peak + step, n_peak))

    def calib_peer(step):
        return (lax.rem(my_calib + step, n_calib), my_peak)

    def greet_peak(step, carry):
        pl.semaphore_signal(
            barrier, inc=1, device_id=peak_peer(step), device_id_type=pl.DeviceIdType.MESH
        )
        return carry

    def greet_calib(step, carry):
        pl.semaphore_signal(
            barrier, inc=1, device_id=calib_peer(step), device_id_type=pl.DeviceIdType.MESH
        )
        return carry

    lax.fori_loop(1, n_peak, greet_peak, 0)
    lax.fori_loop(1, n_calib, greet_calib, 0)
    pl.semaphore_wait(barrier, n_peak - 1 + n_calib - 1)

    def send_near(step, carry):
        pltpu.make_async_remote_copy(
            src_ref=x_ref,
            dst_ref=near.at[n_peak - 1 - step],
            send_sem=near_send,
            recv_sem=near_recv,
            device_id=peak_peer(step),
            device_id_type=pl.DeviceIdType.MESH,
        ).start()
        return carry

    lax.fori_loop(1, n_peak, send_near, 0)
    every_near = pltpu.make_async_remote_copy(
        src_ref=near.at[pl.ds(0, n_peak - 1)],
        dst_ref=near.at[pl.ds(0, n_peak - 1)],
        send_sem=near_send,
        recv_sem=near_recv,
        device_id=peak_peer(1),
        device_id_type=pl.DeviceIdType.MESH,
    )
    every_near.wait_send()
    every_near.wait_recv()

    def add_near(source, acc):
        return acc + near[lax.rem(source - my_peak - 1 + 2 * n_peak, n_peak)]

    partial[...] = lax.fori_loop(0, n_peak, add_near, jnp.zeros(x_ref.shape, x_ref.dtype))
    far[n_calib - 1] = partial[...]

    def send_far(step, carry):
        pltpu.make_async_remote_copy(
            src_ref=partial,
            dst_ref=far.at[n_calib - 1 - step],
            send_sem=far_send,
            recv_sem=far_recv,
            device_id=calib_peer(step),
            device_id_type=pl.DeviceIdType.MESH,
        ).start()
        return carry

    lax.fori_loop(1, n_calib, send_far, 0)
    every_far = pltpu.make_async_remote_copy(
        src_ref=far.at[pl.ds(0, n_calib - 1)],
        dst_ref=far.at[pl.ds(0, n_calib - 1)],
        send_sem=far_send,
        recv_sem=far_recv,
        device_id=calib_peer(1),
        device_id_type=pl.DeviceIdType.MESH,
    )
    every_far.wait_send()
    every_far.wait_recv()

    def add_far(source, acc):
        return acc + far[lax.rem(source - my_calib - 1 + 2 * n_calib, n_calib)]

    o_ref[...] = lax.fori_loop(0, n_calib, add_far, jnp.zeros(x_ref.shape, x_ref.dtype))


def gather_sum(x):
    n_calib = lax.axis_size("calib")
    n_peak = lax.axis_size("peak")
    return pl.pallas_call(
        lambda *refs: gather_sum_kernel(n_calib, n_peak, *refs),
        out_shape=jax.ShapeDtypeStruct(x.shape, x.dtype),
        in_specs=[pl.BlockSpec(memory_space=pltpu.VMEM)],
        out_specs=pl.BlockSpec(memory_space=pltpu.VMEM),
        scratch_shapes=[
            pltpu.VMEM((n_peak,) + x.shape, x.dtype),
            pltpu.VMEM((n_calib,) + x.shape, x.dtype),
            pltpu.VMEM(x.shape, x.dtype),
            pltpu.SemaphoreType.DMA,
            pltpu.SemaphoreType.DMA,
            pltpu.SemaphoreType.DMA,
            pltpu.SemaphoreType.DMA,
        ],
        compiler_params=pltpu.CompilerParams(collective_id=0, has_side_effects=True),
    )(x)


def cycle_stats(first, second, present_flag):
    cycle_average = first / present_flag[None, :]
    cycle_rms = jnp.sqrt(second / present_flag[None, :] + 1e-06)
    return (cycle_average, cycle_rms)


def body(raw, pedestal, gain, good, bounds, table):
    frame_dev, mods, row_dev, cols = raw.shape
    n_calib = lax.axis_size("calib")
    n_peak = lax.axis_size("peak")
    mrows = row_dev * n_calib
    slot_rows = mods // SLOT_C
    width_here = cols // n_peak
    frames_all = frame_dev * n_peak
    row_src = lax.axis_index("calib") * row_dev + jnp.arange(row_dev, dtype=jnp.int32)
    send = calibrate_send(raw, pedestal, gain, good, bounds, table, n_peak)
    send = send.reshape(mods * n_peak, frame_dev, row_dev, width_here)
    present_part = local_present(good, table, row_src, mrows, slot_rows)
    got = lax.all_to_all(send, ("calib", "peak"), 0, 0, tiled=True)
    got = got.reshape(n_calib, n_peak, frame_dev, row_dev, width_here)
    frame = jnp.transpose(got, (1, 2, 0, 3, 4)).reshape(frames_all, mrows, width_here)
    slot = lax.axis_index("calib")
    col_dst = lax.axis_index("peak") * width_here + jnp.arange(width_here, dtype=jnp.int32)
    ypos = slot // SLOT_C * mrows + jnp.arange(mrows, dtype=jnp.int32)
    xpos = slot % SLOT_C * COLS + col_dst
    dy_two = 2 * ypos + 1 - slot_rows * mrows
    dx_two = 2 * xpos + 1 - SLOT_C * COLS
    cycle = cycle_index(dy_two[:, None] * dy_two[:, None] + dx_two[None, :] * dx_two[None, :])
    levels = jnp.arange(CYCLES, dtype=jnp.int32)
    hits = (cycle[None] == levels[:, None, None]).astype(jnp.bfloat16)
    pixels = frame
    values = pixels.astype(jnp.float32)
    square = values * values
    square_top = lax.reduce_precision(square, exponent_bits=8, mantissa_bits=7)
    square_hi = square_top.astype(jnp.bfloat16)
    square_lo = (square - square_top).astype(jnp.bfloat16)
    stacked = jnp.concatenate([pixels, square_hi, square_lo], axis=0)
    sums = jnp.einsum("frc,krc->fk", stacked, hits, preferred_element_type=jnp.float32)
    first = sums[:frames_all]
    second = sums[frames_all : 2 * frames_all] + sums[2 * frames_all :]
    lanes = 128
    packed = jnp.concatenate(
        [
            first,
            second,
            jnp.zeros((frames_all, CYCLES), jnp.float32).at[0].set(present_part),
            jnp.zeros((frames_all, lanes - 3 * CYCLES), jnp.float32),
        ],
        axis=1,
    )
    summed = gather_sum(packed)
    first = summed[:, :CYCLES]
    second = summed[:, CYCLES : 2 * CYCLES]
    present_flag = summed[0, 2 * CYCLES : 3 * CYCLES]
    cycle_average, cycle_rms = cycle_stats(first, second, present_flag)
    edge_cycle = jnp.concatenate([cycle[:, width_here - 1], cycle[:, 0]])
    edge_values = jnp.concatenate([frame[:, :, width_here - 1], frame[:, :, 0]], axis=1)
    edge_hits = (edge_cycle[None, :] == levels[:, None]).astype(jnp.float32)
    edge_table = jnp.einsum(
        "fk,kp->fp",
        jnp.concatenate([cycle_average, cycle_rms], axis=0),
        edge_hits,
        precision=precise_variant,
    )
    edge_score = (edge_values.astype(jnp.float32) - edge_table[:frames_all]) / edge_table[frames_all:]
    fwd = [(i, i + 1) for i in range(n_peak - 1)]
    bwd = [(i + 1, i) for i in range(n_peak - 1)]
    left = lax.ppermute(edge_score[:, :mrows], "peak", fwd)
    right = lax.ppermute(edge_score[:, mrows:], "peak", bwd)
    snr, bent = score_outputs(frame, cycle, cycle_average, cycle_rms, left, right, n_peak)
    return (snr[:, None], bent[:, None])


def solution(mesh):
    in_specs = (
        P("peak", None, "calib", None),
        P(None, None, "calib", None),
        P(None, None, "calib", None),
        P(None, "calib", None),
        P(),
        P(),
    )
    out_specs = (P(None, "calib", None, "peak"), P(None, "calib", None, "peak"))
    return jax.shard_map(body, mesh=mesh, in_specs=in_specs, out_specs=out_specs, check_vma=False)
```

```python
import jax
import jax.numpy as jnp
from jax import lax
from jax.sharding import PartitionSpec as P
from jax.experimental import pallas as pl
from jax.experimental.pallas import tpu as pltpu

COLS = 1024
BANDS = 8
SLOT_C = 4
CYCLES = 32
CYCLE_W = 64


precise_variant = lax.Precision.HIGHEST


def padded_2(block, sides, width):
    for axis, dim in sides:
        count = lax.axis_size(axis)
        forward = [(i, i + 1) for i in range(count - 1)]
        backward = [(target, source) for source, target in forward]
        low = lax.ppermute(
            lax.slice_in_dim(block, block.shape[dim] - width, None, axis=dim), axis, forward
        )
        high = lax.ppermute(lax.slice_in_dim(block, 0, width, axis=dim), axis, backward)
        block = jnp.concatenate([low, block, high], axis=dim)
    return block


def cycle_index(dist):
    levels = jnp.arange(1, CYCLES, dtype=jnp.int32)
    lows = (2 * CYCLE_W * levels) ** 2
    return jnp.sum((dist[..., None] >= lows).astype(jnp.int32), axis=-1)


def cycle_onehot(slot, row_pos, col_pos, mrows, slot_rows):
    ypos = slot // SLOT_C * mrows + row_pos
    xpos = slot % SLOT_C * COLS + col_pos
    dy_two = 2 * ypos + 1 - slot_rows * mrows
    dx_two = 2 * xpos + 1 - SLOT_C * COLS
    dist = dy_two[:, None] * dy_two[:, None] + dx_two[None, :] * dx_two[None, :]
    levels = jnp.arange(CYCLES, dtype=jnp.int32)
    lows = (2 * CYCLE_W * levels) ** 2
    cycle = jnp.sum((dist[None] >= lows[:, None, None]).astype(jnp.int32), axis=0) - 1
    hits = (cycle[None] == levels[:, None, None]).astype(jnp.float32)
    return hits.reshape(CYCLES, -1)


def calibrate(raw, pedestal, gain, good, bounds):
    code = raw // 2048
    counts_adc = (raw % 2048).astype(jnp.float32)
    base = jnp.where(code == 0, pedestal[0], jnp.where(code == 1, pedestal[1], pedestal[2]))
    gain_factor = gain.astype(jnp.float32)
    scale = jnp.where(
        code == 0, gain_factor[0], jnp.where(code == 1, gain_factor[1], gain_factor[2])
    )
    weight_factor = good.astype(jnp.float32)
    energy = weight_factor * (counts_adc - base) / scale
    columns = jnp.arange(raw.shape[-1], dtype=jnp.int32)
    band = jnp.sum((columns[None, :, None] >= bounds[:, None, :]).astype(jnp.int32), axis=2)
    member_entry = (band[:, :, None] == jnp.arange(BANDS, dtype=jnp.int32)[None, None, :]).astype(
        jnp.float32
    )
    totals = jnp.einsum("fmrc,mcb->fmrb", energy, member_entry, precision=precise_variant)
    present_flag = jnp.einsum(
        "tlg,tgd->tld", weight_factor, member_entry, precision=precise_variant
    )
    level = totals / jnp.maximum(present_flag, 1.0)
    spread = jnp.einsum("fmrb,mcb->fmrc", level, member_entry, precision=precise_variant)
    return (weight_factor * (energy - spread)).astype(jnp.bfloat16)


def calibrate_kernel(group, table_ref, bounds_ref, raw_ref, ped_ref, gain_ref, good_ref, out_ref):
    step = pl.program_id(0)
    cols = raw_ref.shape[-1]
    columns = lax.broadcasted_iota(jnp.int32, (1, cols), 1)
    quarters = out_ref.shape[1]
    width = cols // quarters
    for inner in range(group):
        module = step * group + inner
        raw = raw_ref[:, inner]
        code = lax.shift_right_logical(raw, 11)
        counts_adc = (raw & 2047).astype(jnp.float32)
        base = jnp.where(
            code == 0, ped_ref[0, inner], jnp.where(code == 1, ped_ref[1, inner], ped_ref[2, inner])
        )
        scale = jnp.where(
            code == 0,
            gain_ref[0, inner].astype(jnp.float32),
            jnp.where(
                code == 1,
                gain_ref[1, inner].astype(jnp.float32),
                gain_ref[2, inner].astype(jnp.float32),
            ),
        )
        weight_factor = good_ref[inner].astype(jnp.float32)
        energy = weight_factor * (counts_adc - base) / scale
        band = jnp.zeros((1, cols), jnp.int32)
        for j in range(BANDS - 1):
            band = band + (columns >= bounds_ref[module * (BANDS - 1) + j]).astype(jnp.int32)
        spread = jnp.zeros(energy.shape, jnp.float32)
        for b in range(BANDS):
            member = band == b
            totals = jnp.sum(jnp.where(member, energy, 0.0), axis=-1, keepdims=True)
            present = jnp.sum(jnp.where(member, weight_factor, 0.0), axis=-1, keepdims=True)
            spread = jnp.where(member, totals / jnp.maximum(present, 1.0), spread)
        corrected = (weight_factor * (energy - spread)).astype(jnp.bfloat16)
        slot = table_ref[module]
        for q in range(quarters):
            out_ref[slot, q] = corrected[:, :, q * width : (q + 1) * width]


def calibrate_send(raw, pedestal, gain, good, bounds, table, n_peak):
    frame_dev, mods, row_dev, cols = raw.shape
    width = cols // n_peak
    group = 8
    grid_spec = pltpu.PrefetchScalarGridSpec(
        num_scalar_prefetch=2,
        grid=(mods // group,),
        in_specs=[
            pl.BlockSpec((frame_dev, group, row_dev, cols), lambda m, t, b: (0, m, 0, 0)),
            pl.BlockSpec((3, group, row_dev, cols), lambda m, t, b: (0, m, 0, 0)),
            pl.BlockSpec((3, group, row_dev, cols), lambda m, t, b: (0, m, 0, 0)),
            pl.BlockSpec((group, row_dev, cols), lambda m, t, b: (m, 0, 0)),
        ],
        out_specs=pl.BlockSpec(
            (mods, n_peak, frame_dev, row_dev, width), lambda m, t, b: (0, 0, 0, 0, 0)
        ),
    )
    return pl.pallas_call(
        lambda *refs: calibrate_kernel(group, *refs),
        grid_spec=grid_spec,
        out_shape=jax.ShapeDtypeStruct((mods, n_peak, frame_dev, row_dev, width), jnp.bfloat16),
    )(table, bounds.reshape(-1), raw, pedestal, gain, good)


def score_kernel(n_peak, levels, per, low_ref, mean_ref, rms_ref, frame_ref, cycle_ref, left_ref, right_ref, snr_ref, bent_ref):
    cycle = cycle_ref[...]
    rows, cols = cycle.shape
    tops = mean_ref.shape[1] - 1
    peak_pos = lax.axis_index("peak")
    row_ids = lax.broadcasted_iota(jnp.int32, (rows, cols), 0)
    col_ids = lax.broadcasted_iota(jnp.int32, (rows, cols), 1)
    row_shifts = []
    for shift in (1, rows - 1):
        source = pltpu.roll(row_ids, shift, 0)
        row_shifts.append((shift, jnp.abs(source - row_ids) == 1))
    col_shifts = []
    for shift in (1, cols - 1):
        source = pltpu.roll(col_ids, shift, 1)
        col_shifts.append((shift, jnp.abs(source - col_ids) == 1, source == cols - 1))
    hits = []
    for j in range(levels):
        level = jnp.minimum(low_ref[0] + j, tops)
        hits.append((level, cycle == level))
    for inner in range(per):
        frame_pos = pl.program_id(0) * per + inner
        values = frame_ref[inner].astype(jnp.float32)
        pixel_mean = jnp.zeros((rows, cols), jnp.float32)
        pixel_rms = jnp.ones((rows, cols), jnp.float32)
        for level, hit in hits:
            pixel_mean = jnp.where(hit, mean_ref[frame_pos, level], pixel_mean)
            pixel_rms = jnp.where(hit, rms_ref[frame_pos, level], pixel_rms)
        score = (values - pixel_mean) / pixel_rms
        pick = lax.broadcasted_iota(jnp.int32, (rows, left_ref.shape[0]), 1) == frame_pos
        left_all = jnp.transpose(left_ref[...])
        right_all = jnp.transpose(right_ref[...])
        left_col = jnp.sum(jnp.where(pick, left_all, 0.0), axis=1, keepdims=True)
        right_col = jnp.sum(jnp.where(pick, right_all, 0.0), axis=1, keepdims=True)
        left_col = jnp.where(peak_pos == 0, 0.0, left_col)
        right_col = jnp.where(peak_pos == n_peak - 1, 0.0, right_col)
        total = 4.0 * score
        for shift, inside in row_shifts:
            total = total - jnp.where(inside, pltpu.roll(score, shift, 0), 0.0)
        for shift, inside, wrapped_left in col_shifts:
            near = jnp.where(wrapped_left, left_col, right_col)
            total = total - jnp.where(inside, pltpu.roll(score, shift, 1), near)
        snr_ref[inner] = score.astype(snr_ref.dtype)
        bent_ref[inner] = total.astype(bent_ref.dtype)


def score_outputs(frame, cycle, cycle_average, cycle_rms, left, right, n_peak):
    frames, rows, cols = frame.shape
    span = (rows * rows + cols * cols) ** 0.5
    levels = min(CYCLES, int(span // CYCLE_W) + 2)
    per = 4 if frames % 4 == 0 else 1
    low = jnp.min(cycle).reshape(1)
    block = pl.BlockSpec((per, rows, cols), lambda f, *_: (f, 0, 0))
    edge = pl.BlockSpec((frames, rows), lambda f, *_: (0, 0))
    grid_spec = pltpu.PrefetchScalarGridSpec(
        num_scalar_prefetch=3,
        grid=(frames // per,),
        in_specs=[block, pl.BlockSpec((rows, cols), lambda f, *_: (0, 0)), edge, edge],
        out_specs=[block, block],
    )
    return pl.pallas_call(
        lambda *refs: score_kernel(n_peak, levels, per, *refs),
        grid_spec=grid_spec,
        out_shape=[jax.ShapeDtypeStruct(frame.shape, jnp.bfloat16)] * 2,
    )(low, cycle_average, cycle_rms, frame, cycle, left, right)


def laplace(padded):
    center = padded[..., 1:-1, 1:-1]
    return (
        4.0 * center
        - padded[..., :-2, 1:-1]
        - padded[..., 2:, 1:-1]
        - padded[..., 1:-1, :-2]
        - padded[..., 1:-1, 2:]
    )


def local_present(good, table, row_src, mrows, slot_rows):
    n_peak = lax.axis_size("peak")
    width = good.shape[2] // n_peak
    start = lax.axis_index("peak") * width
    part = lax.dynamic_slice_in_dim(good, start, width, axis=2)
    col = start + jnp.arange(width, dtype=jnp.int32)
    ypos = (table // SLOT_C)[:, None] * mrows + row_src[None, :]
    xpos = (table % SLOT_C)[:, None] * COLS + col[None, :]
    dy_two = 2 * ypos + 1 - slot_rows * mrows
    dx_two = 2 * xpos + 1 - SLOT_C * COLS
    dist = dy_two[:, :, None] * dy_two[:, :, None] + dx_two[:, None, :] * dx_two[:, None, :]
    cycle = cycle_index(dist)
    levels = jnp.arange(CYCLES, dtype=jnp.int32)
    hit = jnp.where(cycle[..., None] == levels, part[..., None], 0)
    return jnp.sum(hit, axis=(0, 1, 2)).astype(jnp.float32)


def gather_sum_kernel(
    n_calib, n_peak, x_ref, o_ref, near, far, partial, near_send, near_recv, far_send, far_recv
):
    my_calib = lax.axis_index("calib")
    my_peak = lax.axis_index("peak")
    near[n_peak - 1] = x_ref[...]
    barrier = pltpu.get_barrier_semaphore()

    def peak_peer(step):
        return (my_calib, lax.rem(my_peak + step, n_peak))

    def calib_peer(step):
        return (lax.rem(my_calib + step, n_calib), my_peak)

    def greet_peak(step, carry):
        pl.semaphore_signal(
            barrier, inc=1, device_id=peak_peer(step), device_id_type=pl.DeviceIdType.MESH
        )
        return carry

    def greet_calib(step, carry):
        pl.semaphore_signal(
            barrier, inc=1, device_id=calib_peer(step), device_id_type=pl.DeviceIdType.MESH
        )
        return carry

    lax.fori_loop(1, n_peak, greet_peak, 0)
    lax.fori_loop(1, n_calib, greet_calib, 0)
    pl.semaphore_wait(barrier, n_peak - 1 + n_calib - 1)

    def send_near(step, carry):
        pltpu.make_async_remote_copy(
            src_ref=x_ref,
            dst_ref=near.at[n_peak - 1 - step],
            send_sem=near_send,
            recv_sem=near_recv,
            device_id=peak_peer(step),
            device_id_type=pl.DeviceIdType.MESH,
        ).start()
        return carry

    lax.fori_loop(1, n_peak, send_near, 0)
    every_near = pltpu.make_async_remote_copy(
        src_ref=near.at[pl.ds(0, n_peak - 1)],
        dst_ref=near.at[pl.ds(0, n_peak - 1)],
        send_sem=near_send,
        recv_sem=near_recv,
        device_id=peak_peer(1),
        device_id_type=pl.DeviceIdType.MESH,
    )
    every_near.wait_send()
    every_near.wait_recv()

    def add_near(source, acc):
        return acc + near[lax.rem(source - my_peak - 1 + 2 * n_peak, n_peak)]

    partial[...] = lax.fori_loop(0, n_peak, add_near, jnp.zeros(x_ref.shape, x_ref.dtype))
    far[n_calib - 1] = partial[...]

    def send_far(step, carry):
        pltpu.make_async_remote_copy(
            src_ref=partial,
            dst_ref=far.at[n_calib - 1 - step],
            send_sem=far_send,
            recv_sem=far_recv,
            device_id=calib_peer(step),
            device_id_type=pl.DeviceIdType.MESH,
        ).start()
        return carry

    lax.fori_loop(1, n_calib, send_far, 0)
    every_far = pltpu.make_async_remote_copy(
        src_ref=far.at[pl.ds(0, n_calib - 1)],
        dst_ref=far.at[pl.ds(0, n_calib - 1)],
        send_sem=far_send,
        recv_sem=far_recv,
        device_id=calib_peer(1),
        device_id_type=pl.DeviceIdType.MESH,
    )
    every_far.wait_send()
    every_far.wait_recv()

    def add_far(source, acc):
        return acc + far[lax.rem(source - my_calib - 1 + 2 * n_calib, n_calib)]

    o_ref[...] = lax.fori_loop(0, n_calib, add_far, jnp.zeros(x_ref.shape, x_ref.dtype))


def gather_sum(x):
    n_calib = lax.axis_size("calib")
    n_peak = lax.axis_size("peak")
    return pl.pallas_call(
        lambda *refs: gather_sum_kernel(n_calib, n_peak, *refs),
        out_shape=jax.ShapeDtypeStruct(x.shape, x.dtype),
        in_specs=[pl.BlockSpec(memory_space=pltpu.VMEM)],
        out_specs=pl.BlockSpec(memory_space=pltpu.VMEM),
        scratch_shapes=[
            pltpu.VMEM((n_peak,) + x.shape, x.dtype),
            pltpu.VMEM((n_calib,) + x.shape, x.dtype),
            pltpu.VMEM(x.shape, x.dtype),
            pltpu.SemaphoreType.DMA,
            pltpu.SemaphoreType.DMA,
            pltpu.SemaphoreType.DMA,
            pltpu.SemaphoreType.DMA,
        ],
        compiler_params=pltpu.CompilerParams(collective_id=0, has_side_effects=True),
    )(x)


def cycle_stats(first, second, present_flag):
    cycle_average = first / present_flag[None, :]
    cycle_rms = jnp.sqrt(second / present_flag[None, :] + 1e-06)
    return (cycle_average, cycle_rms)


def body(raw, pedestal, gain, good, bounds, table):
    frame_dev, mods, row_dev, cols = raw.shape
    n_calib = lax.axis_size("calib")
    n_peak = lax.axis_size("peak")
    mrows = row_dev * n_calib
    slot_rows = mods // SLOT_C
    width_here = cols // n_peak
    frames_all = frame_dev * n_peak
    row_src = lax.axis_index("calib") * row_dev + jnp.arange(row_dev, dtype=jnp.int32)
    send = calibrate_send(raw, pedestal, gain, good, bounds, table, n_peak)
    send = send.reshape(mods * n_peak, frame_dev, row_dev, width_here)
    present_part = local_present(good, table, row_src, mrows, slot_rows)
    got = lax.all_to_all(send, ("calib", "peak"), 0, 0, tiled=True)
    got = got.reshape(n_calib, n_peak, frame_dev, row_dev, width_here)
    frame = jnp.transpose(got, (1, 2, 0, 3, 4)).reshape(frames_all, mrows, width_here)
    slot = lax.axis_index("calib")
    col_dst = lax.axis_index("peak") * width_here + jnp.arange(width_here, dtype=jnp.int32)
    ypos = slot // SLOT_C * mrows + jnp.arange(mrows, dtype=jnp.int32)
    xpos = slot % SLOT_C * COLS + col_dst
    dy_two = 2 * ypos + 1 - slot_rows * mrows
    dx_two = 2 * xpos + 1 - SLOT_C * COLS
    cycle = cycle_index(dy_two[:, None] * dy_two[:, None] + dx_two[None, :] * dx_two[None, :])
    levels = jnp.arange(CYCLES, dtype=jnp.int32)
    hits = (cycle[None] == levels[:, None, None]).astype(jnp.bfloat16)
    pixels = frame
    values = pixels.astype(jnp.float32)
    square = values * values
    square_top = lax.reduce_precision(square, exponent_bits=8, mantissa_bits=7)
    square_hi = square_top.astype(jnp.bfloat16)
    square_lo = (square - square_top).astype(jnp.bfloat16)
    stacked = jnp.concatenate([pixels, square_hi, square_lo], axis=0)
    sums = jnp.einsum("frc,krc->fk", stacked, hits, preferred_element_type=jnp.float32)
    first = sums[:frames_all]
    second = sums[frames_all : 2 * frames_all] + sums[2 * frames_all :]
    lanes = 128
    packed = jnp.concatenate(
        [
            first,
            second,
            jnp.zeros((frames_all, CYCLES), jnp.float32).at[0].set(present_part),
            jnp.zeros((frames_all, lanes - 3 * CYCLES), jnp.float32),
        ],
        axis=1,
    )
    summed = gather_sum(packed)
    first = summed[:, :CYCLES]
    second = summed[:, CYCLES : 2 * CYCLES]
    present_flag = summed[0, 2 * CYCLES : 3 * CYCLES]
    cycle_average, cycle_rms = cycle_stats(first, second, present_flag)
    edge_cycle = jnp.concatenate([cycle[:, width_here - 1], cycle[:, 0]])
    edge_values = jnp.concatenate([frame[:, :, width_here - 1], frame[:, :, 0]], axis=1)
    edge_hits = (edge_cycle[None, :] == levels[:, None]).astype(jnp.float32)
    edge_table = jnp.einsum(
        "fk,kp->fp",
        jnp.concatenate([cycle_average, cycle_rms], axis=0),
        edge_hits,
        precision=precise_variant,
    )
    edge_score = (edge_values.astype(jnp.float32) - edge_table[:frames_all]) / edge_table[frames_all:]
    fwd = [(i, i + 1) for i in range(n_peak - 1)]
    bwd = [(i + 1, i) for i in range(n_peak - 1)]
    left = lax.ppermute(edge_score[:, :mrows], "peak", fwd)
    right = lax.ppermute(edge_score[:, mrows:], "peak", bwd)
    snr, bent = score_outputs(frame, cycle, cycle_average, cycle_rms, left, right, n_peak)
    return (snr[:, None], bent[:, None])


def solution(mesh):
    in_specs = (
        P("peak", None, "calib", None),
        P(None, None, "calib", None),
        P(None, None, "calib", None),
        P(None, "calib", None),
        P(),
        P(),
    )
    out_specs = (P(None, "calib", None, "peak"), P(None, "calib", None, "peak"))
    return jax.shard_map(body, mesh=mesh, in_specs=in_specs, out_specs=out_specs, check_vma=False)
```

```python
import jax
import jax.numpy as jnp
from jax import lax
from jax.sharding import PartitionSpec as P
from jax.experimental import pallas as pl
from jax.experimental.pallas import tpu as pltpu

COLS = 1024
BANDS = 8
SLOT_C = 4
CYCLES = 32
CYCLE_W = 64


precise_variant = lax.Precision.HIGHEST


def padded_2(block, sides, width):
    for axis, dim in sides:
        count = lax.axis_size(axis)
        forward = [(i, i + 1) for i in range(count - 1)]
        backward = [(target, source) for source, target in forward]
        low = lax.ppermute(
            lax.slice_in_dim(block, block.shape[dim] - width, None, axis=dim), axis, forward
        )
        high = lax.ppermute(lax.slice_in_dim(block, 0, width, axis=dim), axis, backward)
        block = jnp.concatenate([low, block, high], axis=dim)
    return block


def cycle_index(dist):
    levels = jnp.arange(1, CYCLES, dtype=jnp.int32)
    lows = (2 * CYCLE_W * levels) ** 2
    return jnp.sum((dist[..., None] >= lows).astype(jnp.int32), axis=-1)


def cycle_onehot(slot, row_pos, col_pos, mrows, slot_rows):
    ypos = slot // SLOT_C * mrows + row_pos
    xpos = slot % SLOT_C * COLS + col_pos
    dy_two = 2 * ypos + 1 - slot_rows * mrows
    dx_two = 2 * xpos + 1 - SLOT_C * COLS
    dist = dy_two[:, None] * dy_two[:, None] + dx_two[None, :] * dx_two[None, :]
    levels = jnp.arange(CYCLES, dtype=jnp.int32)
    lows = (2 * CYCLE_W * levels) ** 2
    cycle = jnp.sum((dist[None] >= lows[:, None, None]).astype(jnp.int32), axis=0) - 1
    hits = (cycle[None] == levels[:, None, None]).astype(jnp.float32)
    return hits.reshape(CYCLES, -1)


def calibrate(raw, pedestal, gain, good, bounds):
    code = raw // 2048
    counts_adc = (raw % 2048).astype(jnp.float32)
    base = jnp.where(code == 0, pedestal[0], jnp.where(code == 1, pedestal[1], pedestal[2]))
    gain_factor = gain.astype(jnp.float32)
    scale = jnp.where(
        code == 0, gain_factor[0], jnp.where(code == 1, gain_factor[1], gain_factor[2])
    )
    weight_factor = good.astype(jnp.float32)
    energy = weight_factor * (counts_adc - base) / scale
    columns = jnp.arange(raw.shape[-1], dtype=jnp.int32)
    band = jnp.sum((columns[None, :, None] >= bounds[:, None, :]).astype(jnp.int32), axis=2)
    member_entry = (band[:, :, None] == jnp.arange(BANDS, dtype=jnp.int32)[None, None, :]).astype(
        jnp.float32
    )
    totals = jnp.einsum("fmrc,mcb->fmrb", energy, member_entry, precision=precise_variant)
    present_flag = jnp.einsum(
        "tlg,tgd->tld", weight_factor, member_entry, precision=precise_variant
    )
    level = totals / jnp.maximum(present_flag, 1.0)
    spread = jnp.einsum("fmrb,mcb->fmrc", level, member_entry, precision=precise_variant)
    return (weight_factor * (energy - spread)).astype(jnp.bfloat16)


def calibrate_kernel(group, table_ref, bounds_ref, raw_ref, ped_ref, gain_ref, good_ref, out_ref):
    step = pl.program_id(0)
    cols = raw_ref.shape[-1]
    columns = lax.broadcasted_iota(jnp.int32, (1, cols), 1)
    quarters = out_ref.shape[1]
    width = cols // quarters
    for inner in range(group):
        module = step * group + inner
        raw = raw_ref[:, inner]
        code = lax.shift_right_logical(raw, 11)
        counts_adc = (raw & 2047).astype(jnp.float32)
        base = jnp.where(
            code == 0, ped_ref[0, inner], jnp.where(code == 1, ped_ref[1, inner], ped_ref[2, inner])
        )
        scale = jnp.where(
            code == 0,
            gain_ref[0, inner].astype(jnp.float32),
            jnp.where(
                code == 1,
                gain_ref[1, inner].astype(jnp.float32),
                gain_ref[2, inner].astype(jnp.float32),
            ),
        )
        weight_factor = good_ref[inner].astype(jnp.float32)
        energy = weight_factor * (counts_adc - base) / scale
        band = jnp.zeros((1, cols), jnp.int32)
        for j in range(BANDS - 1):
            band = band + (columns >= bounds_ref[module * (BANDS - 1) + j]).astype(jnp.int32)
        spread = jnp.zeros(energy.shape, jnp.float32)
        for b in range(BANDS):
            member = band == b
            totals = jnp.sum(jnp.where(member, energy, 0.0), axis=-1, keepdims=True)
            present = jnp.sum(jnp.where(member, weight_factor, 0.0), axis=-1, keepdims=True)
            spread = jnp.where(member, totals / jnp.maximum(present, 1.0), spread)
        corrected = (weight_factor * (energy - spread)).astype(jnp.bfloat16)
        slot = table_ref[module]
        for q in range(quarters):
            out_ref[slot, q] = corrected[:, :, q * width : (q + 1) * width]


def calibrate_send(raw, pedestal, gain, good, bounds, table, n_peak):
    frame_dev, mods, row_dev, cols = raw.shape
    width = cols // n_peak
    group = 4
    grid_spec = pltpu.PrefetchScalarGridSpec(
        num_scalar_prefetch=2,
        grid=(mods // group,),
        in_specs=[
            pl.BlockSpec((frame_dev, group, row_dev, cols), lambda m, t, b: (0, m, 0, 0)),
            pl.BlockSpec((3, group, row_dev, cols), lambda m, t, b: (0, m, 0, 0)),
            pl.BlockSpec((3, group, row_dev, cols), lambda m, t, b: (0, m, 0, 0)),
            pl.BlockSpec((group, row_dev, cols), lambda m, t, b: (m, 0, 0)),
        ],
        out_specs=pl.BlockSpec(
            (mods, n_peak, frame_dev, row_dev, width), lambda m, t, b: (0, 0, 0, 0, 0)
        ),
    )
    return pl.pallas_call(
        lambda *refs: calibrate_kernel(group, *refs),
        grid_spec=grid_spec,
        out_shape=jax.ShapeDtypeStruct((mods, n_peak, frame_dev, row_dev, width), jnp.bfloat16),
    )(table, bounds.reshape(-1), raw, pedestal, gain, good)


def score_kernel(n_peak, levels, per, low_ref, mean_ref, rms_ref, frame_ref, cycle_ref, left_ref, right_ref, snr_ref, bent_ref):
    cycle = cycle_ref[...]
    rows, cols = cycle.shape
    tops = mean_ref.shape[1] - 1
    peak_pos = lax.axis_index("peak")
    row_ids = lax.broadcasted_iota(jnp.int32, (rows, cols), 0)
    col_ids = lax.broadcasted_iota(jnp.int32, (rows, cols), 1)
    row_shifts = []
    for shift in (1, rows - 1):
        source = pltpu.roll(row_ids, shift, 0)
        row_shifts.append((shift, jnp.abs(source - row_ids) == 1))
    col_shifts = []
    for shift in (1, cols - 1):
        source = pltpu.roll(col_ids, shift, 1)
        col_shifts.append((shift, jnp.abs(source - col_ids) == 1, source == cols - 1))
    hits = []
    for j in range(levels):
        level = jnp.minimum(low_ref[0] + j, tops)
        hits.append((level, cycle == level))
    for inner in range(per):
        frame_pos = pl.program_id(0) * per + inner
        values = frame_ref[inner].astype(jnp.float32)
        pixel_mean = jnp.zeros((rows, cols), jnp.float32)
        pixel_rms = jnp.ones((rows, cols), jnp.float32)
        for level, hit in hits:
            pixel_mean = jnp.where(hit, mean_ref[frame_pos, level], pixel_mean)
            pixel_rms = jnp.where(hit, rms_ref[frame_pos, level], pixel_rms)
        score = (values - pixel_mean) / pixel_rms
        pick = lax.broadcasted_iota(jnp.int32, (rows, left_ref.shape[0]), 1) == frame_pos
        left_all = jnp.transpose(left_ref[...])
        right_all = jnp.transpose(right_ref[...])
        left_col = jnp.sum(jnp.where(pick, left_all, 0.0), axis=1, keepdims=True)
        right_col = jnp.sum(jnp.where(pick, right_all, 0.0), axis=1, keepdims=True)
        left_col = jnp.where(peak_pos == 0, 0.0, left_col)
        right_col = jnp.where(peak_pos == n_peak - 1, 0.0, right_col)
        total = 4.0 * score
        for shift, inside in row_shifts:
            total = total - jnp.where(inside, pltpu.roll(score, shift, 0), 0.0)
        for shift, inside, wrapped_left in col_shifts:
            near = jnp.where(wrapped_left, left_col, right_col)
            total = total - jnp.where(inside, pltpu.roll(score, shift, 1), near)
        snr_ref[inner] = score.astype(snr_ref.dtype)
        bent_ref[inner] = total.astype(bent_ref.dtype)


def score_outputs(frame, cycle, cycle_average, cycle_rms, left, right, n_peak):
    frames, rows, cols = frame.shape
    span = (rows * rows + cols * cols) ** 0.5
    levels = min(CYCLES, int(span // CYCLE_W) + 2)
    per = 2 if frames % 2 == 0 else 1
    low = jnp.min(cycle).reshape(1)
    block = pl.BlockSpec((per, rows, cols), lambda f, *_: (f, 0, 0))
    edge = pl.BlockSpec((frames, rows), lambda f, *_: (0, 0))
    grid_spec = pltpu.PrefetchScalarGridSpec(
        num_scalar_prefetch=3,
        grid=(frames // per,),
        in_specs=[block, pl.BlockSpec((rows, cols), lambda f, *_: (0, 0)), edge, edge],
        out_specs=[block, block],
    )
    return pl.pallas_call(
        lambda *refs: score_kernel(n_peak, levels, per, *refs),
        grid_spec=grid_spec,
        out_shape=[jax.ShapeDtypeStruct(frame.shape, jnp.bfloat16)] * 2,
    )(low, cycle_average, cycle_rms, frame, cycle, left, right)


def laplace(padded):
    center = padded[..., 1:-1, 1:-1]
    return (
        4.0 * center
        - padded[..., :-2, 1:-1]
        - padded[..., 2:, 1:-1]
        - padded[..., 1:-1, :-2]
        - padded[..., 1:-1, 2:]
    )


def local_present(good, table, row_src, mrows, slot_rows):
    n_peak = lax.axis_size("peak")
    width = good.shape[2] // n_peak
    start = lax.axis_index("peak") * width
    part = lax.dynamic_slice_in_dim(good, start, width, axis=2)
    col = start + jnp.arange(width, dtype=jnp.int32)
    ypos = (table // SLOT_C)[:, None] * mrows + row_src[None, :]
    xpos = (table % SLOT_C)[:, None] * COLS + col[None, :]
    dy_two = 2 * ypos + 1 - slot_rows * mrows
    dx_two = 2 * xpos + 1 - SLOT_C * COLS
    dist = dy_two[:, :, None] * dy_two[:, :, None] + dx_two[:, None, :] * dx_two[:, None, :]
    cycle = cycle_index(dist)
    levels = jnp.arange(CYCLES, dtype=jnp.int32)
    hit = jnp.where(cycle[..., None] == levels, part[..., None], 0)
    return jnp.sum(hit, axis=(0, 1, 2)).astype(jnp.float32)


def gather_sum_kernel(
    n_calib, n_peak, x_ref, o_ref, near, far, partial, near_send, near_recv, far_send, far_recv
):
    my_calib = lax.axis_index("calib")
    my_peak = lax.axis_index("peak")
    near[n_peak - 1] = x_ref[...]
    barrier = pltpu.get_barrier_semaphore()

    def peak_peer(step):
        return (my_calib, lax.rem(my_peak + step, n_peak))

    def calib_peer(step):
        return (lax.rem(my_calib + step, n_calib), my_peak)

    def greet_peak(step, carry):
        pl.semaphore_signal(
            barrier, inc=1, device_id=peak_peer(step), device_id_type=pl.DeviceIdType.MESH
        )
        return carry

    def greet_calib(step, carry):
        pl.semaphore_signal(
            barrier, inc=1, device_id=calib_peer(step), device_id_type=pl.DeviceIdType.MESH
        )
        return carry

    lax.fori_loop(1, n_peak, greet_peak, 0)
    lax.fori_loop(1, n_calib, greet_calib, 0)
    pl.semaphore_wait(barrier, n_peak - 1 + n_calib - 1)

    def send_near(step, carry):
        pltpu.make_async_remote_copy(
            src_ref=x_ref,
            dst_ref=near.at[n_peak - 1 - step],
            send_sem=near_send,
            recv_sem=near_recv,
            device_id=peak_peer(step),
            device_id_type=pl.DeviceIdType.MESH,
        ).start()
        return carry

    lax.fori_loop(1, n_peak, send_near, 0)
    every_near = pltpu.make_async_remote_copy(
        src_ref=near.at[pl.ds(0, n_peak - 1)],
        dst_ref=near.at[pl.ds(0, n_peak - 1)],
        send_sem=near_send,
        recv_sem=near_recv,
        device_id=peak_peer(1),
        device_id_type=pl.DeviceIdType.MESH,
    )
    every_near.wait_send()
    every_near.wait_recv()

    def add_near(source, acc):
        return acc + near[lax.rem(source - my_peak - 1 + 2 * n_peak, n_peak)]

    partial[...] = lax.fori_loop(0, n_peak, add_near, jnp.zeros(x_ref.shape, x_ref.dtype))
    far[n_calib - 1] = partial[...]

    def send_far(step, carry):
        pltpu.make_async_remote_copy(
            src_ref=partial,
            dst_ref=far.at[n_calib - 1 - step],
            send_sem=far_send,
            recv_sem=far_recv,
            device_id=calib_peer(step),
            device_id_type=pl.DeviceIdType.MESH,
        ).start()
        return carry

    lax.fori_loop(1, n_calib, send_far, 0)
    every_far = pltpu.make_async_remote_copy(
        src_ref=far.at[pl.ds(0, n_calib - 1)],
        dst_ref=far.at[pl.ds(0, n_calib - 1)],
        send_sem=far_send,
        recv_sem=far_recv,
        device_id=calib_peer(1),
        device_id_type=pl.DeviceIdType.MESH,
    )
    every_far.wait_send()
    every_far.wait_recv()

    def add_far(source, acc):
        return acc + far[lax.rem(source - my_calib - 1 + 2 * n_calib, n_calib)]

    o_ref[...] = lax.fori_loop(0, n_calib, add_far, jnp.zeros(x_ref.shape, x_ref.dtype))


def gather_sum(x):
    n_calib = lax.axis_size("calib")
    n_peak = lax.axis_size("peak")
    return pl.pallas_call(
        lambda *refs: gather_sum_kernel(n_calib, n_peak, *refs),
        out_shape=jax.ShapeDtypeStruct(x.shape, x.dtype),
        in_specs=[pl.BlockSpec(memory_space=pltpu.VMEM)],
        out_specs=pl.BlockSpec(memory_space=pltpu.VMEM),
        scratch_shapes=[
            pltpu.VMEM((n_peak,) + x.shape, x.dtype),
            pltpu.VMEM((n_calib,) + x.shape, x.dtype),
            pltpu.VMEM(x.shape, x.dtype),
            pltpu.SemaphoreType.DMA,
            pltpu.SemaphoreType.DMA,
            pltpu.SemaphoreType.DMA,
            pltpu.SemaphoreType.DMA,
        ],
        compiler_params=pltpu.CompilerParams(collective_id=0, has_side_effects=True),
    )(x)


def cycle_stats(first, second, present_flag):
    cycle_average = first / present_flag[None, :]
    cycle_rms = jnp.sqrt(second / present_flag[None, :] + 1e-06)
    return (cycle_average, cycle_rms)


def body(raw, pedestal, gain, good, bounds, table):
    frame_dev, mods, row_dev, cols = raw.shape
    n_calib = lax.axis_size("calib")
    n_peak = lax.axis_size("peak")
    mrows = row_dev * n_calib
    slot_rows = mods // SLOT_C
    width_here = cols // n_peak
    frames_all = frame_dev * n_peak
    row_src = lax.axis_index("calib") * row_dev + jnp.arange(row_dev, dtype=jnp.int32)
    send = calibrate_send(raw, pedestal, gain, good, bounds, table, n_peak)
    send = send.reshape(mods * n_peak, frame_dev, row_dev, width_here)
    present_part = local_present(good, table, row_src, mrows, slot_rows)
    got = lax.all_to_all(send, ("calib", "peak"), 0, 0, tiled=True)
    got = got.reshape(n_calib, n_peak, frame_dev, row_dev, width_here)
    frame = jnp.transpose(got, (1, 2, 0, 3, 4)).reshape(frames_all, mrows, width_here)
    slot = lax.axis_index("calib")
    col_dst = lax.axis_index("peak") * width_here + jnp.arange(width_here, dtype=jnp.int32)
    ypos = slot // SLOT_C * mrows + jnp.arange(mrows, dtype=jnp.int32)
    xpos = slot % SLOT_C * COLS + col_dst
    dy_two = 2 * ypos + 1 - slot_rows * mrows
    dx_two = 2 * xpos + 1 - SLOT_C * COLS
    cycle = cycle_index(dy_two[:, None] * dy_two[:, None] + dx_two[None, :] * dx_two[None, :])
    levels = jnp.arange(CYCLES, dtype=jnp.int32)
    hits = (cycle[None] == levels[:, None, None]).astype(jnp.bfloat16)
    pixels = frame
    values = pixels.astype(jnp.float32)
    square = values * values
    square_top = lax.reduce_precision(square, exponent_bits=8, mantissa_bits=7)
    square_hi = square_top.astype(jnp.bfloat16)
    square_lo = (square - square_top).astype(jnp.bfloat16)
    stacked = jnp.concatenate([pixels, square_hi, square_lo], axis=0)
    sums = jnp.einsum("frc,krc->fk", stacked, hits, preferred_element_type=jnp.float32)
    first = sums[:frames_all]
    second = sums[frames_all : 2 * frames_all] + sums[2 * frames_all :]
    lanes = 128
    packed = jnp.concatenate(
        [
            first,
            second,
            jnp.zeros((frames_all, CYCLES), jnp.float32).at[0].set(present_part),
            jnp.zeros((frames_all, lanes - 3 * CYCLES), jnp.float32),
        ],
        axis=1,
    )
    summed = gather_sum(packed)
    first = summed[:, :CYCLES]
    second = summed[:, CYCLES : 2 * CYCLES]
    present_flag = summed[0, 2 * CYCLES : 3 * CYCLES]
    cycle_average, cycle_rms = cycle_stats(first, second, present_flag)
    edge_cycle = jnp.concatenate([cycle[:, width_here - 1], cycle[:, 0]])
    edge_values = jnp.concatenate([frame[:, :, width_here - 1], frame[:, :, 0]], axis=1)
    edge_hits = (edge_cycle[None, :] == levels[:, None]).astype(jnp.float32)
    edge_table = jnp.einsum(
        "fk,kp->fp",
        jnp.concatenate([cycle_average, cycle_rms], axis=0),
        edge_hits,
        precision=precise_variant,
    )
    edge_score = (edge_values.astype(jnp.float32) - edge_table[:frames_all]) / edge_table[frames_all:]
    fwd = [(i, i + 1) for i in range(n_peak - 1)]
    bwd = [(i + 1, i) for i in range(n_peak - 1)]
    left = lax.ppermute(edge_score[:, :mrows], "peak", fwd)
    right = lax.ppermute(edge_score[:, mrows:], "peak", bwd)
    snr, bent = score_outputs(frame, cycle, cycle_average, cycle_rms, left, right, n_peak)
    return (snr[:, None], bent[:, None])


def solution(mesh):
    in_specs = (
        P("peak", None, "calib", None),
        P(None, None, "calib", None),
        P(None, None, "calib", None),
        P(None, "calib", None),
        P(),
        P(),
    )
    out_specs = (P(None, "calib", None, "peak"), P(None, "calib", None, "peak"))
    return jax.shard_map(body, mesh=mesh, in_specs=in_specs, out_specs=out_specs, check_vma=False)
```
